32 devices in a mesh: ctx: 4 (over y, x), vis: 8 (over z, core).
Axes of the slice: x: 2, y: 2, z: 4, core: 2. Of those that a mesh axis runs over, the one named last changes fastest.
Arguments:
- patches: bfloat16 [4096, 1280], P(('ctx', 'vis')), may hold values from -10 to 10
- vis_gain: float32 [1280], replicated, may hold values from 0.5 to 1.5
- w_qkv: bfloat16 [1280, 3840], P(None, 'vis'), may hold values from -2 to 2
- w_out: bfloat16 [1280, 1280], P('vis'), may hold values from -0.15625 to 0.15625
- merge_gain: float32 [1280], replicated, may hold values from 0.5 to 1.5
- w_merge: bfloat16 [5120, 8192], P(None, 'vis'), may hold values from -0.078125 to 0.078125
- token_dest: int32 [4, 256], replicated, may hold values from 0 to 3, as said below
- token_row: int32 [4, 256], replicated, may hold values from 0 to 1023, as said below
- prompt_text: bfloat16 [4096, 8192], P('ctx', 'vis'), may hold values from -6 to 6
- kv_gain: float32 [8192], P('vis'), may hold values from 0.5 to 1.5
- w_kv: bfloat16 [8192, 1024], P('vis'), may hold values from -1 to 1
- queries: bfloat16 [512, 4096], P('ctx'), may hold values from -12 to 12
- resp_kv: bfloat16 [512, 1024], P('ctx'), may hold values from -12 to 12
- resp_len: int32 [4], P('ctx'), may hold values from 64 to 128
Outputs:
- attended: bfloat16 [512, 4096], P('ctx')
The draws below stay inside these ranges and needn't reach their ends.
Inputs may be any that keep to these rules, and one draw needn't show every extreme that they name: `token_dest`: the tokens of one image are in order of their prompt shard; at most 96 tokens of one image go to one shard, and from every image exactly 96 go to some shard. `token_row`: no two visual tokens take the same position of one shard.
All inputs are finite; a program needn't handle non-finite values.
Results may differ from the reference program's by a relative error of at most 0.014.
Values may be sent and summed in bfloat16 or wider, within the bound.
A program may use at most 128 MiB of HBM per device.

```python
import math
import jax
import jax.numpy as jnp
from jax import lax

VD = 1280
VHEADS = 16
D = 8192
HD = 128
QH = 32
KVH = 4
CROWS = 1024
R_TOK = 128
VHD = 80
MD = 5120
GP = 1024
VTOK = 256
IMAGES = 4
BASE = 64
L = 4096
RESP = 512
N_CTX = 4


def routing_tables(key):
    count = IMAGES
    half = BASE // 2
    spare = jax.random.randint(jax.random.fold_in(key, 11), (count, count), 0, half + 1)
    diagonal = jnp.arange(count)
    spare = spare.at[diagonal, diagonal].set(half)
    spare = spare.at[diagonal, (diagonal + 1) % count].set(0)
    amounts = BASE + spare - jnp.roll(spare, -1, axis=1)
    running = jnp.cumsum(amounts, axis=1)
    tokens = jnp.arange(VTOK)
    dest = jnp.sum((tokens[None, :, None] >= running[:, None, :]).astype(jnp.int32), axis=2)
    row_first = running - amounts
    within = tokens[None, :] - jnp.take_along_axis(row_first, dest, axis=1)
    column_first = jnp.cumsum(amounts, axis=0) - amounts
    offset = jnp.take_along_axis(column_first, dest, axis=1)
    keys = jax.random.split(jax.random.fold_in(key, 12), count)
    orders = jax.vmap(lambda single: jax.random.permutation(single, CROWS))(keys)
    rows = orders[dest, offset + within]
    return (dest.astype(jnp.int32), rows.astype(jnp.int32))


def draw_token_dest(key, part):
    return routing_tables(key)[0]


def draw_token_row(key, part):
    return routing_tables(key)[1]


def draw_patches(key, part):
    shape = (N_CTX * GP, VD)
    noise_key = jax.random.fold_in(key, 41)
    base = jax.random.truncated_normal(noise_key, -6.0, 6.0, shape, jnp.float32)
    return base.astype(jnp.bfloat16)


def draw_w_qkv(key, part):
    base = jax.random.truncated_normal(jax.random.fold_in(key, 51), -6.0, 6.0, (VD, 3 * VD), jnp.float32)
    base = base / math.sqrt(VD)
    return base.astype(jnp.bfloat16)


def draw_prompt_text(key, part):
    shape = (L, D)
    noise_key = jax.random.fold_in(key, 81)
    base = jax.random.truncated_normal(noise_key, -6.0, 6.0, shape, jnp.float32)
    return base.astype(jnp.bfloat16)


def draw_w_kv(key, part):
    width = KVH * HD
    base = jax.random.truncated_normal(jax.random.fold_in(key, 91), -6.0, 6.0, (D, 2 * width), jnp.float32)
    base = base / math.sqrt(D)
    return base.astype(jnp.bfloat16)


def draw_resp_kv(key, part):
    shape = (RESP, 2 * KVH * HD)
    noise_key = jax.random.fold_in(key, 61)
    base = jax.random.truncated_normal(noise_key, -6.0, 6.0, shape, jnp.float32)
    return base.astype(jnp.bfloat16)


def draw_queries(key, part):
    shape = (RESP, QH * HD)
    noise_key = jax.random.fold_in(key, 71)
    base = 3.0 * jax.random.truncated_normal(noise_key, -4.0, 4.0, shape, jnp.float32)
    return base.astype(jnp.bfloat16)


def set_ends(values, own_key, smallest, high):
    shape = values.shape
    place = [jax.random.randint(jax.random.fold_in(own_key, axis), (), 0, shape[axis]) for axis in range(len(shape))]
    values = values.at[tuple(place)].set(smallest)
    longest = shape.index(max(shape))
    place[longest] = (place[longest] + 1) % shape[longest]
    return values.at[tuple(place)].set(high)


def block_scale(stream_key, extent, cuts, smallest, largest):
    loudness, own = 1.0, jax.random.fold_in(stream_key, 6)
    for dim, shards_of in cuts:
        heights = jnp.exp(jax.random.uniform(jax.random.fold_in(own, dim), (shards_of,), jnp.float32, smallest / len(cuts), largest / len(cuts)))
        loudness = loudness * jnp.repeat(heights, extent[dim] // shards_of).reshape([-1 if axis == dim else 1 for axis in range(len(extent))])
    return loudness


def bell_draw(rng, dims, deviation, bound, cuts=(), held_as=jnp.bfloat16):
    entries = jax.random.normal(rng, dims, jnp.float32) * deviation
    if len(cuts) > 0:
        entries = block_scale(rng, dims, cuts, -0.22, 0.18) * entries
    return jnp.clip(entries, min=-bound, max=bound).astype(held_as)


def setup_inputs(seed: int = 0) -> dict:
    key_list = jax.random.split(jax.random.key(seed), 15)
    patches = draw_patches(jax.random.fold_in(key_list[14], 71), 0)
    vis_gain = jnp.clip(1.0 + 0.1 * jax.random.normal(key_list[1], (VD,), jnp.float32), 0.5, 1.5)
    w_qkv = draw_w_qkv(jax.random.fold_in(key_list[14], 71), 0)
    w_out = bell_draw(key_list[3], (VD, VD), VD ** -0.5, 0.15625, ((0, 8),))
    merge_gain = jnp.clip(1.0 + 0.1 * jax.random.normal(key_list[4], (VD,), jnp.float32), 0.5, 1.5)
    w_merge = bell_draw(key_list[5], (MD, D), MD ** -0.5, 0.078125, ((1, 8),))
    token_dest = draw_token_dest(jax.random.fold_in(key_list[14], 71), 0)
    token_row = draw_token_row(jax.random.fold_in(key_list[14], 71), 0)
    prompt_text = draw_prompt_text(jax.random.fold_in(key_list[14], 71), 0)
    kv_gain = jnp.clip(1.0 + 0.1 * jax.random.normal(key_list[9], (D,), jnp.float32), 0.5, 1.5)
    w_kv = draw_w_kv(jax.random.fold_in(key_list[14], 71), 0)
    queries = draw_queries(jax.random.fold_in(key_list[14], 71), 0)
    resp_kv = draw_resp_kv(jax.random.fold_in(key_list[14], 71), 0)
    resp_len = set_ends(jax.random.randint(key_list[13], (N_CTX,), R_TOK // 2, R_TOK + 1), jax.random.fold_in(key_list[13], 1), R_TOK // 2, R_TOK).astype(jnp.int32)
    return {"patches": patches, "vis_gain": vis_gain, "w_qkv": w_qkv, "w_out": w_out, "merge_gain": merge_gain, "w_merge": w_merge, "token_dest": token_dest, "token_row": token_row, "prompt_text": prompt_text, "kv_gain": kv_gain, "w_kv": w_kv, "queries": queries, "resp_kv": resp_kv, "resp_len": resp_len}


EPS = 1e-06

def layer_norm(values, gain):
    center = values - lax.optimization_barrier(jnp.mean(values, axis=-1, keepdims=True))
    spread = lax.optimization_barrier(jnp.mean(center * center, axis=-1, keepdims=True))
    return center * lax.rsqrt(spread + EPS) * gain.astype(jnp.float32)

def dense_attention(query, keys, values):
    count = query.shape[0]
    block = min(512, count)
    scale = 1.0 / math.sqrt(query.shape[1])

    def one_block(part):
        scores = jnp.dot(part, keys.T, preferred_element_type=jnp.float32) * scale
        highest = lax.optimization_barrier(jnp.max(scores, axis=1, keepdims=True))
        expo = jnp.exp(scores - highest)
        summed = lax.optimization_barrier(jnp.sum(expo, axis=1, keepdims=True))
        mixed = jnp.dot(expo.astype(jnp.bfloat16), values, preferred_element_type=jnp.float32)
        return (mixed / summed).astype(jnp.bfloat16)
    blocks = query.reshape(count // block, block, query.shape[1])
    return lax.map(one_block, blocks).reshape(count, values.shape[1])

def head_attention(packed):
    stacked = jnp.transpose(packed, (1, 0, 2))

    def one_head(item):
        return dense_attention(item[:, :VHD], item[:, VHD:2 * VHD], item[:, 2 * VHD:])
    return jnp.transpose(lax.map(one_head, stacked), (1, 0, 2))

def reference(patches, vis_gain, w_qkv, w_out, merge_gain, w_merge, token_dest, token_row, prompt_text, kv_gain, w_kv, queries, resp_kv, resp_len):

    def vision_image(patch_rows):
        floats = patch_rows.astype(jnp.float32)
        normed = layer_norm(floats, vis_gain).astype(jnp.bfloat16)
        qkv = jnp.dot(normed, w_qkv, preferred_element_type=jnp.float32).astype(jnp.bfloat16)
        heads = head_attention(qkv.reshape(GP, VHEADS, 3 * VHD)).reshape(GP, VD)
        mixed = floats + jnp.dot(heads, w_out, preferred_element_type=jnp.float32)
        merged = layer_norm(mixed, merge_gain).astype(jnp.bfloat16).reshape(VTOK, MD)
        return jnp.dot(merged, w_merge, preferred_element_type=jnp.float32).astype(jnp.bfloat16)
    visual = lax.map(vision_image, patches.reshape(IMAGES, GP, VD))
    places = (token_dest * CROWS + token_row).reshape(-1).astype(jnp.int32)
    prompt = prompt_text.at[places].set(visual.reshape(IMAGES * VTOK, D))

    def project_block(rows):
        floats = rows.astype(jnp.float32)
        inverse = lax.rsqrt(lax.optimization_barrier(jnp.mean(floats * floats, axis=1, keepdims=True)) + EPS)
        normed = (floats * inverse * kv_gain.astype(jnp.float32)).astype(jnp.bfloat16)
        return jnp.dot(normed, w_kv, preferred_element_type=jnp.float32).astype(jnp.bfloat16)
    kv = lax.map(project_block, prompt.reshape(N_CTX, CROWS, D)).reshape(L, 2 * KVH * HD)
    width = KVH * HD
    prompt_keys = kv[:, :width].reshape(L, KVH, HD)
    prompt_values = kv[:, width:].reshape(L, KVH, HD)
    group = QH // KVH
    scale = 1.0 / math.sqrt(HD)
    position = jnp.arange(R_TOK, dtype=jnp.int32)
    visible = jnp.concatenate([jnp.ones((R_TOK, L), dtype=bool), position[None, :] <= position[:, None]], axis=1)

    def one_response(items):
        query, own, length = items
        q_heads = jnp.transpose(query.reshape(R_TOK, KVH, group, HD), (1, 0, 2, 3))
        keys = jnp.concatenate([prompt_keys, own[:, :width].reshape(R_TOK, KVH, HD)], axis=0)
        values = jnp.concatenate([prompt_values, own[:, width:].reshape(R_TOK, KVH, HD)], axis=0)
        keys = jnp.transpose(keys, (1, 0, 2))
        values = jnp.transpose(values, (1, 0, 2))

        def one_head(triple):
            q_part, k_part, v_part = triple
            scores = jnp.einsum('rgd,nd->grn', q_part.astype(jnp.float32), k_part.astype(jnp.float32)) * scale
            scores = jnp.where(visible[None], scores, -1e+30)
            highest = lax.optimization_barrier(jnp.max(scores, axis=2, keepdims=True))
            expo = jnp.where(visible[None], jnp.exp(scores - highest), 0.0)
            summed = lax.optimization_barrier(jnp.sum(expo, axis=2, keepdims=True))
            mixed = jnp.einsum('grn,nd->grd', expo.astype(jnp.bfloat16).astype(jnp.float32), v_part.astype(jnp.float32))
            return mixed / summed
        result = lax.map(one_head, (q_heads, keys, values))
        result = jnp.transpose(result, (2, 0, 1, 3)).reshape(R_TOK, QH * HD)
        live = (position < length)[:, None]
        return jnp.where(live, result, 0.0).astype(jnp.bfloat16)
    attended = lax.map(one_response, (queries.reshape(N_CTX, R_TOK, QH * HD), resp_kv.reshape(N_CTX, R_TOK, 2 * width), resp_len))
    return attended.reshape(RESP, QH * HD)
```

```python
import functools
import math

import jax
import jax.numpy as jnp
from jax import lax
from jax.experimental import pallas as pl
from jax.experimental.pallas import tpu as pltpu
from jax.sharding import Mesh, PartitionSpec as P

VD = 1280
VHEADS = 16
D = 8192
HD = 128
QH = 32
KVH = 4
VHD = 80
MD = 5120


EPS = 1e-06
VIS = ("vk", "vh", "core")
SUB = ("vh", "core")
MESH = pl.DeviceIdType.MESH
VMEM = pl.BlockSpec(memory_space=pltpu.VMEM)
ANY = pl.BlockSpec(memory_space=pl.ANY)
F32 = jnp.float32
BF16 = jnp.bfloat16
PIECES = 2
SUBROWS = 256
LNROWS = 64
LANES = 256


def layer_norm(values, gain):
    center = values - jnp.mean(values, axis=-1, keepdims=True)
    spread = jnp.mean(center * center, axis=-1, keepdims=True)
    return center * lax.rsqrt(spread + EPS) * gain


def flat_index(names, sizes):
    index = 0
    for name, size in zip(names, sizes):
        index = index * size + lax.axis_index(name)
    return index


def coordinates(index, names, sizes):
    place = {}
    for name, size in reversed(list(zip(names, sizes))):
        place[name] = index % size
        index = index // size
    return place


def exchange_kernel(names, sizes, spread, count, *refs):
    xs, outs = refs[:count], refs[count : 2 * count]
    send_sem, recv_sem, local_sem = refs[2 * count :]
    total = math.prod(sizes)
    me = flat_index(names, sizes)
    barrier = pltpu.get_barrier_semaphore()
    for step in range(1, total):
        pl.semaphore_signal(
            barrier,
            inc=1,
            device_id=coordinates((me + step) % total, names, sizes),
            device_id_type=MESH,
        )
    pl.semaphore_wait(barrier, total - 1)
    copies = []
    for step in range(1, total):
        target = (me + step) % total
        for i in range(count):
            copy = pltpu.make_async_remote_copy(
                src_ref=xs[i] if spread else xs[i].at[target],
                dst_ref=outs[i].at[me],
                send_sem=send_sem.at[i, step],
                recv_sem=recv_sem.at[i, step],
                device_id=coordinates(target, names, sizes),
                device_id_type=MESH,
            )
            copy.start()
            copies.append(copy)
    for i in range(count):
        own = pltpu.make_async_copy(
            xs[i] if spread else xs[i].at[me], outs[i].at[me], local_sem.at[i]
        )
        own.start()
        copies.append(own)
    for copy in copies:
        copy.wait()


def exchange(xs, names, spread, collective_id):
    sizes = tuple(lax.axis_size(name) for name in names)
    total, count = math.prod(sizes), len(xs)
    shapes = [((total,) + x.shape) if spread else x.shape for x in xs]
    return pl.pallas_call(
        functools.partial(exchange_kernel, names, sizes, spread, count),
        out_shape=[jax.ShapeDtypeStruct(sh, x.dtype) for sh, x in zip(shapes, xs)],
        in_specs=[VMEM] * count,
        out_specs=[VMEM] * count,
        scratch_shapes=[
            pltpu.SemaphoreType.DMA((count, total)),
            pltpu.SemaphoreType.DMA((count, total)),
            pltpu.SemaphoreType.DMA((count,)),
        ],
        compiler_params=pltpu.CompilerParams(
            collective_id=collective_id, has_side_effects=True
        ),
        cost_estimate=pl.CostEstimate(flops=0, bytes_accessed=30_000_000, transcendentals=0),
    )(*xs)


def line_kernel(sizes, chunks, x_ref, out_ref, send_sem, recv_sem, share_send, share_recv, local_sem):
    chips = sizes[0] * sizes[1]
    core = lax.axis_index("core")
    chip = lax.axis_index("vk") * sizes[1] + lax.axis_index("vh")
    rows = x_ref.shape[0] // chunks

    def at(where, which):
        return {"vk": where // sizes[1], "vh": where % sizes[1], "core": which}

    def neighbour(direction):
        return chip + 1 if direction == 0 else chip - 1

    def has(direction):
        return chip < chips - 1 if direction == 0 else chip > 0

    barrier = pltpu.get_barrier_semaphore()
    pl.semaphore_signal(barrier, inc=1, device_id=at(chip, 1 - core), device_id_type=MESH)
    for direction in range(2):
        @pl.when(has(direction))
        def _():
            pl.semaphore_signal(
                barrier, inc=1, device_id=at(neighbour(direction), core), device_id_type=MESH
            )
    pl.semaphore_wait(barrier, 1 + jnp.where(has(0), 1, 0) + jnp.where(has(1), 1, 0))

    def slot(origin, which, piece):
        return out_ref.at[origin * 2 + which, pl.ds(piece * rows, rows)]

    def source(origin, piece, hop):
        return x_ref.at[pl.ds(piece * rows, rows)] if hop == 0 else slot(origin, core, piece)

    def origin_of(direction, hop):
        return chip - hop if direction == 0 else chip + hop

    def exists(direction, hop):
        return chip >= hop if direction == 0 else chip + hop < chips

    def pass_on(direction, hop, piece):
        origin = origin_of(direction, hop)
        return pltpu.make_async_remote_copy(
            src_ref=source(origin, piece, hop),
            dst_ref=slot(origin, core, piece),
            send_sem=send_sem.at[direction, hop, piece],
            recv_sem=recv_sem.at[direction, hop, piece],
            device_id=at(neighbour(direction), core),
            device_id_type=MESH,
        )

    def arrival(direction, hop, piece):
        origin = origin_of(direction, hop)
        return pltpu.make_async_remote_copy(
            src_ref=slot(origin, core, piece),
            dst_ref=slot(origin, core, piece),
            send_sem=send_sem.at[direction, hop - 1, piece],
            recv_sem=recv_sem.at[direction, hop - 1, piece],
            device_id=at(chip, 1 - core),
            device_id_type=MESH,
        )

    def share(origin, piece, hop):
        return pltpu.make_async_remote_copy(
            src_ref=source(origin, piece, hop),
            dst_ref=slot(origin, core, piece),
            send_sem=share_send.at[origin, piece],
            recv_sem=share_recv.at[origin, piece],
            device_id=at(chip, 1 - core),
            device_id_type=MESH,
        )

    for piece in range(chunks):
        for direction in range(2):
            @pl.when(has(direction))
            def _():
                pass_on(direction, 0, piece).start()
    own = pltpu.make_async_copy(x_ref, out_ref.at[chip * 2 + core], local_sem)
    own.start()
    for piece in range(chunks):
        share(chip, piece, 0).start()
    for hop in range(1, chips):
        for piece in range(chunks):
            for direction in range(2):
                @pl.when(exists(direction, hop))
                def _():
                    arrival(direction, hop, piece).wait_recv()
                    if hop < chips - 1:
                        @pl.when(has(direction))
                        def _():
                            pass_on(direction, hop, piece).start()
                    share(origin_of(direction, hop), piece, hop).start()
    own.wait()
    for piece in range(chunks):
        share(chip, piece, 0).wait_send()
        for direction in range(2):
            for hop in range(chips):
                if hop < chips - 1:
                    @pl.when(jnp.logical_and(exists(direction, hop), has(direction)))
                    def _():
                        pass_on(direction, hop, piece).wait_send()
                if hop > 0:
                    @pl.when(exists(direction, hop))
                    def _():
                        share(origin_of(direction, hop), piece, hop).wait_send()
        for origin in range(chips):
            pltpu.make_async_remote_copy(
                src_ref=slot(origin, 1 - core, piece),
                dst_ref=slot(origin, 1 - core, piece),
                send_sem=share_send.at[origin, piece],
                recv_sem=share_recv.at[origin, piece],
                device_id=at(chip, 1 - core),
                device_id_type=MESH,
            ).wait_recv()


def line_gather(x, chunks, collective_id):
    sizes = tuple(lax.axis_size(name) for name in VIS)
    chips = sizes[0] * sizes[1]
    return pl.pallas_call(
        functools.partial(line_kernel, sizes, chunks),
        out_shape=jax.ShapeDtypeStruct((2 * chips,) + x.shape, x.dtype),
        in_specs=[VMEM],
        out_specs=VMEM,
        scratch_shapes=[
            pltpu.SemaphoreType.DMA((2, chips, chunks)),
            pltpu.SemaphoreType.DMA((2, chips, chunks)),
            pltpu.SemaphoreType.DMA((chips, chunks)),
            pltpu.SemaphoreType.DMA((chips, chunks)),
            pltpu.SemaphoreType.DMA,
        ],
        compiler_params=pltpu.CompilerParams(
            collective_id=collective_id, has_side_effects=True
        ),
        cost_estimate=pl.CostEstimate(flops=0, bytes_accessed=70_000_000, transcendentals=0),
    )(x)


def front_kernel(sizes, *refs):
    (
        patches_ref, gain_ref, tgain_ref, wqkv_hbm, text_hbm, wkv_hbm,
        qkv_ref, held, chain_last, mine_ref, mine_sq,
        wqkv, wpad, text, wkv, normed, own, own_sq, pair_out, pair_in, chain_out, chain_in,
        load_sem, send_sem, recv_sem, near_send, near_recv, pair_sem, chain_send, chain_recv,
    ) = refs
    chips, vh = sizes[0] * sizes[1], sizes[1]
    core = lax.axis_index("core")
    chip = lax.axis_index("vk") * vh + lax.axis_index("vh")
    count = patches_ref.shape[0]
    half = count // PIECES
    each = mine_ref.shape[0]
    subs = each // SUBROWS

    def at(where, which):
        return {"vk": where // vh, "vh": where % vh, "core": which}

    def neighbour(direction):
        return chip + 1 if direction == 0 else chip - 1

    def has(direction):
        return chip < chips - 1 if direction == 0 else chip > 0

    def remote(src, dst, send, recv, where, which):
        return pltpu.make_async_remote_copy(
            src_ref=src, dst_ref=dst, send_sem=send, recv_sem=recv,
            device_id=at(where, which), device_id_type=MESH,
        )

    loads = [
        pltpu.make_async_copy(text_hbm, text, load_sem.at[0]),
        pltpu.make_async_copy(wkv_hbm, wkv, load_sem.at[1]),
        pltpu.make_async_copy(wqkv_hbm, wqkv, load_sem.at[2]),
    ]
    for load in loads:
        load.start()

    barrier = pltpu.get_barrier_semaphore()
    pl.semaphore_signal(barrier, inc=1, device_id=at(chip, 1 - core), device_id_type=MESH)
    for direction in range(2):
        @pl.when(has(direction))
        def _():
            pl.semaphore_signal(
                barrier, inc=1, device_id=at(neighbour(direction), core), device_id_type=MESH
            )
    pl.semaphore_wait(barrier, 1 + jnp.where(has(0), 1, 0) + jnp.where(has(1), 1, 0))

    def slot(origin, which, piece):
        return held.at[origin * 2 + which, pl.ds(piece * half, half)]

    def source(origin, piece, hop):
        return patches_ref.at[pl.ds(piece * half, half)] if hop == 0 else slot(origin, core, piece)

    def origin_of(direction, hop):
        return chip - hop if direction == 0 else chip + hop

    def exists(direction, hop):
        return chip >= hop if direction == 0 else chip + hop < chips

    def pass_on(direction, hop, piece):
        origin = origin_of(direction, hop)
        return remote(
            source(origin, piece, hop), slot(origin, core, piece),
            send_sem.at[direction, hop, piece], recv_sem.at[direction, hop, piece],
            neighbour(direction), core,
        )

    def arrival(direction, hop, piece):
        origin = origin_of(direction, hop)
        return remote(
            slot(origin, core, piece), slot(origin, core, piece),
            send_sem.at[direction, hop - 1, piece], recv_sem.at[direction, hop - 1, piece],
            chip, 1 - core,
        )

    def give(origin, piece, hop):
        return remote(
            source(origin, piece, hop), slot(origin, core, piece),
            near_send.at[origin, piece], near_recv.at[origin, piece], chip, 1 - core,
        )

    def taken(origin, piece):
        return remote(
            slot(origin, 1 - core, piece), slot(origin, 1 - core, piece),
            near_send.at[origin, piece], near_recv.at[origin, piece], chip, 1 - core,
        )

    for piece in range(PIECES):
        for direction in range(2):
            @pl.when(has(direction))
            def _():
                pass_on(direction, 0, piece).start()
    mine = pltpu.make_async_copy(patches_ref, held.at[chip * 2 + core], load_sem.at[3])
    mine.start()
    for piece in range(PIECES):
        give(chip, piece, 0).start()

    def relay(hop):
        for piece in range(PIECES):
            for direction in range(2):
                @pl.when(exists(direction, hop))
                def _():
                    arrival(direction, hop, piece).wait_recv()
                    if hop < chips - 1:
                        @pl.when(has(direction))
                        def _():
                            pass_on(direction, hop, piece).start()
                    give(origin_of(direction, hop), piece, hop).start()

    def text_rows(v, which, write):
        for s in range(subs):
            first = pl.multiple_of((v * 2 + which) * each + s * SUBROWS, SUBROWS)
            rows = text[pl.ds(first, SUBROWS), :].astype(F32)
            total = jnp.sum(rows * rows, axis=1, keepdims=True)
            line = jnp.transpose(jnp.broadcast_to(total, (SUBROWS, 128)))
            own_sq[v, s : s + 1, :] = line[0:1]
            scaled = (rows * tgain_ref[...]).astype(BF16)
            for side in range(2):
                for pair in range(KVH // 2):
                    begin = (side * KVH + pair * 2) * HD
                    raw = jnp.dot(scaled, wkv[:, begin : begin + 2 * HD], preferred_element_type=F32)
                    for i in range(2):
                        write((pair * 2 + i) * vh + v, s, side, raw[:, i * HD : (i + 1) * HD])

    def tail(total):
        coarse = total.astype(BF16).astype(F32)
        return jnp.concatenate([coarse, total - coarse], axis=0).astype(BF16)

    def untail(block):
        block = block.astype(F32)
        return block[:8] + block[8:]

    def write_pair(d, s, side, value):
        pair_out[d, s * SUBROWS : (s + 1) * SUBROWS, side * HD : (side + 1) * HD] = value.astype(BF16)

    def write_own(d, s, side, value):
        own[d, s * SUBROWS : (s + 1) * SUBROWS, side * HD : (side + 1) * HD] = value

    own_sq[...] = jnp.zeros_like(own_sq)
    loads[0].wait()
    loads[1].wait()
    for v in range(vh):
        text_rows(v, 1 - core, write_pair)
        for h in range(KVH):
            pair_out[h * vh + v, each:, :] = tail(own_sq[v])
    swap = remote(pair_out, pair_in, pair_sem.at[0], pair_sem.at[1], chip, 1 - core)
    swap.start()
    for v in range(vh):
        text_rows(v, core, write_own)

    loads[2].wait()
    wpad[...] = jnp.zeros_like(wpad)
    for part in range(wqkv.shape[1] // VHD):
        wpad[:, part * 128 : part * 128 + VHD] = wqkv[:, part * VHD : (part + 1) * VHD]

    def project(origin):
        def norm_rows(i, carry):
            which = i // (count // LNROWS)
            begin = pl.multiple_of((i % (count // LNROWS)) * LNROWS, LNROWS)
            floats = held[origin * 2 + which, pl.ds(begin, LNROWS), :].astype(F32)
            place = pl.multiple_of(i * LNROWS, LNROWS)
            normed[pl.ds(place, LNROWS), :] = layer_norm(floats, gain_ref[...]).astype(BF16)
            return carry

        lax.fori_loop(0, 2 * count // LNROWS, norm_rows, 0)
        first = pl.multiple_of(origin * 2 * count, 2 * count)
        qkv_ref[pl.ds(first, 2 * count), :] = jnp.dot(
            normed[...], wpad[...], preferred_element_type=F32
        ).astype(BF16)

    def project_hop(hop):
        for direction in range(2 if hop else 1):
            @pl.when(exists(direction, hop))
            def _():
                origin = origin_of(direction, hop)
                for piece in range(PIECES):
                    taken(origin, piece).wait_recv()
                project(origin)

    def link(direction, d):
        return remote(
            chain_out.at[direction, d], chain_in.at[direction, d],
            chain_send.at[direction, d], chain_recv.at[direction, d], neighbour(direction), core,
        )

    def sum_up(d, source, put, put_square):
        def body(i, carry):
            rows = pl.ds(pl.multiple_of(i * 128, 128), 128)
            value = own[d, rows, :] + pair_in[d, rows, :].astype(F32)
            if source is not None:
                value += source[rows, :].astype(F32)
            put(rows, value)
            return carry

        lax.fori_loop(0, each // 128, body, 0)
        square = own_sq[d % vh] + untail(pair_in[d, each:, :])
        if source is not None:
            square += untail(source[each:, :])
        put_square(square)

    def chain(step):
        for direction in range(2):
            rank = chip if direction == 0 else chips - 1 - chip
            ahead = chips - step
            d = chip + ahead if direction == 0 else chip - ahead
            last = step == chips - 1

            def block():
                return chain_last.at[direction] if last else chain_out.at[direction, d]

            def put(rows, value):
                block()[rows, :] = value.astype(BF16)

            def put_square(square):
                block()[each:, :] = tail(square)

            @pl.when(rank < step)
            def _():
                @pl.when(rank == 0)
                def _():
                    sum_up(d, None, put, put_square)

                if step > 1:
                    @pl.when(rank > 0)
                    def _():
                        link(direction, d).wait_recv()
                        sum_up(d, chain_in.at[direction, d], put, put_square)

                if not last:
                    link(direction, d).start()

    relay(1)
    swap.wait_recv()
    if chips > 2:
        chain(1)
    mine.wait()
    project_hop(0)
    for hop in range(2, chips):
        relay(hop)
        if hop < chips - 1:
            chain(hop)
        project_hop(hop - 1)

    def put_mine(rows, value):
        mine_ref[rows, :] = value

    def put_mine_square(square):
        mine_sq[...] = square

    sum_up(chip, None, put_mine, put_mine_square)
    chain(chips - 1)
    project_hop(chips - 1)

    swap.wait_send()
    for piece in range(PIECES):
        give(chip, piece, 0).wait_send()
        for direction in range(2):
            for hop in range(chips):
                if hop < chips - 1:
                    @pl.when(jnp.logical_and(exists(direction, hop), has(direction)))
                    def _():
                        pass_on(direction, hop, piece).wait_send()
                if hop > 0:
                    @pl.when(exists(direction, hop))
                    def _():
                        give(origin_of(direction, hop), piece, hop).wait_send()
    for direction in range(2):
        for d in range(chips):
            @pl.when(chip < d - 1 if direction == 0 else chip > d + 1)
            def _():
                link(direction, d).wait_send()


def front(patches, vis_gain, w_qkv, text, kv_gain, w_kv, collective_id):
    sizes = tuple(lax.axis_size(name) for name in VIS)
    chips = sizes[0] * sizes[1]
    parts = sizes[1] * 2
    count, width = patches.shape
    rows, features = text.shape
    each = rows // parts
    heads3 = w_qkv.shape[1] // VHD
    block = (each + 16, 2 * HD)
    DMA = pltpu.SemaphoreType.DMA
    return pl.pallas_call(
        functools.partial(front_kernel, sizes),
        out_shape=[
            jax.ShapeDtypeStruct((2 * chips * count, heads3 * 128), BF16),
            jax.ShapeDtypeStruct((2 * chips, count, width), BF16),
            jax.ShapeDtypeStruct((2,) + block, BF16),
            jax.ShapeDtypeStruct((each, 2 * HD), F32),
            jax.ShapeDtypeStruct((8, SUBROWS), F32),
        ],
        in_specs=[VMEM] * 3 + [ANY] * 3,
        out_specs=[VMEM] * 5,
        scratch_shapes=[
            pltpu.VMEM(w_qkv.shape, BF16),
            pltpu.VMEM((width, heads3 * 128), BF16),
            pltpu.VMEM(text.shape, BF16),
            pltpu.VMEM(w_kv.shape, BF16),
            pltpu.VMEM((2 * count, width), BF16),
            pltpu.VMEM((chips,) + (each, 2 * HD), F32),
            pltpu.VMEM((sizes[1], 8, SUBROWS), F32),
            pltpu.VMEM((chips,) + block, BF16),
            pltpu.VMEM((chips,) + block, BF16),
            pltpu.VMEM((2, chips) + block, BF16),
            pltpu.VMEM((2, chips) + block, BF16),
            DMA((4,)),
            DMA((2, chips, PIECES)),
            DMA((2, chips, PIECES)),
            DMA((chips, PIECES)),
            DMA((chips, PIECES)),
            DMA((2,)),
            DMA((2, chips)),
            DMA((2, chips)),
        ],
        compiler_params=pltpu.CompilerParams(
            collective_id=collective_id, has_side_effects=True, vmem_limit_bytes=48 * 2**20
        ),
    )(patches, vis_gain.reshape(1, -1), kv_gain.reshape(1, -1), w_qkv, text, w_kv)


def spread_of(rows, width, places):
    best = (1, 1)
    for down in range(1, rows // 16 + 1):
        for across in range(1, width // 128 + 1):
            if rows % (16 * down) or width % (128 * across) or down * across > places:
                continue
            if down * across > best[0] * best[1]:
                best = (down, across)
    return best


def middle_kernel(sizes, ctxs, *refs):
    (
        qkv_ref, patches_ref, wout_ref, gain_ref, chain_ref, mine_ref, sq_ref, wmerge_hbm,
        visual_ref, text_ref,
        held, wall, wmerge, mixed, merged, values, chain_in,
        load_sem, send_sem, recv_sem, near_send, near_recv, chain_send, chain_recv,
        line_send, line_recv, plane_send, plane_recv, pair_send, pair_recv,
        text_send, text_recv, twin_send, twin_recv,
    ) = refs
    chips, vh = sizes[0] * sizes[1], sizes[1]
    core, ctx = lax.axis_index("core"), lax.axis_index("ctx")
    vk_index, vh_index = lax.axis_index("vk"), lax.axis_index("vh")
    chip = vk_index * vh + vh_index
    me = chip * 2 + core
    each = mine_ref.shape[0]
    subs = each // SUBROWS
    deep, width = wout_ref.shape
    total = qkv_ref.shape[0]
    blocks = total // LANES
    heads = deep // VHD
    planes = ctxs * vh
    plane = ctx * vh + vh_index

    def at(where, which):
        return {"vk": where // vh, "vh": where % vh, "core": which}

    def beside(where):
        return {"ctx": where // vh, "vh": where % vh}

    def neighbour(direction):
        return chip + 1 if direction == 0 else chip - 1

    def has(direction):
        return chip < chips - 1 if direction == 0 else chip > 0

    def remote(src, dst, send, recv, device):
        return pltpu.make_async_remote_copy(
            src_ref=src, dst_ref=dst, send_sem=send, recv_sem=recv,
            device_id=device, device_id_type=MESH,
        )

    twin = at(chip, 1 - core)
    load = pltpu.make_async_copy(wmerge_hbm, wmerge, load_sem.at[0])
    load.start()
    my_rows = pl.ds(pl.multiple_of(me * deep, 16), deep)
    keep = pltpu.make_async_copy(wout_ref, wall.at[my_rows], load_sem.at[1])
    keep.start()

    barrier = pltpu.get_barrier_semaphore()
    pl.semaphore_signal(barrier, inc=1, device_id=twin, device_id_type=MESH)
    for k in range(1, chips):
        pl.semaphore_signal(
            barrier, inc=1, device_id=at((chip + k) % chips, core), device_id_type=MESH
        )
    for j in range(1, planes):
        pl.semaphore_signal(
            barrier, inc=1, device_id=beside((plane + j) % planes), device_id_type=MESH
        )
    pl.semaphore_wait(barrier, chips + planes - 1)

    def last_link(direction):
        return remote(
            chain_ref.at[direction], chain_in.at[direction],
            chain_send.at[direction], chain_recv.at[direction], at(neighbour(direction), core),
        )

    for direction in range(2):
        @pl.when(has(direction))
        def _():
            last_link(direction).start()

    down, across = spread_of(deep, width, ctxs)
    used, high, wide = down * across, deep // down, width // across

    def part(origin, which, index):
        first = pl.multiple_of((origin * 2 + which) * deep + (index // across) * high, 16)
        lane = pl.multiple_of((index % across) * wide, 128)
        return wall.at[pl.ds(first, high), pl.ds(lane, wide)]

    def line_part(k):
        first = pl.multiple_of((ctx // across) * high, 16)
        lane = pl.multiple_of((ctx % across) * wide, 128)
        return remote(
            wout_ref.at[pl.ds(first, high), pl.ds(lane, wide)], part(chip, core, ctx),
            line_send.at[k], line_recv.at[k], at((chip + k) % chips, core),
        )

    def from_line(k, j):
        block = part((chip - k) % chips, core, ctx)
        return remote(
            block, block, plane_send.at[k, j], plane_recv.at[k, j], {"ctx": (ctx + j) % ctxs}
        )

    def to_twin(k, j, which):
        block = part((chip - k) % chips, which, (ctx - j) % ctxs)
        return remote(block, block, pair_send.at[k, j], pair_recv.at[k, j], twin)

    def own_to_twin():
        return remote(wout_ref, wall.at[my_rows], pair_send.at[0, 0], pair_recv.at[0, 0], twin)

    for k in range(1, chips):
        @pl.when(ctx < used)
        def _():
            line_part(k).start()
    own_to_twin().start()

    def slot(origin, which, piece):
        first = pl.multiple_of((origin * 2 + which) * deep, 16)
        return held.at[pl.ds(first, deep), pl.ds(pl.multiple_of(piece * LANES, LANES), LANES)]

    def origin_of(direction, hop):
        return chip - hop if direction == 0 else chip + hop

    def exists(direction, hop):
        return chip >= hop if direction == 0 else chip + hop < chips

    def pass_on(direction, hop, piece):
        block = slot(origin_of(direction, hop), core, piece)
        return remote(
            block, block, send_sem.at[direction, hop, piece], recv_sem.at[direction, hop, piece],
            at(neighbour(direction), core),
        )

    def arrival(direction, hop, piece):
        block = slot(origin_of(direction, hop), core, piece)
        return remote(
            block, block, send_sem.at[direction, hop - 1, piece],
            recv_sem.at[direction, hop - 1, piece], twin,
        )

    def give(origin, piece, which):
        block = slot(origin, which, piece)
        return remote(
            block, block, near_send.at[origin, piece], near_recv.at[origin, piece], twin
        )

    scale = 1.0 / math.sqrt(VHD)
    for h in range(heads):
        first = (h * 3 + 2) * 128
        values[h] = jnp.transpose(qkv_ref[:, first : first + 128].astype(F32)).astype(BF16)

    def attend(b, carry):
        lanes = pl.ds(pl.multiple_of(b * LANES, LANES), LANES)
        for h in range(heads):
            first = h * 3 * 128
            query = qkv_ref[lanes, first : first + 128]
            keys = qkv_ref[:, first + 128 : first + 256]
            scores = lax.dot_general(
                keys, query, (((1,), (1,)), ((), ())), preferred_element_type=F32
            ) * scale
            expo = jnp.exp(scores - jnp.max(scores, axis=0, keepdims=True))
            summed = jnp.sum(expo, axis=0, keepdims=True)
            mix = jnp.dot(values[h], expo.astype(BF16), preferred_element_type=F32)
            rows = pl.ds(pl.multiple_of(me * deep + h * VHD, 16), VHD)
            held[rows, lanes] = (mix[:VHD] / summed).astype(BF16)
        for direction in range(2):
            @pl.when(has(direction))
            def _():
                pass_on(direction, 0, b).start()
        give(chip, b, core).start()
        return carry

    lax.fori_loop(0, blocks, attend, 0)

    def relay(hop):
        def body(piece, carry):
            for direction in range(2):
                @pl.when(exists(direction, hop))
                def _():
                    arrival(direction, hop, piece).wait_recv()
                    if hop < chips - 1:
                        @pl.when(has(direction))
                        def _():
                            pass_on(direction, hop, piece).start()
                    give(origin_of(direction, hop), piece, core).start()
            return carry

        lax.fori_loop(0, blocks, body, 0)

    def text_slot(place, which):
        return text_ref.at[pl.ds(pl.multiple_of((place * 2 + which) * each, 16), each)]

    def text_link(j):
        block = text_slot(plane, core)
        return remote(
            block, block, text_send.at[j], text_recv.at[j], beside((plane + j) % planes)
        )

    def text_from(j):
        block = text_slot((plane - j) % planes, core)
        return remote(block, block, text_send.at[j], text_recv.at[j], twin)

    def text_twin(j, which):
        block = text_slot((plane - j) % planes, which)
        return remote(block, block, twin_send.at[j], twin_recv.at[j], twin)

    def untail(block):
        block = block.astype(F32)
        return block[:8] + block[8:]

    def gain_from(direction):
        last_link(direction).wait_recv()

        def body(i, carry):
            rows = pl.ds(pl.multiple_of(i * 128, 128), 128)
            mine_sum[rows, :] += chain_in[direction, rows, :].astype(F32)
            return carry

        lax.fori_loop(0, each // 128, body, 0)
        squares[...] += untail(chain_in[direction, each:, :])

    def finish_text(sum_ref, square_ref):
        nonlocal mine_sum, squares
        mine_sum, squares = sum_ref, square_ref
        mine_sum[...] = mine_ref[...]
        squares[...] = sq_ref[...]
        for direction in range(2):
            @pl.when(has(1 - direction))
            def _():
                gain_from(direction)
        inverse = lax.rsqrt(squares[...] / D + EPS)
        for s in range(subs):
            factor = jnp.transpose(jnp.broadcast_to(inverse[s : s + 1], (128, SUBROWS)))
            place = pl.multiple_of((plane * 2 + core) * each + s * SUBROWS, 16)
            for side in range(2):
                lanes = slice(side * HD, (side + 1) * HD)
                value = mine_sum[s * SUBROWS : (s + 1) * SUBROWS, lanes] * factor
                text_ref[pl.ds(place, SUBROWS), lanes] = value.astype(BF16)

    mine_sum = squares = None
    pl.run_scoped(
        finish_text, pltpu.VMEM((each, 2 * HD), F32), pltpu.VMEM((8, SUBROWS), F32)
    )
    for j in range(1, planes):
        text_link(j).start()
    text_twin(0, core).start()

    relay(1)
    for k in range(1, chips):
        @pl.when(ctx < used)
        def _():
            line_part(k).wait_recv()
            for j in range(1, ctxs):
                from_line(k, j).start()
            to_twin(k, 0, core).start()

    def add_chip(origin, fresh):
        rows = pl.ds(pl.multiple_of(origin * 2 * deep, 16), 2 * deep)

        def body(i, carry):
            places = pl.ds(pl.multiple_of(i * LANES, LANES), LANES)
            product = lax.dot_general(
                held[rows, places], wall[rows, :], (((0,), (0,)), ((), ())),
                preferred_element_type=F32,
            )
            if fresh:
                product += patches_ref[places, :].astype(F32)
            for c in range(width // 128):
                lanes = product[:, c * 128 : (c + 1) * 128]
                mixed[c, places, :] = lanes if fresh else mixed[c, places, :] + lanes
            return carry

        lax.fori_loop(0, blocks, body, 0)

    def add_hop(hop):
        for direction in range(2 if hop else 1):
            @pl.when(exists(direction, hop))
            def _():
                origin = origin_of(direction, hop)
                for piece in range(blocks):
                    give(origin, piece, 1 - core).wait_recv()
                add_chip(origin, hop == 0)

    keep.wait()
    own_to_twin().wait_recv()
    add_hop(0)
    if chips > 2:
        relay(2)
    for j in range(1, planes):
        text_from(j).wait_recv()
        text_twin(j, core).start()
    for k in range(1, chips):
        for j in range(1, ctxs):
            @pl.when((ctx - j) % ctxs < used)
            def _():
                block = part((chip - k) % chips, core, (ctx - j) % ctxs)
                remote(
                    block, block, plane_send.at[k, j], plane_recv.at[k, j], twin
                ).wait_recv()
                to_twin(k, j, core).start()
    for k in range(1, chips):
        for j in range(ctxs):
            @pl.when((ctx - j) % ctxs < used)
            def _():
                to_twin(k, j, 1 - core).wait_recv()
    add_hop(1)
    for hop in range(3, chips):
        relay(hop)
        add_hop(hop - 1)
    if chips > 2:
        add_hop(chips - 1)

    load.wait()
    tokens = total // 4
    for r in range(4):
        def norm_rows(i, carry):
            every = pl.ds(i * 4 * LNROWS + r, LNROWS, stride=4)
            rows = jnp.concatenate([mixed[c, every, :] for c in range(width // 128)], axis=1)
            place = pl.ds(pl.multiple_of(i * LNROWS, LNROWS), LNROWS)
            merged[r, place, :] = layer_norm(rows, gain_ref[...]).astype(BF16)
            return carry

        lax.fori_loop(0, tokens // LNROWS, norm_rows, 0)

    def column(c, carry):
        lanes = pl.ds(pl.multiple_of(c * LANES, LANES), LANES)
        value = jnp.dot(merged[0], wmerge[:width, lanes], preferred_element_type=F32)
        for r in range(1, 4):
            value += jnp.dot(
                merged[r], wmerge[r * width : (r + 1) * width, lanes], preferred_element_type=F32
            )
        visual_ref[:, lanes] = value.astype(BF16)
        return carry

    lax.fori_loop(0, visual_ref.shape[1] // LANES, column, 0)

    for j in range(planes):
        text_twin(j, 1 - core).wait_recv()
        text_twin(j, core).wait_send()
        if j:
            text_link(j).wait_send()
    own_to_twin().wait_send()
    for k in range(1, chips):
        @pl.when(ctx < used)
        def _():
            line_part(k).wait_send()
            for j in range(1, ctxs):
                from_line(k, j).wait_send()
        for j in range(ctxs):
            @pl.when((ctx - j) % ctxs < used)
            def _():
                to_twin(k, j, core).wait_send()
    for direction in range(2):
        @pl.when(has(direction))
        def _():
            last_link(direction).wait_send()

    def drain(piece, carry):
        give(chip, piece, core).wait_send()
        for direction in range(2):
            for hop in range(chips):
                if hop < chips - 1:
                    @pl.when(jnp.logical_and(exists(direction, hop), has(direction)))
                    def _():
                        pass_on(direction, hop, piece).wait_send()
                if hop > 0:
                    @pl.when(exists(direction, hop))
                    def _():
                        give(origin_of(direction, hop), piece, core).wait_send()
        return carry

    lax.fori_loop(0, blocks, drain, 0)


def middle(qkv, gathered, w_out, merge_gain, w_merge, chain_last, mine, mine_sq, collective_id):
    sizes = tuple(lax.axis_size(name) for name in VIS)
    ctxs = lax.axis_size("ctx")
    chips, planes = sizes[0] * sizes[1], ctxs * sizes[1]
    total, width = qkv.shape[0], w_out.shape[1]
    each = mine.shape[0]
    blocks = total // LANES
    heads = w_out.shape[0] // VHD
    tokens = total // 4
    DMA = pltpu.SemaphoreType.DMA
    return pl.pallas_call(
        functools.partial(middle_kernel, sizes, ctxs),
        out_shape=[
            jax.ShapeDtypeStruct((tokens, w_merge.shape[1]), BF16),
            jax.ShapeDtypeStruct((planes * 2 * each, 2 * HD), BF16),
        ],
        in_specs=[VMEM] * 7 + [ANY],
        out_specs=[VMEM] * 2,
        scratch_shapes=[
            pltpu.VMEM((VD, total), BF16),
            pltpu.VMEM((VD, width), BF16),
            pltpu.VMEM(w_merge.shape, BF16),
            pltpu.VMEM((width // 128, total, 128), F32),
            pltpu.VMEM((4, tokens, width), BF16),
            pltpu.VMEM((heads, 128, total), BF16),
            pltpu.VMEM(chain_last.shape, BF16),
            DMA((2,)),
            DMA((2, chips, blocks)),
            DMA((2, chips, blocks)),
            DMA((chips, blocks)),
            DMA((chips, blocks)),
            DMA((2,)),
            DMA((2,)),
            DMA((chips,)),
            DMA((chips,)),
            DMA((chips, ctxs)),
            DMA((chips, ctxs)),
            DMA((chips, ctxs)),
            DMA((chips, ctxs)),
            DMA((planes,)),
            DMA((planes,)),
            DMA((planes,)),
            DMA((planes,)),
        ],
        compiler_params=pltpu.CompilerParams(
            collective_id=collective_id, has_side_effects=True, vmem_limit_bytes=52 * 2**20
        ),
    )(
        qkv, gathered.reshape(total, width), w_out, merge_gain.reshape(1, -1), chain_last, mine,
        mine_sq, w_merge,
    )


def project_kernel(joined, rows_ref, weight_ref, out_ref, *rest):
    each = rows_ref.shape[0]
    rows = rows_ref[...]
    floats = rows.astype(F32)
    squares = floats * floats
    coarse = squares.astype(BF16)
    fine = (squares - coarse.astype(F32)).astype(BF16)
    ones = jnp.ones((8, rows.shape[1]), BF16)
    dims = (((1,), (1,)), ((), ()))
    sums = lax.dot_general(ones, coarse, dims, preferred_element_type=F32)
    sums += lax.dot_general(ones, fine, dims, preferred_element_type=F32)
    for half in range(2):
        for pair in range(KVH // 2):
            first = (half * KVH + pair * 2) * HD
            raw = jnp.dot(
                rows, weight_ref[:, first : first + 2 * HD], preferred_element_type=F32
            ).astype(out_ref.dtype)
            for i in range(2):
                out_ref[pair * 2 + i, 0, :each, half * HD : (half + 1) * HD] = raw[
                    :, i * HD : (i + 1) * HD
                ]
    for h in range(KVH):
        if joined:
            out_ref[h, 0, each:, :] = sums[:, : 2 * HD]
            for part in range(1, each // (2 * HD)):
                out_ref[h, 0, each + part : each + part + 1, :] = sums[
                    :1, part * 2 * HD : (part + 1) * 2 * HD
                ]
        else:
            rest[0][h, 0] = sums


def project(rows, weight, parts, joined):
    count, depth = rows.shape
    each = count // parts
    if joined:
        shapes = [jax.ShapeDtypeStruct((KVH, parts, each + 8, 2 * HD), F32)]
    else:
        shapes = [
            jax.ShapeDtypeStruct((KVH, parts, each, 2 * HD), BF16),
            jax.ShapeDtypeStruct((KVH, parts, 8, each), F32),
        ]
    outs = pl.pallas_call(
        functools.partial(project_kernel, joined),
        grid=(parts,),
        out_shape=shapes,
        in_specs=[
            pl.BlockSpec((each, depth), lambda p: (p, 0)),
            pl.BlockSpec(weight.shape, lambda p: (0, 0)),
        ],
        out_specs=[
            pl.BlockSpec((KVH, 1) + shape.shape[2:], lambda p: (0, p, 0, 0)) for shape in shapes
        ],
        cost_estimate=pl.CostEstimate(
            flops=2 * count * depth * KVH * 2 * HD,
            bytes_accessed=count * depth * 10,
            transcendentals=0,
        ),
    )(rows, weight)
    return [out.reshape((KVH * parts,) + out.shape[2:]) for out in outs]


def whole_image(visual, weight, parts):
    pieces, squares = project(visual, weight, parts, False)
    pieces, squares = exchange((pieces, squares), VIS, False, 3)
    total = jnp.sum(pieces.astype(F32), axis=0)
    inverse = lax.rsqrt(jnp.sum(squares[:, 0, :], axis=0) / D + EPS)
    share = (total * inverse[:, None]).astype(BF16)
    (whole,) = exchange((share,), ("ctx",) + SUB, True, 4)
    return whole.reshape(-1, 2 * HD)


def per_device(
    patches,
    vis_gain,
    w_qkv,
    w_out,
    merge_gain,
    w_merge,
    token_dest,
    token_row,
    prompt_text,
    kv_gain,
    w_kv,
    queries,
    resp_kv,
    resp_len,
):
    parts = lax.axis_size("vh") * lax.axis_size("core")
    vis_count = lax.axis_size("vk") * parts
    ctx_count = lax.axis_size("ctx")
    vis_index = flat_index(VIS, tuple(lax.axis_size(name) for name in VIS))
    shard_rows = prompt_text.shape[0]

    qkv, gathered, chain_last, text_mine, text_sq = front(
        patches, vis_gain, w_qkv, prompt_text, kv_gain, w_kv, 0
    )
    visual, text_kv = middle(
        qkv, gathered, w_out, merge_gain, w_merge, chain_last, text_mine, text_sq, 1
    )
    weight = (w_kv.astype(F32) * kv_gain[:, None]).astype(BF16)

    image_kv = whole_image(visual, weight, parts)

    flat = (token_dest * shard_rows + token_row).reshape(-1)
    positions = jnp.arange(ctx_count * shard_rows, dtype=jnp.int32)
    taken = jnp.any(positions[:, None] == flat[None, :], axis=1)

    width = KVH * HD
    group = QH // KVH
    mine = QH // vis_count
    resp_rows = queries.shape[0]
    scale = 1.0 / math.sqrt(HD)
    query = lax.dynamic_slice_in_dim(queries, vis_index * mine * HD, mine * HD, 1)
    query = query.reshape(resp_rows, mine, HD).transpose(1, 0, 2).reshape(mine * resp_rows, HD)
    kv_head = (vis_index * mine) // group
    own_keys = lax.dynamic_slice_in_dim(resp_kv, kv_head * HD, HD, 1)
    own_values = lax.dynamic_slice_in_dim(resp_kv, width + kv_head * HD, HD, 1)
    early_keys = jnp.concatenate([text_kv[:, :HD], own_keys], axis=0)
    early_values = jnp.concatenate([text_kv[:, HD:], own_values], axis=0)
    query_positions = jnp.arange(resp_rows, dtype=jnp.int32)
    causal = query_positions[None, :] <= query_positions[:, None]
    visible = jnp.concatenate(
        [jnp.broadcast_to(~taken[None, :], (resp_rows, taken.shape[0])), causal], axis=1
    )
    visible = jnp.broadcast_to(visible[None], (mine,) + visible.shape).reshape(
        mine * resp_rows, -1
    )

    def scores_of(keys):
        return jnp.einsum("qd,kd->qk", query, keys, preferred_element_type=F32) * scale

    scores = jnp.where(visible, scores_of(early_keys), -1e30)
    early_high = jnp.max(scores, axis=1, keepdims=True)
    expo = jnp.where(visible, jnp.exp(scores - early_high), 0.0)
    early_sum = jnp.sum(expo, axis=1, keepdims=True)
    early_mix = jnp.dot(expo.astype(BF16), early_values, preferred_element_type=F32)

    late_scores = scores_of(image_kv[:, :HD])
    high = jnp.maximum(early_high, jnp.max(late_scores, axis=1, keepdims=True))
    late = jnp.exp(late_scores - high)
    fade = jnp.exp(early_high - high)
    summed = early_sum * fade + jnp.sum(late, axis=1, keepdims=True)
    mix = early_mix * fade + jnp.dot(
        late.astype(BF16), image_kv[:, HD:], preferred_element_type=F32
    )
    live = jnp.tile(query_positions < resp_len[0], mine)[:, None]
    result = jnp.where(live, mix / summed, 0.0).astype(BF16)
    result = result.reshape(mine, resp_rows, HD).transpose(1, 0, 2)
    whole = line_gather(result.reshape(resp_rows, mine * HD), 2, 5)
    return whole.transpose(1, 0, 2).reshape(resp_rows, QH * HD)


def solution(mesh):
    ctx_count, vis_count = mesh.shape["ctx"], mesh.shape["vis"]
    parts = vis_count // KVH
    shape = (ctx_count, vis_count // parts, parts // 2, 2)
    fine = Mesh(mesh.devices.reshape(shape), ("ctx",) + VIS)
    return jax.shard_map(
        per_device,
        mesh=fine,
        in_specs=(
            P(("ctx",) + VIS, None),
            P(),
            P(None, VIS),
            P(VIS, None),
            P(),
            P(None, VIS),
            P(),
            P(),
            P("ctx", VIS),
            P(VIS),
            P(VIS, None),
            P("ctx", None),
            P("ctx", None),
            P("ctx"),
        ),
        out_specs=P("ctx", None),
        check_vma=False,
    )
```

```python
import functools
import math

import jax
import jax.numpy as jnp
from jax import lax
from jax.experimental import pallas as pl
from jax.experimental.pallas import tpu as pltpu
from jax.sharding import Mesh, PartitionSpec as P

VD = 1280
D = 8192
HD = 128
QH = 32
KVH = 4
VHD = 80
MD = 5120


EPS = 1e-06
VIS = ("vk", "vh", "core")
MESH = pl.DeviceIdType.MESH
VMEM = pl.BlockSpec(memory_space=pltpu.VMEM)
ANY = pl.BlockSpec(memory_space=pl.ANY)
F32 = jnp.float32
BF16 = jnp.bfloat16
PIECES = 2
SUBROWS = 256
LNROWS = 64
LANES = 256
KEYS = 512


def layer_norm(values, gain):
    center = values - jnp.mean(values, axis=-1, keepdims=True)
    spread = jnp.mean(center * center, axis=-1, keepdims=True)
    return center * lax.rsqrt(spread + EPS) * gain


def front_kernel(sizes, *refs):
    (
        patches_ref, gain_ref, tgain_ref, wqkv_hbm, text_hbm, wkv_hbm,
        qkv_ref, held, chain_last, mine_ref, mine_sq,
        wqkv, wpad, text, wkv, normed, own, own_sq, pair_out, pair_in, chain_out, chain_in,
        load_sem, send_sem, recv_sem, near_send, near_recv, pair_sem, chain_send, chain_recv,
    ) = refs
    chips, vh = sizes[0] * sizes[1], sizes[1]
    core = lax.axis_index("core")
    chip = lax.axis_index("vk") * vh + lax.axis_index("vh")
    count = patches_ref.shape[0]
    half = count // PIECES
    each = mine_ref.shape[0]
    subs = each // SUBROWS

    def at(where, which):
        return {"vk": where // vh, "vh": where % vh, "core": which}

    def neighbour(direction):
        return chip + 1 if direction == 0 else chip - 1

    def has(direction):
        return chip < chips - 1 if direction == 0 else chip > 0

    def remote(src, dst, send, recv, where, which):
        return pltpu.make_async_remote_copy(
            src_ref=src, dst_ref=dst, send_sem=send, recv_sem=recv,
            device_id=at(where, which), device_id_type=MESH,
        )

    loads = [
        pltpu.make_async_copy(text_hbm, text, load_sem.at[0]),
        pltpu.make_async_copy(wkv_hbm, wkv, load_sem.at[1]),
        pltpu.make_async_copy(wqkv_hbm, wqkv, load_sem.at[2]),
    ]
    for load in loads:
        load.start()

    barrier = pltpu.get_barrier_semaphore()
    pl.semaphore_signal(barrier, inc=1, device_id=at(chip, 1 - core), device_id_type=MESH)
    for direction in range(2):
        @pl.when(has(direction))
        def _():
            pl.semaphore_signal(
                barrier, inc=1, device_id=at(neighbour(direction), core), device_id_type=MESH
            )
    pl.semaphore_wait(barrier, 1 + jnp.where(has(0), 1, 0) + jnp.where(has(1), 1, 0))

    def slot(origin, which, piece):
        return held.at[origin * 2 + which, pl.ds(piece * half, half)]

    def source(origin, piece, hop):
        return patches_ref.at[pl.ds(piece * half, half)] if hop == 0 else slot(origin, core, piece)

    def origin_of(direction, hop):
        return chip - hop if direction == 0 else chip + hop

    def exists(direction, hop):
        return chip >= hop if direction == 0 else chip + hop < chips

    def pass_on(direction, hop, piece):
        origin = origin_of(direction, hop)
        return remote(
            source(origin, piece, hop), slot(origin, core, piece),
            send_sem.at[direction, hop, piece], recv_sem.at[direction, hop, piece],
            neighbour(direction), core,
        )

    def arrival(direction, hop, piece):
        origin = origin_of(direction, hop)
        return remote(
            slot(origin, core, piece), slot(origin, core, piece),
            send_sem.at[direction, hop - 1, piece], recv_sem.at[direction, hop - 1, piece],
            chip, 1 - core,
        )

    def give(origin, piece, hop):
        return remote(
            source(origin, piece, hop), slot(origin, core, piece),
            near_send.at[origin, piece], near_recv.at[origin, piece], chip, 1 - core,
        )

    def taken(origin, piece):
        return remote(
            slot(origin, 1 - core, piece), slot(origin, 1 - core, piece),
            near_send.at[origin, piece], near_recv.at[origin, piece], chip, 1 - core,
        )

    for piece in range(PIECES):
        for direction in range(2):
            @pl.when(has(direction))
            def _():
                pass_on(direction, 0, piece).start()
    mine = pltpu.make_async_copy(patches_ref, held.at[chip * 2 + core], load_sem.at[3])
    mine.start()
    for piece in range(PIECES):
        give(chip, piece, 0).start()

    def relay(hop):
        for piece in range(PIECES):
            for direction in range(2):
                @pl.when(exists(direction, hop))
                def _():
                    arrival(direction, hop, piece).wait_recv()
                    if hop < chips - 1:
                        @pl.when(has(direction))
                        def _():
                            pass_on(direction, hop, piece).start()
                    give(origin_of(direction, hop), piece, hop).start()

    def text_rows(v, which, write):
        for s in range(subs):
            first = pl.multiple_of((v * 2 + which) * each + s * SUBROWS, SUBROWS)
            rows = text[pl.ds(first, SUBROWS), :].astype(F32)
            total = jnp.sum(rows * rows, axis=1, keepdims=True)
            line = jnp.transpose(jnp.broadcast_to(total, (SUBROWS, 128)))
            own_sq[v, s : s + 1, :] = line[0:1]
            scaled = (rows * tgain_ref[...]).astype(BF16)
            for side in range(2):
                for pair in range(KVH // 2):
                    begin = (side * KVH + pair * 2) * HD
                    raw = jnp.dot(scaled, wkv[:, begin : begin + 2 * HD], preferred_element_type=F32)
                    for i in range(2):
                        write((pair * 2 + i) * vh + v, s, side, raw[:, i * HD : (i + 1) * HD])

    def tail(total):
        coarse = total.astype(BF16).astype(F32)
        return jnp.concatenate([coarse, total - coarse], axis=0).astype(BF16)

    def untail(block):
        block = block.astype(F32)
        return block[:8] + block[8:]

    def write_pair(d, s, side, value):
        pair_out[d, s * SUBROWS : (s + 1) * SUBROWS, side * HD : (side + 1) * HD] = value.astype(BF16)

    def write_own(d, s, side, value):
        own[d, s * SUBROWS : (s + 1) * SUBROWS, side * HD : (side + 1) * HD] = value

    own_sq[...] = jnp.zeros_like(own_sq)
    loads[0].wait()
    loads[1].wait()
    for v in range(vh):
        text_rows(v, 1 - core, write_pair)
        for h in range(KVH):
            pair_out[h * vh + v, each:, :] = tail(own_sq[v])
    swap = remote(pair_out, pair_in, pair_sem.at[0], pair_sem.at[1], chip, 1 - core)
    swap.start()
    for v in range(vh):
        text_rows(v, core, write_own)

    loads[2].wait()
    wpad[...] = jnp.zeros_like(wpad)
    for part in range(wqkv.shape[1] // VHD):
        wpad[:, part * 128 : part * 128 + VHD] = wqkv[:, part * VHD : (part + 1) * VHD]

    def project(origin):
        def norm_rows(i, carry):
            which = i // (count // LNROWS)
            begin = pl.multiple_of((i % (count // LNROWS)) * LNROWS, LNROWS)
            floats = held[origin * 2 + which, pl.ds(begin, LNROWS), :].astype(F32)
            place = pl.multiple_of(i * LNROWS, LNROWS)
            normed[pl.ds(place, LNROWS), :] = layer_norm(floats, gain_ref[...]).astype(BF16)
            return carry

        lax.fori_loop(0, 2 * count // LNROWS, norm_rows, 0)
        first = pl.multiple_of(origin * 2 * count, 2 * count)
        qkv_ref[pl.ds(first, 2 * count), :] = jnp.dot(
            normed[...], wpad[...], preferred_element_type=F32
        ).astype(BF16)

    def project_hop(hop):
        for direction in range(2 if hop else 1):
            @pl.when(exists(direction, hop))
            def _():
                origin = origin_of(direction, hop)
                for piece in range(PIECES):
                    taken(origin, piece).wait_recv()
                project(origin)

    def link(direction, d):
        return remote(
            chain_out.at[direction, d], chain_in.at[direction, d],
            chain_send.at[direction, d], chain_recv.at[direction, d], neighbour(direction), core,
        )

    def sum_up(d, source, put, put_square):
        def body(i, carry):
            rows = pl.ds(pl.multiple_of(i * 128, 128), 128)
            value = own[d, rows, :] + pair_in[d, rows, :].astype(F32)
            if source is not None:
                value += source[rows, :].astype(F32)
            put(rows, value)
            return carry

        lax.fori_loop(0, each // 128, body, 0)
        square = own_sq[d % vh] + untail(pair_in[d, each:, :])
        if source is not None:
            square += untail(source[each:, :])
        put_square(square)

    def chain(step):
        for direction in range(2):
            rank = chip if direction == 0 else chips - 1 - chip
            ahead = chips - step
            d = chip + ahead if direction == 0 else chip - ahead
            last = step == chips - 1

            def block():
                return chain_last.at[direction] if last else chain_out.at[direction, d]

            def put(rows, value):
                block()[rows, :] = value.astype(BF16)

            def put_square(square):
                block()[each:, :] = tail(square)

            @pl.when(rank < step)
            def _():
                @pl.when(rank == 0)
                def _():
                    sum_up(d, None, put, put_square)

                if step > 1:
                    @pl.when(rank > 0)
                    def _():
                        link(direction, d).wait_recv()
                        sum_up(d, chain_in.at[direction, d], put, put_square)

                if not last:
                    link(direction, d).start()

    relay(1)
    swap.wait_recv()
    if chips > 2:
        chain(1)
    mine.wait()
    project_hop(0)
    for hop in range(2, chips):
        relay(hop)
        if hop < chips - 1:
            chain(hop)
        project_hop(hop - 1)

    def put_mine(rows, value):
        mine_ref[rows, :] = value

    def put_mine_square(square):
        mine_sq[...] = square

    sum_up(chip, None, put_mine, put_mine_square)
    chain(chips - 1)
    project_hop(chips - 1)

    swap.wait_send()
    for piece in range(PIECES):
        give(chip, piece, 0).wait_send()
        for direction in range(2):
            for hop in range(chips):
                if hop < chips - 1:
                    @pl.when(jnp.logical_and(exists(direction, hop), has(direction)))
                    def _():
                        pass_on(direction, hop, piece).wait_send()
                if hop > 0:
                    @pl.when(exists(direction, hop))
                    def _():
                        give(origin_of(direction, hop), piece, hop).wait_send()
    for direction in range(2):
        for d in range(chips):
            @pl.when(chip < d - 1 if direction == 0 else chip > d + 1)
            def _():
                link(direction, d).wait_send()


def front(patches, vis_gain, w_qkv, text, kv_gain, w_kv, collective_id):
    sizes = tuple(lax.axis_size(name) for name in VIS)
    chips = sizes[0] * sizes[1]
    parts = sizes[1] * 2
    count, width = patches.shape
    rows, features = text.shape
    each = rows // parts
    heads3 = w_qkv.shape[1] // VHD
    block = (each + 16, 2 * HD)
    DMA = pltpu.SemaphoreType.DMA
    return pl.pallas_call(
        functools.partial(front_kernel, sizes),
        out_shape=[
            jax.ShapeDtypeStruct((2 * chips * count, heads3 * 128), BF16),
            jax.ShapeDtypeStruct((2 * chips, count, width), BF16),
            jax.ShapeDtypeStruct((2,) + block, BF16),
            jax.ShapeDtypeStruct((each, 2 * HD), F32),
            jax.ShapeDtypeStruct((8, SUBROWS), F32),
        ],
        in_specs=[VMEM] * 3 + [ANY] * 3,
        out_specs=[VMEM] * 5,
        scratch_shapes=[
            pltpu.VMEM(w_qkv.shape, BF16),
            pltpu.VMEM((width, heads3 * 128), BF16),
            pltpu.VMEM(text.shape, BF16),
            pltpu.VMEM(w_kv.shape, BF16),
            pltpu.VMEM((2 * count, width), BF16),
            pltpu.VMEM((chips,) + (each, 2 * HD), F32),
            pltpu.VMEM((sizes[1], 8, SUBROWS), F32),
            pltpu.VMEM((chips,) + block, BF16),
            pltpu.VMEM((chips,) + block, BF16),
            pltpu.VMEM((2, chips) + block, BF16),
            pltpu.VMEM((2, chips) + block, BF16),
            DMA((4,)),
            DMA((2, chips, PIECES)),
            DMA((2, chips, PIECES)),
            DMA((chips, PIECES)),
            DMA((chips, PIECES)),
            DMA((2,)),
            DMA((2, chips)),
            DMA((2, chips)),
        ],
        compiler_params=pltpu.CompilerParams(
            collective_id=collective_id, has_side_effects=True, vmem_limit_bytes=48 * 2**20
        ),
    )(patches, vis_gain.reshape(1, -1), kv_gain.reshape(1, -1), w_qkv, text, w_kv)


def spread_of(rows, width, places):
    best = (1, 1)
    for down in range(1, rows // 16 + 1):
        for across in range(1, width // 128 + 1):
            if rows % (16 * down) or width % (128 * across) or down * across > places:
                continue
            if down * across > best[0] * best[1]:
                best = (down, across)
    return best


def middle_kernel(sizes, ctxs, *refs):
    (
        qkv_ref, patches_ref, wout_ref, gain_ref, chain_ref, mine_ref, sq_ref, wmerge_hbm,
        visual_ref, text_ref,
        held, wall, wmerge, mixed, merged, values, chain_in,
        load_sem, send_sem, recv_sem, near_send, near_recv, chain_send, chain_recv,
        line_send, line_recv, plane_send, plane_recv, pair_send, pair_recv,
        text_send, text_recv, twin_send, twin_recv,
    ) = refs
    chips, vh = sizes[0] * sizes[1], sizes[1]
    core, ctx = lax.axis_index("core"), lax.axis_index("ctx")
    vk_index, vh_index = lax.axis_index("vk"), lax.axis_index("vh")
    chip = vk_index * vh + vh_index
    me = chip * 2 + core
    each = mine_ref.shape[0]
    subs = each // SUBROWS
    deep, width = wout_ref.shape
    total = qkv_ref.shape[0]
    blocks = total // LANES
    heads = deep // VHD
    planes = ctxs * vh
    plane = ctx * vh + vh_index

    def at(where, which):
        return {"vk": where // vh, "vh": where % vh, "core": which}

    def beside(where):
        return {"ctx": where // vh, "vh": where % vh}

    def neighbour(direction):
        return chip + 1 if direction == 0 else chip - 1

    def has(direction):
        return chip < chips - 1 if direction == 0 else chip > 0

    def remote(src, dst, send, recv, device):
        return pltpu.make_async_remote_copy(
            src_ref=src, dst_ref=dst, send_sem=send, recv_sem=recv,
            device_id=device, device_id_type=MESH,
        )

    twin = at(chip, 1 - core)
    load = pltpu.make_async_copy(wmerge_hbm, wmerge, load_sem.at[0])
    load.start()
    my_rows = pl.ds(pl.multiple_of(me * deep, 16), deep)
    keep = pltpu.make_async_copy(wout_ref, wall.at[my_rows], load_sem.at[1])
    keep.start()

    barrier = pltpu.get_barrier_semaphore()
    pl.semaphore_signal(barrier, inc=1, device_id=twin, device_id_type=MESH)
    for k in range(1, chips):
        pl.semaphore_signal(
            barrier, inc=1, device_id=at((chip + k) % chips, core), device_id_type=MESH
        )
    for j in range(1, planes):
        pl.semaphore_signal(
            barrier, inc=1, device_id=beside((plane + j) % planes), device_id_type=MESH
        )
    pl.semaphore_wait(barrier, chips + planes - 1)

    def last_link(direction):
        return remote(
            chain_ref.at[direction], chain_in.at[direction],
            chain_send.at[direction], chain_recv.at[direction], at(neighbour(direction), core),
        )

    for direction in range(2):
        @pl.when(has(direction))
        def _():
            last_link(direction).start()

    down, across = spread_of(deep, width, ctxs)
    used, high, wide = down * across, deep // down, width // across

    def part(origin, which, index):
        first = pl.multiple_of((origin * 2 + which) * deep + (index // across) * high, 16)
        lane = pl.multiple_of((index % across) * wide, 128)
        return wall.at[pl.ds(first, high), pl.ds(lane, wide)]

    def line_part(k):
        first = pl.multiple_of((ctx // across) * high, 16)
        lane = pl.multiple_of((ctx % across) * wide, 128)
        return remote(
            wout_ref.at[pl.ds(first, high), pl.ds(lane, wide)], part(chip, core, ctx),
            line_send.at[k], line_recv.at[k], at((chip + k) % chips, core),
        )

    def from_line(k, j):
        block = part((chip - k) % chips, core, ctx)
        return remote(
            block, block, plane_send.at[k, j], plane_recv.at[k, j], {"ctx": (ctx + j) % ctxs}
        )

    def to_twin(k, j, which):
        block = part((chip - k) % chips, which, (ctx - j) % ctxs)
        return remote(block, block, pair_send.at[k, j], pair_recv.at[k, j], twin)

    def own_to_twin():
        return remote(wout_ref, wall.at[my_rows], pair_send.at[0, 0], pair_recv.at[0, 0], twin)

    for k in range(1, chips):
        @pl.when(ctx < used)
        def _():
            line_part(k).start()
    own_to_twin().start()

    def slot(origin, which, piece):
        first = pl.multiple_of((origin * 2 + which) * deep, 16)
        return held.at[pl.ds(first, deep), pl.ds(pl.multiple_of(piece * LANES, LANES), LANES)]

    def origin_of(direction, hop):
        return chip - hop if direction == 0 else chip + hop

    def exists(direction, hop):
        return chip >= hop if direction == 0 else chip + hop < chips

    def pass_on(direction, hop, piece):
        block = slot(origin_of(direction, hop), core, piece)
        return remote(
            block, block, send_sem.at[direction, hop, piece], recv_sem.at[direction, hop, piece],
            at(neighbour(direction), core),
        )

    def arrival(direction, hop, piece):
        block = slot(origin_of(direction, hop), core, piece)
        return remote(
            block, block, send_sem.at[direction, hop - 1, piece],
            recv_sem.at[direction, hop - 1, piece], twin,
        )

    def give(origin, piece, which):
        block = slot(origin, which, piece)
        return remote(
            block, block, near_send.at[origin, piece], near_recv.at[origin, piece], twin
        )

    scale = 1.0 / math.sqrt(VHD)
    for h in range(heads):
        first = (h * 3 + 2) * 128
        values[h] = jnp.transpose(qkv_ref[:, first : first + 128].astype(F32)).astype(BF16)

    def attend(b, carry):
        lanes = pl.ds(pl.multiple_of(b * LANES, LANES), LANES)
        for h in range(heads):
            first = h * 3 * 128
            query = qkv_ref[lanes, first : first + 128]
            keys = qkv_ref[:, first + 128 : first + 256]
            scores = lax.dot_general(
                keys, query, (((1,), (1,)), ((), ())), preferred_element_type=F32
            ) * scale
            expo = jnp.exp(scores - jnp.max(scores, axis=0, keepdims=True))
            summed = jnp.sum(expo, axis=0, keepdims=True)
            mix = jnp.dot(values[h], expo.astype(BF16), preferred_element_type=F32)
            rows = pl.ds(pl.multiple_of(me * deep + h * VHD, 16), VHD)
            held[rows, lanes] = (mix[:VHD] / summed).astype(BF16)
        for direction in range(2):
            @pl.when(has(direction))
            def _():
                pass_on(direction, 0, b).start()
        give(chip, b, core).start()
        return carry

    lax.fori_loop(0, blocks, attend, 0)

    def relay(hop):
        def body(piece, carry):
            for direction in range(2):
                @pl.when(exists(direction, hop))
                def _():
                    arrival(direction, hop, piece).wait_recv()
                    if hop < chips - 1:
                        @pl.when(has(direction))
                        def _():
                            pass_on(direction, hop, piece).start()
                    give(origin_of(direction, hop), piece, core).start()
            return carry

        lax.fori_loop(0, blocks, body, 0)

    def text_slot(place, which):
        return text_ref.at[pl.ds(pl.multiple_of((place * 2 + which) * each, 16), each)]

    def text_link(j):
        block = text_slot(plane, core)
        return remote(
            block, block, text_send.at[j], text_recv.at[j], beside((plane + j) % planes)
        )

    def text_from(j):
        block = text_slot((plane - j) % planes, core)
        return remote(block, block, text_send.at[j], text_recv.at[j], twin)

    def text_twin(j, which):
        block = text_slot((plane - j) % planes, which)
        return remote(block, block, twin_send.at[j], twin_recv.at[j], twin)

    def untail(block):
        block = block.astype(F32)
        return block[:8] + block[8:]

    def gain_from(direction):
        last_link(direction).wait_recv()

        def body(i, carry):
            rows = pl.ds(pl.multiple_of(i * 128, 128), 128)
            mine_sum[rows, :] += chain_in[direction, rows, :].astype(F32)
            return carry

        lax.fori_loop(0, each // 128, body, 0)
        squares[...] += untail(chain_in[direction, each:, :])

    def finish_text(sum_ref, square_ref):
        nonlocal mine_sum, squares
        mine_sum, squares = sum_ref, square_ref
        mine_sum[...] = mine_ref[...]
        squares[...] = sq_ref[...]
        for direction in range(2):
            @pl.when(has(1 - direction))
            def _():
                gain_from(direction)
        inverse = lax.rsqrt(squares[...] / D + EPS)
        for s in range(subs):
            factor = jnp.transpose(jnp.broadcast_to(inverse[s : s + 1], (128, SUBROWS)))
            place = pl.multiple_of((plane * 2 + core) * each + s * SUBROWS, 16)
            for side in range(2):
                lanes = slice(side * HD, (side + 1) * HD)
                value = mine_sum[s * SUBROWS : (s + 1) * SUBROWS, lanes] * factor
                text_ref[pl.ds(place, SUBROWS), lanes] = value.astype(BF16)

    mine_sum = squares = None
    pl.run_scoped(
        finish_text, pltpu.VMEM((each, 2 * HD), F32), pltpu.VMEM((8, SUBROWS), F32)
    )
    for j in range(1, planes):
        text_link(j).start()
    text_twin(0, core).start()

    relay(1)
    for k in range(1, chips):
        @pl.when(ctx < used)
        def _():
            line_part(k).wait_recv()
            for j in range(1, ctxs):
                from_line(k, j).start()
            to_twin(k, 0, core).start()

    def add_chip(origin, fresh):
        rows = pl.ds(pl.multiple_of(origin * 2 * deep, 16), 2 * deep)

        def body(i, carry):
            places = pl.ds(pl.multiple_of(i * LANES, LANES), LANES)
            product = lax.dot_general(
                held[rows, places], wall[rows, :], (((0,), (0,)), ((), ())),
                preferred_element_type=F32,
            )
            if fresh:
                product += patches_ref[places, :].astype(F32)
            for c in range(width // 128):
                lanes = product[:, c * 128 : (c + 1) * 128]
                mixed[c, places, :] = lanes if fresh else mixed[c, places, :] + lanes
            return carry

        lax.fori_loop(0, blocks, body, 0)

    def add_hop(hop):
        for direction in range(2 if hop else 1):
            @pl.when(exists(direction, hop))
            def _():
                origin = origin_of(direction, hop)
                for piece in range(blocks):
                    give(origin, piece, 1 - core).wait_recv()
                add_chip(origin, hop == 0)

    keep.wait()
    own_to_twin().wait_recv()
    add_hop(0)
    if chips > 2:
        relay(2)
    for j in range(1, planes):
        text_from(j).wait_recv()
        text_twin(j, core).start()
    for k in range(1, chips):
        for j in range(1, ctxs):
            @pl.when((ctx - j) % ctxs < used)
            def _():
                block = part((chip - k) % chips, core, (ctx - j) % ctxs)
                remote(
                    block, block, plane_send.at[k, j], plane_recv.at[k, j], twin
                ).wait_recv()
                to_twin(k, j, core).start()
    for k in range(1, chips):
        for j in range(ctxs):
            @pl.when((ctx - j) % ctxs < used)
            def _():
                to_twin(k, j, 1 - core).wait_recv()
    add_hop(1)
    for hop in range(3, chips):
        relay(hop)
        add_hop(hop - 1)
    if chips > 2:
        add_hop(chips - 1)

    load.wait()
    tokens = total // 4
    for r in range(4):
        def norm_rows(i, carry):
            every = pl.ds(i * 4 * LNROWS + r, LNROWS, stride=4)
            rows = jnp.concatenate([mixed[c, every, :] for c in range(width // 128)], axis=1)
            place = pl.ds(pl.multiple_of(i * LNROWS, LNROWS), LNROWS)
            merged[r, place, :] = layer_norm(rows, gain_ref[...]).astype(BF16)
            return carry

        lax.fori_loop(0, tokens // LNROWS, norm_rows, 0)

    def column(c, carry):
        lanes = pl.ds(pl.multiple_of(c * LANES, LANES), LANES)
        value = jnp.dot(merged[0], wmerge[:width, lanes], preferred_element_type=F32)
        for r in range(1, 4):
            value += jnp.dot(
                merged[r], wmerge[r * width : (r + 1) * width, lanes], preferred_element_type=F32
            )
        visual_ref[:, lanes] = value.astype(BF16)
        return carry

    lax.fori_loop(0, visual_ref.shape[1] // LANES, column, 0)

    for j in range(planes):
        text_twin(j, 1 - core).wait_recv()
        text_twin(j, core).wait_send()
        if j:
            text_link(j).wait_send()
    own_to_twin().wait_send()
    for k in range(1, chips):
        @pl.when(ctx < used)
        def _():
            line_part(k).wait_send()
            for j in range(1, ctxs):
                from_line(k, j).wait_send()
        for j in range(ctxs):
            @pl.when((ctx - j) % ctxs < used)
            def _():
                to_twin(k, j, core).wait_send()
    for direction in range(2):
        @pl.when(has(direction))
        def _():
            last_link(direction).wait_send()

    def drain(piece, carry):
        give(chip, piece, core).wait_send()
        for direction in range(2):
            for hop in range(chips):
                if hop < chips - 1:
                    @pl.when(jnp.logical_and(exists(direction, hop), has(direction)))
                    def _():
                        pass_on(direction, hop, piece).wait_send()
                if hop > 0:
                    @pl.when(exists(direction, hop))
                    def _():
                        give(origin_of(direction, hop), piece, core).wait_send()
        return carry

    lax.fori_loop(0, blocks, drain, 0)


def middle(qkv, gathered, w_out, merge_gain, w_merge, chain_last, mine, mine_sq, collective_id):
    sizes = tuple(lax.axis_size(name) for name in VIS)
    ctxs = lax.axis_size("ctx")
    chips, planes = sizes[0] * sizes[1], ctxs * sizes[1]
    total, width = qkv.shape[0], w_out.shape[1]
    each = mine.shape[0]
    blocks = total // LANES
    heads = w_out.shape[0] // VHD
    tokens = total // 4
    DMA = pltpu.SemaphoreType.DMA
    return pl.pallas_call(
        functools.partial(middle_kernel, sizes, ctxs),
        out_shape=[
            jax.ShapeDtypeStruct((tokens, w_merge.shape[1]), BF16),
            jax.ShapeDtypeStruct((planes * 2 * each, 2 * HD), BF16),
        ],
        in_specs=[VMEM] * 7 + [ANY],
        out_specs=[VMEM] * 2,
        scratch_shapes=[
            pltpu.VMEM((VD, total), BF16),
            pltpu.VMEM((VD, width), BF16),
            pltpu.VMEM(w_merge.shape, BF16),
            pltpu.VMEM((width // 128, total, 128), F32),
            pltpu.VMEM((4, tokens, width), BF16),
            pltpu.VMEM((heads, 128, total), BF16),
            pltpu.VMEM(chain_last.shape, BF16),
            DMA((2,)),
            DMA((2, chips, blocks)),
            DMA((2, chips, blocks)),
            DMA((chips, blocks)),
            DMA((chips, blocks)),
            DMA((2,)),
            DMA((2,)),
            DMA((chips,)),
            DMA((chips,)),
            DMA((chips, ctxs)),
            DMA((chips, ctxs)),
            DMA((chips, ctxs)),
            DMA((chips, ctxs)),
            DMA((planes,)),
            DMA((planes,)),
            DMA((planes,)),
            DMA((planes,)),
        ],
        compiler_params=pltpu.CompilerParams(
            collective_id=collective_id, has_side_effects=True, vmem_limit_bytes=52 * 2**20
        ),
    )(
        qkv, gathered.reshape(total, width), w_out, merge_gain.reshape(1, -1), chain_last, mine,
        mine_sq, w_merge,
    )


def tail_kernel(sizes, ctxs, mine, shard_rows, *refs):
    (
        visual_ref, tgain_ref, dest_ref, row_ref, len_ref, text_ref, wkv_hbm, query_hbm, own_hbm,
        out_ref,
        wkv, query_in, query, own_kv, bias, image, own, own_sq, pair_out, pair_in, line_out, line_in,
        high, summed, mix,
        load_sem, swap_sem, line_send, line_recv, plane_send, plane_recv, twin_send, twin_recv,
        send_sem, recv_sem, near_send, near_recv,
    ) = refs
    chips, vh = sizes[0] * sizes[1], sizes[1]
    core, ctx = lax.axis_index("core"), lax.axis_index("ctx")
    vh_index = lax.axis_index("vh")
    chip = lax.axis_index("vk") * vh + vh_index
    me = chip * 2 + core
    parts = 2 * vh
    each = visual_ref.shape[0] // parts
    planes = ctxs * vh
    plane = ctx * vh + vh_index
    resp = query_in.shape[0]
    group = QH // KVH

    def at(where, which):
        return {"vk": where // vh, "vh": where % vh, "core": which}

    def beside(where):
        return {"ctx": where // vh, "vh": where % vh}

    def neighbour(direction):
        return chip + 1 if direction == 0 else chip - 1

    def has(direction):
        return chip < chips - 1 if direction == 0 else chip > 0

    def remote(src, dst, send, recv, device):
        return pltpu.make_async_remote_copy(
            src_ref=src, dst_ref=dst, send_sem=send, recv_sem=recv,
            device_id=device, device_id_type=MESH,
        )

    twin = at(chip, 1 - core)
    lane = pl.multiple_of(me * mine * HD, HD)
    head = pl.multiple_of(((me * mine) // group) * HD, HD)
    loads = [
        pltpu.make_async_copy(wkv_hbm, wkv, load_sem.at[0]),
        pltpu.make_async_copy(query_hbm.at[:, pl.ds(lane, mine * HD)], query_in, load_sem.at[1]),
        pltpu.make_async_copy(own_hbm.at[:, pl.ds(head, HD)], own_kv.at[0], load_sem.at[2]),
        pltpu.make_async_copy(
            own_hbm.at[:, pl.ds(pl.multiple_of(KVH * HD + head, HD), HD)], own_kv.at[1], load_sem.at[3]
        ),
    ]
    for load in loads:
        load.start()

    barrier = pltpu.get_barrier_semaphore()
    pl.semaphore_signal(barrier, inc=1, device_id=twin, device_id_type=MESH)
    for k in range(1, chips):
        pl.semaphore_signal(
            barrier, inc=1, device_id=at((chip + k) % chips, core), device_id_type=MESH
        )
    for j in range(1, planes):
        pl.semaphore_signal(
            barrier, inc=1, device_id=beside((plane + j) % planes), device_id_type=MESH
        )
    pl.semaphore_wait(barrier, chips + planes - 1)

    def token_rows(v, which, write):
        first = pl.multiple_of((v * 2 + which) * each, each)
        rows = visual_ref[pl.ds(first, each), :].astype(F32)
        total = jnp.sum(rows * rows, axis=1, keepdims=True)
        own_sq[v, 0:1, :each] = jnp.transpose(jnp.broadcast_to(total, (each, 128)))[0:1]
        scaled = (rows * tgain_ref[...]).astype(BF16)
        for side in range(2):
            for pair in range(KVH // 2):
                begin = (side * KVH + pair * 2) * HD
                raw = jnp.dot(scaled, wkv[:, begin : begin + 2 * HD], preferred_element_type=F32)
                for i in range(2):
                    write((pair * 2 + i) * vh + v, side, raw[:, i * HD : (i + 1) * HD])

    def split(total):
        coarse = total.astype(BF16).astype(F32)
        return jnp.concatenate([coarse, total - coarse], axis=0).astype(BF16)

    def joined(block):
        block = block.astype(F32)
        return block[:8] + block[8:]

    def write_pair(d, side, value):
        pair_out[d, :each, side * HD : (side + 1) * HD] = value.astype(BF16)

    def write_own(d, side, value):
        own[d, :, side * HD : (side + 1) * HD] = value

    own_sq[...] = jnp.zeros_like(own_sq)
    loads[0].wait()
    for v in range(vh):
        token_rows(v, 1 - core, write_pair)
        for h in range(KVH):
            pair_out[h * vh + v, each:, :] = split(own_sq[v])
    swap = remote(pair_out, pair_in, swap_sem.at[0], swap_sem.at[1], twin)
    swap.start()
    for v in range(vh):
        token_rows(v, core, write_own)
    for load in loads[1:]:
        load.wait()
    for j in range(mine):
        query[j * resp : (j + 1) * resp, :] = query_in[:, j * HD : (j + 1) * HD]

    def line_link(k):
        d = (chip + k) % chips
        return remote(
            line_out.at[d], line_in.at[k], line_send.at[k], line_recv.at[k], at(d, core)
        )

    swap.wait_recv()
    for k in range(1, chips):
        d = (chip + k) % chips
        line_out[d, :each, :] = (own[d] + pair_in[d, :each, :].astype(F32)).astype(BF16)
        line_out[d, each:, :] = split(own_sq[d % vh] + joined(pair_in[d, each:, :]))
        line_link(k).start()

    groups = bias.shape[0] // 128
    padded = -(-groups // 128) * 128
    count = jnp.zeros((128, padded), F32)
    for i in range(dest_ref.shape[0]):
        flat = dest_ref[i : i + 1, :] * shard_rows + row_ref[i : i + 1, :]
        low = lax.broadcasted_iota(jnp.int32, (128, flat.shape[1]), 0) == flat % 128
        upper = lax.broadcasted_iota(jnp.int32, (padded, flat.shape[1]), 0) == flat // 128
        count += lax.dot_general(
            jnp.where(low, 1.0, 0.0).astype(BF16), jnp.where(upper, 1.0, 0.0).astype(BF16),
            (((1,), (1,)), ((), ())), preferred_element_type=F32,
        )
    hidden = jnp.where(count > 0.5, -1e30, 0.0)
    for g in range(groups):
        bias[g * 128 : (g + 1) * 128, :] = jnp.broadcast_to(hidden[:, g : g + 1], (128, 128))

    high[...] = jnp.full_like(high, -1e30)
    summed[...] = jnp.zeros_like(summed)
    mix[...] = jnp.zeros_like(mix)
    scale = 1.0 / math.sqrt(HD)

    def attend(keys, values, mask):
        scores = lax.dot_general(
            keys, query[...], (((1,), (1,)), ((), ())), preferred_element_type=F32
        ) * scale
        scores = mask(scores)
        top = jnp.maximum(high[...], jnp.max(scores, axis=0, keepdims=True))
        fade = jnp.exp(high[...] - top)
        expo = jnp.exp(scores - top)
        high[...] = top
        summed[...] = summed[...] * fade + jnp.sum(expo, axis=0, keepdims=True)
        mix[...] = mix[...] * fade + jnp.dot(
            jnp.transpose(values.astype(F32)).astype(BF16), expo.astype(BF16),
            preferred_element_type=F32,
        )

    def causal(scores):
        key = lax.broadcasted_iota(jnp.int32, scores.shape, 0)
        place = lax.broadcasted_iota(jnp.int32, scores.shape, 1) % resp
        return jnp.where(key <= place, scores, -1e30)

    def text_chunk(i, carry):
        rows = pl.ds(pl.multiple_of(i * KEYS, KEYS), KEYS)
        attend(text_ref[rows, :HD], text_ref[rows, HD:], lambda scores: scores + bias[rows, 0:1])
        return carry

    chunks = text_ref.shape[0] // KEYS
    early = chunks * 3 // 4
    attend(own_kv[0], own_kv[1], causal)
    lax.fori_loop(0, early, text_chunk, 0)

    def slot(place, which):
        return image.at[pl.ds(pl.multiple_of((place * 2 + which) * each, 16), each)]

    def plane_link(j):
        block = slot(plane, core)
        return remote(
            block, block, plane_send.at[j], plane_recv.at[j], beside((plane + j) % planes)
        )

    def plane_from(j):
        block = slot((plane - j) % planes, core)
        return remote(block, block, plane_send.at[j], plane_recv.at[j], twin)

    def twin_link(j, which):
        block = slot((plane - j) % planes, which)
        return remote(block, block, twin_send.at[j], twin_recv.at[j], twin)

    for k in range(1, chips):
        line_link(k).wait_recv()
    total = own[chip] + pair_in[chip, :each, :].astype(F32)
    square = own_sq[chip % vh] + joined(pair_in[chip, each:, :])
    for k in range(1, chips):
        total += line_in[k, :each, :].astype(F32)
        square += joined(line_in[k, each:, :])
    inverse = lax.rsqrt(square / D + EPS)
    factor = jnp.transpose(jnp.broadcast_to(inverse[0:1, :each], (128, each)))
    place = pl.multiple_of((plane * 2 + core) * each, 16)
    for side in range(2):
        lanes = slice(side * HD, (side + 1) * HD)
        image[pl.ds(place, each), lanes] = (total[:, lanes] * factor).astype(BF16)
    for j in range(1, planes):
        plane_link(j).start()
    twin_link(0, core).start()
    lax.fori_loop(early, chunks, text_chunk, 0)
    for j in range(1, planes):
        plane_from(j).wait_recv()
        twin_link(j, core).start()
    for j in range(planes):
        twin_link(j, 1 - core).wait_recv()

    def image_chunk(i, carry):
        rows = pl.ds(pl.multiple_of(i * KEYS, KEYS), KEYS)
        attend(image[rows, :HD], image[rows, HD:], lambda scores: scores)
        return carry

    lax.fori_loop(0, image.shape[0] // KEYS, image_chunk, 0)

    piece_width = mine * HD // 2

    def result_slot(origin, which, piece):
        first = ((origin * 2 + which) * 2 + piece) * piece_width
        return out_ref.at[:, pl.ds(pl.multiple_of(first, 128), piece_width)]

    def origin_of(direction, hop):
        return chip - hop if direction == 0 else chip + hop

    def exists(direction, hop):
        return chip >= hop if direction == 0 else chip + hop < chips

    def pass_on(direction, hop, piece):
        block = result_slot(origin_of(direction, hop), core, piece)
        return remote(
            block, block, send_sem.at[direction, hop, piece], recv_sem.at[direction, hop, piece],
            at(neighbour(direction), core),
        )

    def arrival(direction, hop, piece):
        block = result_slot(origin_of(direction, hop), core, piece)
        return remote(
            block, block, send_sem.at[direction, hop - 1, piece],
            recv_sem.at[direction, hop - 1, piece], twin,
        )

    def give(origin, piece, which):
        block = result_slot(origin, which, piece)
        return remote(
            block, block, near_send.at[origin, piece], near_recv.at[origin, piece], twin
        )

    live = lax.broadcasted_iota(jnp.int32, (resp, HD), 0) < len_ref[0]
    for piece in range(2):
        for j in range(piece * mine // 2, (piece + 1) * mine // 2):
            lanes = slice(j * resp, (j + 1) * resp)
            value = jnp.transpose(mix[:, lanes] / summed[:, lanes])
            out_ref[:, pl.ds(pl.multiple_of(lane + j * HD, HD), HD)] = jnp.where(
                live, value, 0.0
            ).astype(BF16)
        for direction in range(2):
            @pl.when(has(direction))
            def _():
                pass_on(direction, 0, piece).start()
        give(chip, piece, core).start()
    for hop in range(1, chips):
        for piece in range(2):
            for direction in range(2):
                @pl.when(exists(direction, hop))
                def _():
                    arrival(direction, hop, piece).wait_recv()
                    if hop < chips - 1:
                        @pl.when(has(direction))
                        def _():
                            pass_on(direction, hop, piece).start()
                    give(origin_of(direction, hop), piece, core).start()

    swap.wait_send()
    for k in range(1, chips):
        line_link(k).wait_send()
    for j in range(planes):
        twin_link(j, core).wait_send()
        if j:
            plane_link(j).wait_send()
    for piece in range(2):
        for origin in range(chips):
            give(origin, piece, 1 - core).wait_recv()
        give(chip, piece, core).wait_send()
        for direction in range(2):
            for hop in range(chips):
                if hop < chips - 1:
                    @pl.when(jnp.logical_and(exists(direction, hop), has(direction)))
                    def _():
                        pass_on(direction, hop, piece).wait_send()
                if hop > 0:
                    @pl.when(exists(direction, hop))
                    def _():
                        give(origin_of(direction, hop), piece, core).wait_send()


def tail(visual, kv_gain, token_dest, token_row, resp_len, text_kv, w_kv, queries, resp_kv, shard_rows, collective_id):
    sizes = tuple(lax.axis_size(name) for name in VIS)
    ctxs = lax.axis_size("ctx")
    chips, planes = sizes[0] * sizes[1], ctxs * sizes[1]
    each = visual.shape[0] // (2 * sizes[1])
    mine = QH // (2 * chips)
    resp = queries.shape[0]
    block = (chips, each + 16, 2 * HD)
    DMA = pltpu.SemaphoreType.DMA
    return pl.pallas_call(
        functools.partial(tail_kernel, sizes, ctxs, mine, shard_rows),
        out_shape=jax.ShapeDtypeStruct((resp, QH * HD), BF16),
        in_specs=[VMEM] * 4 + [pl.BlockSpec(memory_space=pltpu.SMEM), VMEM] + [ANY] * 3,
        out_specs=VMEM,
        scratch_shapes=[
            pltpu.VMEM(w_kv.shape, BF16),
            pltpu.VMEM((resp, mine * HD), BF16),
            pltpu.VMEM((mine * resp, HD), BF16),
            pltpu.VMEM((2, resp, HD), BF16),
            pltpu.VMEM((ctxs * shard_rows, 128), F32),
            pltpu.VMEM((planes * 2 * each, 2 * HD), BF16),
            pltpu.VMEM((chips, each, 2 * HD), F32),
            pltpu.VMEM((sizes[1], 8, 2 * HD), F32),
            pltpu.VMEM(block, BF16),
            pltpu.VMEM(block, BF16),
            pltpu.VMEM(block, BF16),
            pltpu.VMEM(block, BF16),
            pltpu.VMEM((1, mine * resp), F32),
            pltpu.VMEM((1, mine * resp), F32),
            pltpu.VMEM((HD, mine * resp), F32),
            DMA((4,)),
            DMA((2,)),
            DMA((chips,)),
            DMA((chips,)),
            DMA((planes,)),
            DMA((planes,)),
            DMA((planes,)),
            DMA((planes,)),
            DMA((2, chips, 2)),
            DMA((2, chips, 2)),
            DMA((chips, 2)),
            DMA((chips, 2)),
        ],
        compiler_params=pltpu.CompilerParams(
            collective_id=collective_id, has_side_effects=True, vmem_limit_bytes=48 * 2**20
        ),
    )(
        visual, kv_gain.reshape(1, -1), token_dest, token_row, resp_len, text_kv, w_kv, queries,
        resp_kv,
    )


def per_device(
    patches,
    vis_gain,
    w_qkv,
    w_out,
    merge_gain,
    w_merge,
    token_dest,
    token_row,
    prompt_text,
    kv_gain,
    w_kv,
    queries,
    resp_kv,
    resp_len,
):
    qkv, gathered, chain_last, text_mine, text_sq = front(
        patches, vis_gain, w_qkv, prompt_text, kv_gain, w_kv, 0
    )
    visual, text_kv = middle(
        qkv, gathered, w_out, merge_gain, w_merge, chain_last, text_mine, text_sq, 1
    )
    return tail(
        visual, kv_gain, token_dest, token_row, resp_len, text_kv, w_kv, queries, resp_kv,
        prompt_text.shape[0], 2
    )


def solution(mesh):
    ctx_count, vis_count = mesh.shape["ctx"], mesh.shape["vis"]
    parts = vis_count // KVH
    shape = (ctx_count, vis_count // parts, parts // 2, 2)
    fine = Mesh(mesh.devices.reshape(shape), ("ctx",) + VIS)
    return jax.shard_map(
        per_device,
        mesh=fine,
        in_specs=(
            P(("ctx",) + VIS, None),
            P(),
            P(None, VIS),
            P(VIS, None),
            P(),
            P(None, VIS),
            P(),
            P(),
            P("ctx", VIS),
            P(VIS),
            P(VIS, None),
            P("ctx", None),
            P("ctx", None),
            P("ctx"),
        ),
        out_specs=P("ctx", None),
        check_vma=False,
    )
```

```python
import functools
import math

import jax
import jax.numpy as jnp
from jax import lax
from jax.experimental import pallas as pl
from jax.experimental.pallas import tpu as pltpu
from jax.sharding import Mesh, PartitionSpec as P

VD = 1280
D = 8192
HD = 128
QH = 32
KVH = 4
VHD = 80
MD = 5120


EPS = 1e-06
VIS = ("vk", "vh", "core")
MESH = pl.DeviceIdType.MESH
VMEM = pl.BlockSpec(memory_space=pltpu.VMEM)
ANY = pl.BlockSpec(memory_space=pl.ANY)
HBM = pl.BlockSpec(memory_space=pltpu.MemorySpace.HBM)
F32 = jnp.float32
BF16 = jnp.bfloat16
PIECES = 2
SUBROWS = 256
LNROWS = 64
LANES = 256
KEYS = 512


def layer_norm(values, gain):
    center = values - jnp.mean(values, axis=-1, keepdims=True)
    spread = jnp.mean(center * center, axis=-1, keepdims=True)
    return center * lax.rsqrt(spread + EPS) * gain


def front_kernel(sizes, *refs):
    (
        patches_ref, gain_ref, tgain_ref, wqkv_hbm, text_hbm, wkv_hbm,
        qkv_ref, held, chain_last, mine_ref, mine_sq,
        wpad, text, wkv, normed, own, own_sq, pair_out, pair_in, chain_out, chain_in,
        load_sem, send_sem, recv_sem, near_send, near_recv, pair_sem, chain_send, chain_recv,
    ) = refs
    chips, vh = sizes[0] * sizes[1], sizes[1]
    core = lax.axis_index("core")
    chip = lax.axis_index("vk") * vh + lax.axis_index("vh")
    count = patches_ref.shape[0]
    half = count // PIECES
    each = mine_ref.shape[0]
    subs = each // SUBROWS

    def at(where, which):
        return {"vk": where // vh, "vh": where % vh, "core": which}

    def neighbour(direction):
        return chip + 1 if direction == 0 else chip - 1

    def has(direction):
        return chip < chips - 1 if direction == 0 else chip > 0

    def remote(src, dst, send, recv, where, which):
        return pltpu.make_async_remote_copy(
            src_ref=src, dst_ref=dst, send_sem=send, recv_sem=recv,
            device_id=at(where, which), device_id_type=MESH,
        )

    loads = [
        pltpu.make_async_copy(text_hbm, text, load_sem.at[0]),
        pltpu.make_async_copy(wkv_hbm, wkv, load_sem.at[1]),
    ] + [
        pltpu.make_async_copy(
            wqkv_hbm.at[pl.ds(part * VHD, VHD)], wpad.at[pl.ds(part * 128, VHD)],
            load_sem.at[2 + part],
        )
        for part in range(wqkv_hbm.shape[0] // VHD)
    ]
    for load in loads:
        load.start()

    barrier = pltpu.get_barrier_semaphore()
    pl.semaphore_signal(barrier, inc=1, device_id=at(chip, 1 - core), device_id_type=MESH)
    for direction in range(2):
        @pl.when(has(direction))
        def _():
            pl.semaphore_signal(
                barrier, inc=1, device_id=at(neighbour(direction), core), device_id_type=MESH
            )
    pl.semaphore_wait(barrier, 1 + jnp.where(has(0), 1, 0) + jnp.where(has(1), 1, 0))

    def slot(origin, which, piece):
        return held.at[origin * 2 + which, pl.ds(piece * half, half)]

    def source(origin, piece, hop):
        return patches_ref.at[pl.ds(piece * half, half)] if hop == 0 else slot(origin, core, piece)

    def origin_of(direction, hop):
        return chip - hop if direction == 0 else chip + hop

    def exists(direction, hop):
        return chip >= hop if direction == 0 else chip + hop < chips

    def pass_on(direction, hop, piece):
        origin = origin_of(direction, hop)
        return remote(
            source(origin, piece, hop), slot(origin, core, piece),
            send_sem.at[direction, hop, piece], recv_sem.at[direction, hop, piece],
            neighbour(direction), core,
        )

    def arrival(direction, hop, piece):
        origin = origin_of(direction, hop)
        return remote(
            slot(origin, core, piece), slot(origin, core, piece),
            send_sem.at[direction, hop - 1, piece], recv_sem.at[direction, hop - 1, piece],
            chip, 1 - core,
        )

    def give(origin, piece, hop):
        return remote(
            source(origin, piece, hop), slot(origin, core, piece),
            near_send.at[origin, piece], near_recv.at[origin, piece], chip, 1 - core,
        )

    def taken(origin, piece):
        return remote(
            slot(origin, 1 - core, piece), slot(origin, 1 - core, piece),
            near_send.at[origin, piece], near_recv.at[origin, piece], chip, 1 - core,
        )

    for piece in range(PIECES):
        for direction in range(2):
            @pl.when(has(direction))
            def _():
                pass_on(direction, 0, piece).start()
    mine = pltpu.make_async_copy(patches_ref, held.at[chip * 2 + core], load_sem.at[len(loads)])
    mine.start()
    for piece in range(PIECES):
        give(chip, piece, 0).start()

    def relay(hop):
        for piece in range(PIECES):
            for direction in range(2):
                @pl.when(exists(direction, hop))
                def _():
                    arrival(direction, hop, piece).wait_recv()
                    if hop < chips - 1:
                        @pl.when(has(direction))
                        def _():
                            pass_on(direction, hop, piece).start()
                    give(origin_of(direction, hop), piece, hop).start()

    def text_rows(v, which, write):
        for s in range(subs):
            first = pl.multiple_of((v * 2 + which) * each + s * SUBROWS, SUBROWS)
            rows = text[pl.ds(first, SUBROWS), :].astype(F32)
            total = jnp.sum(rows * rows, axis=1, keepdims=True)
            line = jnp.transpose(jnp.broadcast_to(total, (SUBROWS, 128)))
            own_sq[v, s : s + 1, :] = line[0:1]
            scaled = (rows * tgain_ref[...]).astype(BF16)
            for side in range(2):
                for pair in range(KVH // 2):
                    begin = (side * KVH + pair * 2) * HD
                    raw = jnp.dot(scaled, wkv[:, begin : begin + 2 * HD], preferred_element_type=F32)
                    for i in range(2):
                        write((pair * 2 + i) * vh + v, s, side, raw[:, i * HD : (i + 1) * HD])

    def tail(total):
        coarse = total.astype(BF16).astype(F32)
        return jnp.concatenate([coarse, total - coarse], axis=0).astype(BF16)

    def untail(block):
        block = block.astype(F32)
        return block[:8] + block[8:]

    def write_pair(d, s, side, value):
        pair_out[d, s * SUBROWS : (s + 1) * SUBROWS, side * HD : (side + 1) * HD] = value.astype(BF16)

    def write_own(d, s, side, value):
        own[d, s * SUBROWS : (s + 1) * SUBROWS, side * HD : (side + 1) * HD] = value

    own_sq[...] = jnp.zeros_like(own_sq)
    loads[0].wait()
    loads[1].wait()
    for v in range(vh):
        text_rows(v, 1 - core, write_pair)
        for h in range(KVH):
            pair_out[h * vh + v, each:, :] = tail(own_sq[v])
    swap = remote(pair_out, pair_in, pair_sem.at[0], pair_sem.at[1], chip, 1 - core)
    swap.start()
    for v in range(vh):
        text_rows(v, core, write_own)

    for part, load in enumerate(loads[2:]):
        wpad[part * 128 + VHD : (part + 1) * 128, :] = jnp.zeros((128 - VHD, wpad.shape[1]), BF16)
        load.wait()

    def project(origin):
        def norm_rows(i, carry):
            which = i // (count // LNROWS)
            begin = pl.multiple_of((i % (count // LNROWS)) * LNROWS, LNROWS)
            floats = held[origin * 2 + which, pl.ds(begin, LNROWS), :].astype(F32)
            place = pl.multiple_of(i * LNROWS, LNROWS)
            normed[pl.ds(place, LNROWS), :] = layer_norm(floats, gain_ref[...]).astype(BF16)
            return carry

        lax.fori_loop(0, 2 * count // LNROWS, norm_rows, 0)
        first = pl.multiple_of(origin * 2 * count, 2 * count)
        qkv_ref[pl.ds(first, 2 * count), :] = lax.dot_general(
            normed[...], wpad[...], (((1,), (1,)), ((), ())), preferred_element_type=F32
        ).astype(BF16)

    def project_hop(hop):
        for direction in range(2 if hop else 1):
            @pl.when(exists(direction, hop))
            def _():
                origin = origin_of(direction, hop)
                for piece in range(PIECES):
                    taken(origin, piece).wait_recv()
                project(origin)

    def link(direction, d):
        return remote(
            chain_out.at[direction, d], chain_in.at[direction, d],
            chain_send.at[direction, d], chain_recv.at[direction, d], neighbour(direction), core,
        )

    def sum_up(d, source, put, put_square):
        def body(i, carry):
            rows = pl.ds(pl.multiple_of(i * 128, 128), 128)
            value = own[d, rows, :] + pair_in[d, rows, :].astype(F32)
            if source is not None:
                value += source[rows, :].astype(F32)
            put(rows, value)
            return carry

        lax.fori_loop(0, each // 128, body, 0)
        square = own_sq[d % vh] + untail(pair_in[d, each:, :])
        if source is not None:
            square += untail(source[each:, :])
        put_square(square)

    def chain(step):
        for direction in range(2):
            rank = chip if direction == 0 else chips - 1 - chip
            ahead = chips - step
            d = chip + ahead if direction == 0 else chip - ahead
            last = step == chips - 1

            def block():
                return chain_last.at[direction] if last else chain_out.at[direction, d]

            def put(rows, value):
                block()[rows, :] = value.astype(BF16)

            def put_square(square):
                block()[each:, :] = tail(square)

            @pl.when(rank < step)
            def _():
                @pl.when(rank == 0)
                def _():
                    sum_up(d, None, put, put_square)

                if step > 1:
                    @pl.when(rank > 0)
                    def _():
                        link(direction, d).wait_recv()
                        sum_up(d, chain_in.at[direction, d], put, put_square)

                if not last:
                    link(direction, d).start()

    relay(1)
    swap.wait_recv()
    if chips > 2:
        chain(1)
    mine.wait()
    project_hop(0)
    for hop in range(2, chips):
        relay(hop)
        if hop < chips - 1:
            chain(hop)
        project_hop(hop - 1)

    def put_mine(rows, value):
        mine_ref[rows, :] = value

    def put_mine_square(square):
        mine_sq[...] = square

    sum_up(chip, None, put_mine, put_mine_square)
    chain(chips - 1)
    project_hop(chips - 1)

    swap.wait_send()
    for piece in range(PIECES):
        give(chip, piece, 0).wait_send()
        for direction in range(2):
            for hop in range(chips):
                if hop < chips - 1:
                    @pl.when(jnp.logical_and(exists(direction, hop), has(direction)))
                    def _():
                        pass_on(direction, hop, piece).wait_send()
                if hop > 0:
                    @pl.when(exists(direction, hop))
                    def _():
                        give(origin_of(direction, hop), piece, hop).wait_send()
    for direction in range(2):
        for d in range(chips):
            @pl.when(chip < d - 1 if direction == 0 else chip > d + 1)
            def _():
                link(direction, d).wait_send()


def in_hbm(array):
    return pltpu.with_memory_space_constraint(array, pltpu.MemorySpace.HBM)


def front(patches, vis_gain, w_qkv, text, kv_gain, w_kv, collective_id):
    sizes = tuple(lax.axis_size(name) for name in VIS)
    chips = sizes[0] * sizes[1]
    parts = sizes[1] * 2
    count, width = patches.shape
    rows, features = text.shape
    each = rows // parts
    heads3 = w_qkv.shape[1] // VHD
    block = (each + 16, 2 * HD)
    DMA = pltpu.SemaphoreType.DMA
    return pl.pallas_call(
        functools.partial(front_kernel, sizes),
        out_shape=[
            jax.ShapeDtypeStruct((2 * chips * count, heads3 * 128), BF16),
            jax.ShapeDtypeStruct((2 * chips, count, width), BF16),
            jax.ShapeDtypeStruct((2,) + block, BF16),
            jax.ShapeDtypeStruct((each, 2 * HD), F32),
            jax.ShapeDtypeStruct((8, SUBROWS), F32),
        ],
        in_specs=[VMEM] * 3 + [HBM] * 3,
        out_specs=[VMEM] * 5,
        scratch_shapes=[
            pltpu.VMEM((heads3 * 128, width), BF16),
            pltpu.VMEM(text.shape, BF16),
            pltpu.VMEM(w_kv.shape, BF16),
            pltpu.VMEM((2 * count, width), BF16),
            pltpu.VMEM((chips,) + (each, 2 * HD), F32),
            pltpu.VMEM((sizes[1], 8, SUBROWS), F32),
            pltpu.VMEM((chips,) + block, BF16),
            pltpu.VMEM((chips,) + block, BF16),
            pltpu.VMEM((2, chips) + block, BF16),
            pltpu.VMEM((2, chips) + block, BF16),
            DMA((3 + heads3,)),
            DMA((2, chips, PIECES)),
            DMA((2, chips, PIECES)),
            DMA((chips, PIECES)),
            DMA((chips, PIECES)),
            DMA((2,)),
            DMA((2, chips)),
            DMA((2, chips)),
        ],
        compiler_params=pltpu.CompilerParams(
            collective_id=collective_id, has_side_effects=True, vmem_limit_bytes=40 * 2**20
        ),
    )(patches, vis_gain.reshape(1, -1), kv_gain.reshape(1, -1), *map(in_hbm, (w_qkv.T, text, w_kv)))


def spread_of(rows, width, places):
    best = (1, 1)
    for down in range(1, rows // 16 + 1):
        for across in range(1, width // 128 + 1):
            if rows % (16 * down) or width % (128 * across) or down * across > places:
                continue
            if down * across > best[0] * best[1]:
                best = (down, across)
    return best


def middle_kernel(sizes, ctxs, *refs):
    (
        qkv_ref, wout_ref, gain_ref, chain_ref, mine_ref, sq_ref, patches_hbm, wmerge_hbm,
        visual_ref, share_ref,
        patches, held, wall, wmerge, mixed, merged, token_sum, values, staged, chain_in,
        load_sem, send_sem, recv_sem, near_send, near_recv, merge_send, merge_recv,
        chain_send, chain_recv,
        line_send, line_recv, plane_send, plane_recv, pair_send, pair_recv,
    ) = refs
    chips, vh = sizes[0] * sizes[1], sizes[1]
    core, ctx = lax.axis_index("core"), lax.axis_index("ctx")
    vk_index, vh_index = lax.axis_index("vk"), lax.axis_index("vh")
    chip = vk_index * vh + vh_index
    me = chip * 2 + core
    each = mine_ref.shape[0]
    subs = each // SUBROWS
    deep, width = wout_ref.shape
    total = qkv_ref.shape[0]
    half = total // 2
    blocks = half // LANES
    heads = deep // VHD
    planes = ctxs * vh
    plane = ctx * vh + vh_index

    def at(where, which):
        return {"vk": where // vh, "vh": where % vh, "core": which}

    def beside(where):
        return {"ctx": where // vh, "vh": where % vh}

    def neighbour(direction):
        return chip + 1 if direction == 0 else chip - 1

    def has(direction):
        return chip < chips - 1 if direction == 0 else chip > 0

    def remote(src, dst, send, recv, device):
        return pltpu.make_async_remote_copy(
            src_ref=src, dst_ref=dst, send_sem=send, recv_sem=recv,
            device_id=device, device_id_type=MESH,
        )

    twin = at(chip, 1 - core)
    my_half = pl.ds(pl.multiple_of(core * half, LANES), half)
    fetch = pltpu.make_async_copy(patches_hbm.at[my_half], patches, load_sem.at[2])
    fetch.start()
    load = pltpu.make_async_copy(wmerge_hbm, wmerge, load_sem.at[0])
    load.start()
    my_rows = pl.ds(pl.multiple_of(me * deep, 16), deep)
    keep = pltpu.make_async_copy(wout_ref, wall.at[my_rows], load_sem.at[1])
    keep.start()

    barrier = pltpu.get_barrier_semaphore()
    pl.semaphore_signal(barrier, inc=1, device_id=twin, device_id_type=MESH)
    for k in range(1, chips):
        pl.semaphore_signal(
            barrier, inc=1, device_id=at((chip + k) % chips, core), device_id_type=MESH
        )
    for j in range(1, planes):
        pl.semaphore_signal(
            barrier, inc=1, device_id=beside((plane + j) % planes), device_id_type=MESH
        )
    pl.semaphore_wait(barrier, chips + planes - 1)

    def last_link(direction):
        return remote(
            chain_ref.at[direction], chain_in.at[direction],
            chain_send.at[direction], chain_recv.at[direction], at(neighbour(direction), core),
        )

    down, across = spread_of(deep, width, ctxs)
    used, high, wide = down * across, deep // down, width // across

    def part(origin, which, index):
        first = pl.multiple_of((origin * 2 + which) * deep + (index // across) * high, 16)
        lane = pl.multiple_of((index % across) * wide, 128)
        return wall.at[pl.ds(first, high), pl.ds(lane, wide)]

    def line_part(k):
        first = pl.multiple_of((ctx // across) * high, 16)
        lane = pl.multiple_of((ctx % across) * wide, 128)
        return remote(
            wout_ref.at[pl.ds(first, high), pl.ds(lane, wide)], part(chip, core, ctx),
            line_send.at[k], line_recv.at[k], at((chip + k) % chips, core),
        )

    def from_line(k, j):
        block = part((chip - k) % chips, core, ctx)
        return remote(
            block, block, plane_send.at[k, j], plane_recv.at[k, j], {"ctx": (ctx + j) % ctxs}
        )

    def to_twin(k, j, which):
        block = part((chip - k) % chips, which, (ctx - j) % ctxs)
        return remote(block, block, pair_send.at[k, j], pair_recv.at[k, j], twin)

    def own_to_twin():
        return remote(wout_ref, wall.at[my_rows], pair_send.at[0, 0], pair_recv.at[0, 0], twin)

    for k in range(1, chips):
        @pl.when(ctx < used)
        def _():
            line_part(k).start()
    own_to_twin().start()

    def lanes_of(piece):
        return pl.ds(pl.multiple_of(piece * LANES, LANES), LANES)

    def slot(origin, piece):
        first = pl.multiple_of(origin * 2 * deep, 16)
        return held.at[pl.ds(first, 2 * deep), lanes_of(piece)]

    def origin_of(direction, hop):
        return chip - hop if direction == 0 else chip + hop

    def exists(direction, hop):
        return chip >= hop if direction == 0 else chip + hop < chips

    def pass_on(direction, hop, piece):
        block = slot(origin_of(direction, hop), piece)
        return remote(
            block, block, send_sem.at[direction, hop, piece], recv_sem.at[direction, hop, piece],
            at(neighbour(direction), core),
        )

    def arrival(direction, hop, piece):
        block = slot(origin_of(direction, hop), piece)
        return remote(
            block, block, send_sem.at[direction, hop - 1, piece],
            recv_sem.at[direction, hop - 1, piece], twin,
        )

    def give(piece):
        return remote(
            staged.at[:, lanes_of(piece)], held.at[my_rows, lanes_of(piece)],
            near_send.at[piece], near_recv.at[piece], twin,
        )

    def taken(piece):
        first = pl.multiple_of((chip * 2 + 1 - core) * deep, 16)
        block = held.at[pl.ds(first, deep), lanes_of(piece)]
        return remote(block, block, near_send.at[piece], near_recv.at[piece], twin)

    scale = 1.0 / math.sqrt(VHD)
    for h in range(heads):
        first = (h * 3 + 2) * 128
        values[h] = jnp.transpose(qkv_ref[:, first : first + 128].astype(F32)).astype(BF16)

    def attend(piece, side, put):
        places = pl.ds(pl.multiple_of(side * half + piece * LANES, LANES), LANES)
        for h in range(heads):
            first = h * 3 * 128
            query = qkv_ref[places, first : first + 128]
            keys = qkv_ref[:, first + 128 : first + 256]
            scores = lax.dot_general(
                keys, query, (((1,), (1,)), ((), ())), preferred_element_type=F32
            ) * scale
            expo = jnp.exp(scores - jnp.max(scores, axis=0, keepdims=True))
            summed = jnp.sum(expo, axis=0, keepdims=True)
            mix = jnp.dot(values[h], expo.astype(BF16), preferred_element_type=F32)
            put(h, (mix[:VHD] / summed).astype(BF16))

    def attend_far(piece, carry):
        def put(h, value):
            staged[h * VHD : (h + 1) * VHD, lanes_of(piece)] = value

        attend(piece, 1 - core, put)
        give(piece).start()
        return carry

    def attend_near(piece, carry):
        def put(h, value):
            rows = pl.ds(pl.multiple_of(me * deep + h * VHD, 16), VHD)
            held[rows, lanes_of(piece)] = value

        attend(piece, core, put)
        taken(piece).wait_recv()
        for direction in range(2):
            @pl.when(has(direction))
            def _():
                pass_on(direction, 0, piece).start()
        return carry

    lax.fori_loop(0, blocks, attend_far, 0)
    lax.fori_loop(0, blocks, attend_near, 0)

    def relay(hop):
        def body(piece, carry):
            for direction in range(2):
                @pl.when(exists(direction, hop))
                def _():
                    arrival(direction, hop, piece).wait_recv()
                    if hop < chips - 1:
                        @pl.when(has(direction))
                        def _():
                            pass_on(direction, hop, piece).start()
            return carry

        lax.fori_loop(0, blocks, body, 0)

    def untail(block):
        block = block.astype(F32)
        return block[:8] + block[8:]

    def gain_from(direction):
        last_link(direction).wait_recv()

        def body(i, carry):
            rows = pl.ds(pl.multiple_of(i * 128, 128), 128)
            mine_sum[rows, :] += chain_in[direction, rows, :].astype(F32)
            return carry

        lax.fori_loop(0, each // 128, body, 0)
        squares[...] += untail(chain_in[direction, each:, :])

    def finish_text(sum_ref, square_ref):
        nonlocal mine_sum, squares
        mine_sum, squares = sum_ref, square_ref
        mine_sum[...] = mine_ref[...]
        squares[...] = sq_ref[...]
        for direction in range(2):
            @pl.when(has(1 - direction))
            def _():
                gain_from(direction)
        inverse = lax.rsqrt(squares[...] / D + EPS)
        for s in range(subs):
            factor = jnp.transpose(jnp.broadcast_to(inverse[s : s + 1], (128, SUBROWS)))
            for side in range(2):
                lanes = slice(side * HD, (side + 1) * HD)
                rows = slice(s * SUBROWS, (s + 1) * SUBROWS)
                share_ref[rows, lanes] = (mine_sum[rows, lanes] * factor).astype(BF16)

    for k in range(1, chips):
        @pl.when(ctx < used)
        def _():
            line_part(k).wait_recv()
            for j in range(1, ctxs):
                from_line(k, j).start()
            to_twin(k, 0, core).start()
    relay(1)
    mine_sum = squares = None

    def add_chip(origin, fresh):
        rows = pl.ds(pl.multiple_of(origin * 2 * deep, 16), 2 * deep)

        def body(i, carry):
            places = pl.ds(pl.multiple_of(i * LANES, LANES), LANES)
            product = lax.dot_general(
                held[rows, places], wall[rows, :], (((0,), (0,)), ((), ())),
                preferred_element_type=F32,
            )
            if fresh:
                product += patches[places, :].astype(F32)
            for c in range(width // 128):
                lanes = product[:, c * 128 : (c + 1) * 128]
                mixed[c, places, :] = lanes if fresh else mixed[c, places, :] + lanes
            return carry

        lax.fori_loop(0, blocks, body, 0)

    def add_hop(hop):
        for direction in range(2 if hop else 1):
            @pl.when(exists(direction, hop))
            def _():
                add_chip(origin_of(direction, hop), hop == 0)

    keep.wait()
    fetch.wait()
    own_to_twin().wait_recv()
    add_hop(0)
    def last_sends():
        for direction in range(2):
            @pl.when(has(direction))
            def _():
                last_link(direction).start()

    if chips > 2:
        relay(2)
    if chips < 5:
        last_sends()
    for k in range(1, chips):
        for j in range(1, ctxs):
            @pl.when((ctx - j) % ctxs < used)
            def _():
                block = part((chip - k) % chips, core, (ctx - j) % ctxs)
                remote(
                    block, block, plane_send.at[k, j], plane_recv.at[k, j], twin
                ).wait_recv()
                to_twin(k, j, core).start()
    for k in range(1, chips):
        for j in range(ctxs):
            @pl.when((ctx - j) % ctxs < used)
            def _():
                to_twin(k, j, 1 - core).wait_recv()
    add_hop(1)
    for hop in range(3, chips):
        add_hop(hop - 1)
        relay(hop)
        if hop == chips - 2:
            last_sends()
    if chips > 2:
        add_hop(chips - 1)

    tokens = half // 4
    my_tokens = pl.ds(pl.multiple_of(core * tokens, LNROWS), tokens)

    def merge_link(r, which):
        block = merged.at[r, pl.ds(pl.multiple_of(which * tokens, LNROWS), tokens)]
        return remote(block, block, merge_send.at[r], merge_recv.at[r], twin)

    for r in range(4):
        def norm_rows(i, carry):
            every = pl.ds(i * 4 * LNROWS + r, LNROWS, stride=4)
            rows = jnp.concatenate([mixed[c, every, :] for c in range(width // 128)], axis=1)
            place = pl.ds(pl.multiple_of(core * tokens + i * LNROWS, LNROWS), LNROWS)
            merged[r, place, :] = layer_norm(rows, gain_ref[...]).astype(BF16)
            return carry

        lax.fori_loop(0, tokens // LNROWS, norm_rows, 0)
        merge_link(r, core).start()
    load.wait()
    for r in range(4):
        merge_link(r, 1 - core).wait_recv()

        def column(c, carry):
            lanes = pl.ds(pl.multiple_of(c * LANES, LANES), LANES)
            value = jnp.dot(
                merged[r], wmerge[r * width : (r + 1) * width, lanes], preferred_element_type=F32
            )
            if r:
                value += token_sum[:, lanes]
            if r < 3:
                token_sum[:, lanes] = value
            else:
                visual_ref[:, lanes] = value.astype(BF16)
            return carry

        lax.fori_loop(0, visual_ref.shape[1] // LANES, column, 0)

    pl.run_scoped(
        finish_text, pltpu.VMEM((each, 2 * HD), F32), pltpu.VMEM((8, SUBROWS), F32)
    )
    own_to_twin().wait_send()
    for k in range(1, chips):
        @pl.when(ctx < used)
        def _():
            line_part(k).wait_send()
            for j in range(1, ctxs):
                from_line(k, j).wait_send()
        for j in range(ctxs):
            @pl.when((ctx - j) % ctxs < used)
            def _():
                to_twin(k, j, core).wait_send()
    for direction in range(2):
        @pl.when(has(direction))
        def _():
            last_link(direction).wait_send()

    for r in range(4):
        merge_link(r, core).wait_send()

    def drain(piece, carry):
        give(piece).wait_send()
        for direction in range(2):
            for hop in range(chips - 1):
                @pl.when(jnp.logical_and(exists(direction, hop), has(direction)))
                def _():
                    pass_on(direction, hop, piece).wait_send()
        return carry

    lax.fori_loop(0, blocks, drain, 0)


def middle(qkv, gathered, w_out, merge_gain, w_merge, chain_last, mine, mine_sq, collective_id):
    sizes = tuple(lax.axis_size(name) for name in VIS)
    ctxs = lax.axis_size("ctx")
    chips, planes = sizes[0] * sizes[1], ctxs * sizes[1]
    total, width = qkv.shape[0], w_out.shape[1]
    each = mine.shape[0]
    half = total // 2
    blocks = half // LANES
    heads = w_out.shape[0] // VHD
    tokens = total // 4
    DMA = pltpu.SemaphoreType.DMA
    return pl.pallas_call(
        functools.partial(middle_kernel, sizes, ctxs),
        out_shape=[
            jax.ShapeDtypeStruct((tokens, w_merge.shape[1]), BF16),
            jax.ShapeDtypeStruct((each, 2 * HD), BF16),
        ],
        in_specs=[VMEM] * 6 + [ANY] * 2,
        out_specs=[VMEM] * 2,
        scratch_shapes=[
            pltpu.VMEM((half, width), BF16),
            pltpu.VMEM((VD, half), BF16),
            pltpu.VMEM((VD, width), BF16),
            pltpu.VMEM(w_merge.shape, BF16),
            pltpu.VMEM((width // 128, half, 128), F32),
            pltpu.VMEM((4, tokens, width), BF16),
            pltpu.VMEM((tokens, w_merge.shape[1]), F32),
            pltpu.VMEM((heads, 128, total), BF16),
            pltpu.VMEM((w_out.shape[0], half), BF16),
            pltpu.VMEM(chain_last.shape, BF16),
            DMA((3,)),
            DMA((2, chips, blocks)),
            DMA((2, chips, blocks)),
            DMA((blocks,)),
            DMA((blocks,)),
            DMA((4,)),
            DMA((4,)),
            DMA((2,)),
            DMA((2,)),
            DMA((chips,)),
            DMA((chips,)),
            DMA((chips, ctxs)),
            DMA((chips, ctxs)),
            DMA((chips, ctxs)),
            DMA((chips, ctxs)),
        ],
        compiler_params=pltpu.CompilerParams(
            collective_id=collective_id, has_side_effects=True, vmem_limit_bytes=40 * 2**20
        ),
    )(
        qkv, w_out, merge_gain.reshape(1, -1), chain_last, mine, mine_sq,
        gathered.reshape(total, width), w_merge,
    )


def tail_kernel(sizes, ctxs, mine, shard_rows, *refs):
    (
        visual_ref, tgain_ref, dest_ref, row_ref, len_ref, share_ref, wkv_hbm, query_hbm, own_hbm,
        out_ref,
        wkv, query_in, query, own_kv, bias, text, image, own, own_sq, pair_out, pair_in, line_out, line_in,
        high, summed, mix,
        load_sem, swap_sem, line_send, line_recv, plane_send, plane_recv, twin_send, twin_recv,
        text_send, text_recv, pass_send, pass_recv, send_sem, recv_sem, near_send, near_recv,
    ) = refs
    chips, vh = sizes[0] * sizes[1], sizes[1]
    core, ctx = lax.axis_index("core"), lax.axis_index("ctx")
    vh_index = lax.axis_index("vh")
    chip = lax.axis_index("vk") * vh + vh_index
    me = chip * 2 + core
    parts = 2 * vh
    each = visual_ref.shape[0] // parts
    planes = ctxs * vh
    plane = ctx * vh + vh_index
    resp = query_in.shape[0]
    group = QH // KVH

    def at(where, which):
        return {"vk": where // vh, "vh": where % vh, "core": which}

    def beside(where):
        return {"ctx": where // vh, "vh": where % vh}

    def neighbour(direction):
        return chip + 1 if direction == 0 else chip - 1

    def has(direction):
        return chip < chips - 1 if direction == 0 else chip > 0

    def remote(src, dst, send, recv, device):
        return pltpu.make_async_remote_copy(
            src_ref=src, dst_ref=dst, send_sem=send, recv_sem=recv,
            device_id=device, device_id_type=MESH,
        )

    twin = at(chip, 1 - core)
    lane = pl.multiple_of(me * mine * HD, HD)
    head = pl.multiple_of(((me * mine) // group) * HD, HD)
    loads = [
        pltpu.make_async_copy(wkv_hbm, wkv, load_sem.at[0]),
        pltpu.make_async_copy(query_hbm.at[:, pl.ds(lane, mine * HD)], query_in, load_sem.at[1]),
        pltpu.make_async_copy(own_hbm.at[:, pl.ds(head, HD)], own_kv.at[0], load_sem.at[2]),
        pltpu.make_async_copy(
            own_hbm.at[:, pl.ds(pl.multiple_of(KVH * HD + head, HD), HD)], own_kv.at[1], load_sem.at[3]
        ),
    ]
    for load in loads:
        load.start()

    barrier = pltpu.get_barrier_semaphore()
    pl.semaphore_signal(barrier, inc=1, device_id=twin, device_id_type=MESH)
    for k in range(1, chips):
        pl.semaphore_signal(
            barrier, inc=1, device_id=at((chip + k) % chips, core), device_id_type=MESH
        )
    for j in range(1, planes):
        pl.semaphore_signal(
            barrier, inc=1, device_id=beside((plane + j) % planes), device_id_type=MESH
        )
    pl.semaphore_wait(barrier, chips + planes - 1)

    rows_text = share_ref.shape[0]

    def text_slot(place, which):
        return text.at[pl.ds(pl.multiple_of((place * 2 + which) * rows_text, 16), rows_text)]

    def text_link(j):
        return remote(
            share_ref, text_slot(plane, core), text_send.at[j], text_recv.at[j],
            beside((plane + j) % planes),
        )

    def text_from(j):
        block = text_slot((plane - j) % planes, core)
        return remote(block, block, text_send.at[j], text_recv.at[j], twin)

    def text_twin(j, which):
        block = text_slot((plane - j) % planes, which)
        return remote(block, block, pass_send.at[j], pass_recv.at[j], twin)

    def text_own():
        return remote(share_ref, text_slot(plane, core), pass_send.at[0], pass_recv.at[0], twin)

    for j in range(1, planes):
        text_link(j).start()
    text_own().start()

    def token_rows(v, which, write):
        first = pl.multiple_of((v * 2 + which) * each, each)
        rows = visual_ref[pl.ds(first, each), :].astype(F32)
        total = jnp.sum(rows * rows, axis=1, keepdims=True)
        own_sq[v, 0:1, :each] = jnp.transpose(jnp.broadcast_to(total, (each, 128)))[0:1]
        scaled = (rows * tgain_ref[...]).astype(BF16)
        for side in range(2):
            for pair in range(KVH // 2):
                begin = (side * KVH + pair * 2) * HD
                raw = jnp.dot(scaled, wkv[:, begin : begin + 2 * HD], preferred_element_type=F32)
                for i in range(2):
                    write((pair * 2 + i) * vh + v, side, raw[:, i * HD : (i + 1) * HD])

    def split(total):
        coarse = total.astype(BF16).astype(F32)
        return jnp.concatenate([coarse, total - coarse], axis=0).astype(BF16)

    def joined(block):
        block = block.astype(F32)
        return block[:8] + block[8:]

    def write_pair(d, side, value):
        pair_out[d, :each, side * HD : (side + 1) * HD] = value.astype(BF16)

    def write_own(d, side, value):
        own[d, :, side * HD : (side + 1) * HD] = value

    own_sq[...] = jnp.zeros_like(own_sq)
    loads[0].wait()
    for v in range(vh):
        token_rows(v, 1 - core, write_pair)
        for h in range(KVH):
            pair_out[h * vh + v, each:, :] = split(own_sq[v])
    swap = remote(pair_out, pair_in, swap_sem.at[0], swap_sem.at[1], twin)
    swap.start()
    for v in range(vh):
        token_rows(v, core, write_own)
    for load in loads[1:]:
        load.wait()
    for j in range(mine):
        query[j * resp : (j + 1) * resp, :] = query_in[:, j * HD : (j + 1) * HD]

    def line_link(k):
        d = (chip + k) % chips
        return remote(
            line_out.at[d], line_in.at[k], line_send.at[k], line_recv.at[k], at(d, core)
        )

    swap.wait_recv()
    for k in range(1, chips):
        d = (chip + k) % chips
        line_out[d, :each, :] = (own[d] + pair_in[d, :each, :].astype(F32)).astype(BF16)
        line_out[d, each:, :] = split(own_sq[d % vh] + joined(pair_in[d, each:, :]))
        line_link(k).start()

    groups = bias.shape[0] // 128
    padded = -(-groups // 128) * 128
    count = jnp.zeros((128, padded), F32)
    for i in range(dest_ref.shape[0]):
        flat = dest_ref[i : i + 1, :] * shard_rows + row_ref[i : i + 1, :]
        low = lax.broadcasted_iota(jnp.int32, (128, flat.shape[1]), 0) == flat % 128
        upper = lax.broadcasted_iota(jnp.int32, (padded, flat.shape[1]), 0) == flat // 128
        count += lax.dot_general(
            jnp.where(low, 1.0, 0.0).astype(BF16), jnp.where(upper, 1.0, 0.0).astype(BF16),
            (((1,), (1,)), ((), ())), preferred_element_type=F32,
        )
    hidden = jnp.where(count > 0.5, -1e30, 0.0)
    for g in range(groups):
        bias[g * 128 : (g + 1) * 128, :] = jnp.broadcast_to(hidden[:, g : g + 1], (128, 128))

    high[...] = jnp.full_like(high, -1e30)
    summed[...] = jnp.zeros_like(summed)
    mix[...] = jnp.zeros_like(mix)
    scale = 1.0 / math.sqrt(HD)

    def attend(keys, values, mask):
        scores = lax.dot_general(
            keys, query[...], (((1,), (1,)), ((), ())), preferred_element_type=F32
        ) * scale
        scores = mask(scores)
        top = jnp.maximum(high[...], jnp.max(scores, axis=0, keepdims=True))
        fade = jnp.exp(high[...] - top)
        expo = jnp.exp(scores - top)
        high[...] = top
        summed[...] = summed[...] * fade + jnp.sum(expo, axis=0, keepdims=True)
        mix[...] = mix[...] * fade + jnp.dot(
            jnp.transpose(values.astype(F32)).astype(BF16), expo.astype(BF16),
            preferred_element_type=F32,
        )

    def causal(scores):
        key = lax.broadcasted_iota(jnp.int32, scores.shape, 0)
        place = lax.broadcasted_iota(jnp.int32, scores.shape, 1) % resp
        return jnp.where(key <= place, scores, -1e30)

    def text_rows(place, which):
        first = (place * 2 + which) * rows_text
        rows = pl.ds(pl.multiple_of(first, 128), rows_text)
        attend(text[rows, :HD], text[rows, HD:], lambda scores: scores + bias[rows, 0:1])

    attend(own_kv[0], own_kv[1], causal)
    first_row = pl.multiple_of((plane * 2 + core) * rows_text, 128)
    text[pl.ds(first_row, rows_text), :] = share_ref[...]
    text_rows(plane, core)
    text_twin(0, 1 - core).wait_recv()
    text_rows(plane, 1 - core)

    def slot(place, which):
        return image.at[pl.ds(pl.multiple_of((place * 2 + which) * each, 16), each)]

    def plane_link(j):
        block = slot(plane, core)
        return remote(
            block, block, plane_send.at[j], plane_recv.at[j], beside((plane + j) % planes)
        )

    def plane_from(j):
        block = slot((plane - j) % planes, core)
        return remote(block, block, plane_send.at[j], plane_recv.at[j], twin)

    def twin_link(j, which):
        block = slot((plane - j) % planes, which)
        return remote(block, block, twin_send.at[j], twin_recv.at[j], twin)

    for k in range(1, chips):
        line_link(k).wait_recv()
    total = own[chip] + pair_in[chip, :each, :].astype(F32)
    square = own_sq[chip % vh] + joined(pair_in[chip, each:, :])
    for k in range(1, chips):
        total += line_in[k, :each, :].astype(F32)
        square += joined(line_in[k, each:, :])
    inverse = lax.rsqrt(square / D + EPS)
    factor = jnp.transpose(jnp.broadcast_to(inverse[0:1, :each], (128, each)))
    place = pl.multiple_of((plane * 2 + core) * each, 16)
    for side in range(2):
        lanes = slice(side * HD, (side + 1) * HD)
        image[pl.ds(place, each), lanes] = (total[:, lanes] * factor).astype(BF16)
    for j in range(1, planes):
        plane_link(j).start()
    twin_link(0, core).start()
    for j in range(1, planes):
        text_from(j).wait_recv()
        text_twin(j, core).start()

    def text_near(j, carry):
        text_rows((plane - j) % planes, core)
        return carry

    def text_far(j, carry):
        text_twin(j, 1 - core).wait_recv()
        text_rows((plane - j) % planes, 1 - core)
        return carry

    lax.fori_loop(1, planes, text_near, 0)
    for j in range(1, planes):
        plane_from(j).wait_recv()
        twin_link(j, core).start()
    lax.fori_loop(1, planes, text_far, 0)
    for j in range(planes):
        twin_link(j, 1 - core).wait_recv()

    def image_chunk(i, carry):
        rows = pl.ds(pl.multiple_of(i * KEYS, KEYS), KEYS)
        attend(image[rows, :HD], image[rows, HD:], lambda scores: scores)
        return carry

    lax.fori_loop(0, image.shape[0] // KEYS, image_chunk, 0)

    piece_width = mine * HD // 2

    def result_slot(origin, which, piece):
        first = ((origin * 2 + which) * 2 + piece) * piece_width
        return out_ref.at[:, pl.ds(pl.multiple_of(first, 128), piece_width)]

    def origin_of(direction, hop):
        return chip - hop if direction == 0 else chip + hop

    def exists(direction, hop):
        return chip >= hop if direction == 0 else chip + hop < chips

    def pass_on(direction, hop, piece):
        block = result_slot(origin_of(direction, hop), core, piece)
        return remote(
            block, block, send_sem.at[direction, hop, piece], recv_sem.at[direction, hop, piece],
            at(neighbour(direction), core),
        )

    def arrival(direction, hop, piece):
        block = result_slot(origin_of(direction, hop), core, piece)
        return remote(
            block, block, send_sem.at[direction, hop - 1, piece],
            recv_sem.at[direction, hop - 1, piece], twin,
        )

    def give(origin, piece, which):
        block = result_slot(origin, which, piece)
        return remote(
            block, block, near_send.at[origin, piece], near_recv.at[origin, piece], twin
        )

    live = lax.broadcasted_iota(jnp.int32, (resp, HD), 0) < len_ref[0]
    for piece in range(2):
        for j in range(piece * mine // 2, (piece + 1) * mine // 2):
            lanes = slice(j * resp, (j + 1) * resp)
            value = jnp.transpose(mix[:, lanes] / summed[:, lanes])
            out_ref[:, pl.ds(pl.multiple_of(lane + j * HD, HD), HD)] = jnp.where(
                live, value, 0.0
            ).astype(BF16)
        for direction in range(2):
            @pl.when(has(direction))
            def _():
                pass_on(direction, 0, piece).start()
        give(chip, piece, core).start()
    for hop in range(1, chips):
        for piece in range(2):
            for direction in range(2):
                @pl.when(exists(direction, hop))
                def _():
                    arrival(direction, hop, piece).wait_recv()
                    if hop < chips - 1:
                        @pl.when(has(direction))
                        def _():
                            pass_on(direction, hop, piece).start()
                    give(origin_of(direction, hop), piece, core).start()

    swap.wait_send()
    for k in range(1, chips):
        line_link(k).wait_send()
    text_own().wait_send()
    for j in range(planes):
        twin_link(j, core).wait_send()
        if j:
            plane_link(j).wait_send()
            text_link(j).wait_send()
            text_twin(j, core).wait_send()
    for piece in range(2):
        for origin in range(chips):
            give(origin, piece, 1 - core).wait_recv()
        give(chip, piece, core).wait_send()
        for direction in range(2):
            for hop in range(chips):
                if hop < chips - 1:
                    @pl.when(jnp.logical_and(exists(direction, hop), has(direction)))
                    def _():
                        pass_on(direction, hop, piece).wait_send()
                if hop > 0:
                    @pl.when(exists(direction, hop))
                    def _():
                        give(origin_of(direction, hop), piece, core).wait_send()


def tail(visual, kv_gain, token_dest, token_row, resp_len, text_share, w_kv, queries, resp_kv, shard_rows, collective_id):
    sizes = tuple(lax.axis_size(name) for name in VIS)
    ctxs = lax.axis_size("ctx")
    chips, planes = sizes[0] * sizes[1], ctxs * sizes[1]
    each = visual.shape[0] // (2 * sizes[1])
    mine = QH // (2 * chips)
    resp = queries.shape[0]
    block = (chips, each + 16, 2 * HD)
    DMA = pltpu.SemaphoreType.DMA
    return pl.pallas_call(
        functools.partial(tail_kernel, sizes, ctxs, mine, shard_rows),
        out_shape=jax.ShapeDtypeStruct((resp, QH * HD), BF16),
        in_specs=[VMEM] * 4 + [pl.BlockSpec(memory_space=pltpu.SMEM), VMEM] + [ANY] * 3,
        out_specs=VMEM,
        scratch_shapes=[
            pltpu.VMEM(w_kv.shape, BF16),
            pltpu.VMEM((resp, mine * HD), BF16),
            pltpu.VMEM((mine * resp, HD), BF16),
            pltpu.VMEM((2, resp, HD), BF16),
            pltpu.VMEM((ctxs * shard_rows, 128), F32),
            pltpu.VMEM((planes * 2 * text_share.shape[0], 2 * HD), BF16),
            pltpu.VMEM((planes * 2 * each, 2 * HD), BF16),
            pltpu.VMEM((chips, each, 2 * HD), F32),
            pltpu.VMEM((sizes[1], 8, 2 * HD), F32),
            pltpu.VMEM(block, BF16),
            pltpu.VMEM(block, BF16),
            pltpu.VMEM(block, BF16),
            pltpu.VMEM(block, BF16),
            pltpu.VMEM((1, mine * resp), F32),
            pltpu.VMEM((1, mine * resp), F32),
            pltpu.VMEM((HD, mine * resp), F32),
            DMA((4,)),
            DMA((2,)),
            DMA((chips,)),
            DMA((chips,)),
            DMA((planes,)),
            DMA((planes,)),
            DMA((planes,)),
            DMA((planes,)),
            DMA((planes,)),
            DMA((planes,)),
            DMA((planes,)),
            DMA((planes,)),
            DMA((2, chips, 2)),
            DMA((2, chips, 2)),
            DMA((chips, 2)),
            DMA((chips, 2)),
        ],
        compiler_params=pltpu.CompilerParams(
            collective_id=collective_id, has_side_effects=True, vmem_limit_bytes=32 * 2**20
        ),
    )(
        visual, kv_gain.reshape(1, -1), token_dest, token_row, resp_len, text_share, w_kv, queries,
        resp_kv,
    )


def per_device(
    patches,
    vis_gain,
    w_qkv,
    w_out,
    merge_gain,
    w_merge,
    token_dest,
    token_row,
    prompt_text,
    kv_gain,
    w_kv,
    queries,
    resp_kv,
    resp_len,
):
    qkv, gathered, chain_last, text_mine, text_sq = front(
        patches, vis_gain, w_qkv, prompt_text, kv_gain, w_kv, 0
    )
    visual, text_share = middle(
        qkv, gathered, w_out, merge_gain, w_merge, chain_last, text_mine, text_sq, 1
    )
    return tail(
        visual, kv_gain, token_dest, token_row, resp_len, text_share, w_kv, queries, resp_kv,
        prompt_text.shape[0], 2
    )


def solution(mesh):
    ctx_count, vis_count = mesh.shape["ctx"], mesh.shape["vis"]
    parts = vis_count // KVH
    shape = (ctx_count, vis_count // parts, parts // 2, 2)
    fine = Mesh(mesh.devices.reshape(shape), ("ctx",) + VIS)
    return jax.shard_map(
        per_device,
        mesh=fine,
        in_specs=(
            P(("ctx",) + VIS, None),
            P(),
            P(None, VIS),
            P(VIS, None),
            P(),
            P(None, VIS),
            P(),
            P(),
            P("ctx", VIS),
            P(VIS),
            P(VIS, None),
            P("ctx", None),
            P("ctx", None),
            P("ctx"),
        ),
        out_specs=P("ctx", None),
        check_vma=False,
    )
```

```python
import functools
import math

import jax
import jax.numpy as jnp
from jax import lax
from jax.experimental import pallas as pl
from jax.experimental.pallas import tpu as pltpu
from jax.sharding import Mesh, PartitionSpec as P

VD = 1280
D = 8192
HD = 128
QH = 32
KVH = 4
VHD = 80
MD = 5120


EPS = 1e-06
VIS = ("vk", "vh", "core")
MESH = pl.DeviceIdType.MESH
VMEM = pl.BlockSpec(memory_space=pltpu.VMEM)
ANY = pl.BlockSpec(memory_space=pl.ANY)
F32 = jnp.float32
BF16 = jnp.bfloat16
PIECES = 2
SUBROWS = 256
LNROWS = 64
LANES = 256
KEYS = 1024


def layer_norm(values, gain):
    center = values - jnp.mean(values, axis=-1, keepdims=True)
    spread = jnp.mean(center * center, axis=-1, keepdims=True)
    return center * lax.rsqrt(spread + EPS) * gain


def front_kernel(sizes, *refs):
    (
        patches_ref, gain_ref, tgain_ref, wqkv_hbm, text_hbm, wkv_hbm, greet,
        qkv_ref, held, chain_last, mine_ref, mine_sq,
        wpad, text, wkv, normed, own, own_sq, pair_out, pair_in, chain_out, chain_in,
        load_sem, send_sem, recv_sem, near_send, near_recv, pair_sem, chain_send, chain_recv,
    ) = refs
    chips, vh = sizes[0] * sizes[1], sizes[1]
    core = lax.axis_index("core")
    chip = lax.axis_index("vk") * vh + lax.axis_index("vh")
    count = patches_ref.shape[0]
    half = count // PIECES
    each = mine_ref.shape[0]
    subs = each // SUBROWS

    def at(where, which):
        return {"vk": where // vh, "vh": where % vh, "core": which}

    def neighbour(direction):
        return chip + 1 if direction == 0 else chip - 1

    def has(direction):
        return chip < chips - 1 if direction == 0 else chip > 0

    def remote(src, dst, send, recv, where, which):
        return pltpu.make_async_remote_copy(
            src_ref=src, dst_ref=dst, send_sem=send, recv_sem=recv,
            device_id=at(where, which), device_id_type=MESH,
        )

    loads = [
        pltpu.make_async_copy(text_hbm, text, load_sem.at[0]),
        pltpu.make_async_copy(wkv_hbm, wkv, load_sem.at[1]),
    ] + [
        pltpu.make_async_copy(
            wqkv_hbm.at[pl.ds(part * VHD, VHD)], wpad.at[pl.ds(part * 128, VHD)],
            load_sem.at[2 + part],
        )
        for part in range(wqkv_hbm.shape[0] // VHD)
    ]
    for load in loads:
        load.start()

    greet()

    def slot(origin, which, piece):
        first = pl.multiple_of((origin * 2 + which) * count + piece * half, 16)
        return held.at[pl.ds(first, half)]

    def source(origin, piece, hop):
        return patches_ref.at[pl.ds(piece * half, half)] if hop == 0 else slot(origin, core, piece)

    def origin_of(direction, hop):
        return chip - hop if direction == 0 else chip + hop

    def exists(direction, hop):
        return chip >= hop if direction == 0 else chip + hop < chips

    def pass_on(direction, hop, piece):
        origin = origin_of(direction, hop)
        return remote(
            source(origin, piece, hop), slot(origin, core, piece),
            send_sem.at[direction, hop, piece], recv_sem.at[direction, hop, piece],
            neighbour(direction), core,
        )

    def arrival(direction, hop, piece):
        origin = origin_of(direction, hop)
        return remote(
            slot(origin, core, piece), slot(origin, core, piece),
            send_sem.at[direction, hop - 1, piece], recv_sem.at[direction, hop - 1, piece],
            chip, 1 - core,
        )

    def give(origin, piece, hop):
        return remote(
            source(origin, piece, hop), slot(origin, core, piece),
            near_send.at[origin, piece], near_recv.at[origin, piece], chip, 1 - core,
        )

    def taken(origin, piece):
        return remote(
            slot(origin, 1 - core, piece), slot(origin, 1 - core, piece),
            near_send.at[origin, piece], near_recv.at[origin, piece], chip, 1 - core,
        )

    for piece in range(PIECES):
        for direction in range(2):
            @pl.when(has(direction))
            def _():
                pass_on(direction, 0, piece).start()
    my_rows = pl.ds(pl.multiple_of((chip * 2 + core) * count, 16), count)
    mine = pltpu.make_async_copy(patches_ref, held.at[my_rows], load_sem.at[len(loads)])
    mine.start()
    for piece in range(PIECES):
        give(chip, piece, 0).start()

    def relay(hop):
        for piece in range(PIECES):
            for direction in range(2):
                @pl.when(exists(direction, hop))
                def _():
                    arrival(direction, hop, piece).wait_recv()
                    if hop < chips - 1:
                        @pl.when(has(direction))
                        def _():
                            pass_on(direction, hop, piece).start()
                    give(origin_of(direction, hop), piece, hop).start()

    def text_rows(v, which, write):
        for s in range(subs):
            first = pl.multiple_of((v * 2 + which) * each + s * SUBROWS, SUBROWS)
            rows = text[pl.ds(first, SUBROWS), :].astype(F32)
            total = jnp.sum(rows * rows, axis=1, keepdims=True)
            line = jnp.transpose(jnp.broadcast_to(total, (SUBROWS, 128)))
            own_sq[v, s : s + 1, :] = line[0:1]
            scaled = (rows * tgain_ref[...]).astype(BF16)
            for side in range(2):
                for pair in range(KVH // 2):
                    begin = (side * KVH + pair * 2) * HD
                    raw = jnp.dot(scaled, wkv[:, begin : begin + 2 * HD], preferred_element_type=F32)
                    for i in range(2):
                        write((pair * 2 + i) * vh + v, s, side, raw[:, i * HD : (i + 1) * HD])

    def tail(total):
        coarse = total.astype(BF16).astype(F32)
        return jnp.concatenate([coarse, total - coarse], axis=0).astype(BF16)

    def untail(block):
        block = block.astype(F32)
        return block[:8] + block[8:]

    def write_pair(d, s, side, value):
        pair_out[d, s * SUBROWS : (s + 1) * SUBROWS, side * HD : (side + 1) * HD] = value.astype(BF16)

    def write_own(d, s, side, value):
        own[d, s * SUBROWS : (s + 1) * SUBROWS, side * HD : (side + 1) * HD] = value

    own_sq[...] = jnp.zeros_like(own_sq)
    loads[0].wait()
    loads[1].wait()
    for v in range(vh):
        text_rows(v, 1 - core, write_pair)
        for h in range(KVH):
            pair_out[h * vh + v, each:, :] = tail(own_sq[v])
    swap = remote(pair_out, pair_in, pair_sem.at[0], pair_sem.at[1], chip, 1 - core)
    swap.start()
    for v in range(vh):
        text_rows(v, core, write_own)

    for part, load in enumerate(loads[2:]):
        wpad[part * 128 + VHD : (part + 1) * 128, :] = jnp.zeros((128 - VHD, wpad.shape[1]), BF16)
        load.wait()

    def project(origin):
        def norm_rows(i, carry):
            begin = pl.multiple_of(origin * 2 * count + i * LNROWS, LNROWS)
            floats = held[pl.ds(begin, LNROWS), :].astype(F32)
            place = pl.multiple_of(i * LNROWS, LNROWS)
            normed[pl.ds(place, LNROWS), :] = layer_norm(floats, gain_ref[...]).astype(BF16)
            return carry

        lax.fori_loop(0, 2 * count // LNROWS, norm_rows, 0)
        first = pl.multiple_of(origin * 2 * count, 2 * count)
        qkv_ref[pl.ds(first, 2 * count), :] = lax.dot_general(
            normed[...], wpad[...], (((1,), (1,)), ((), ())), preferred_element_type=F32
        ).astype(BF16)

    def project_hop(hop):
        for direction in range(2 if hop else 1):
            @pl.when(exists(direction, hop))
            def _():
                origin = origin_of(direction, hop)
                for piece in range(PIECES):
                    taken(origin, piece).wait_recv()
                project(origin)

    def link(direction, d):
        return remote(
            chain_out.at[direction, d], chain_in.at[direction, d],
            chain_send.at[direction, d], chain_recv.at[direction, d], neighbour(direction), core,
        )

    def sum_up(d, source, put, put_square):
        def body(i, carry):
            rows = pl.ds(pl.multiple_of(i * 128, 128), 128)
            value = own[d, rows, :] + pair_in[d, rows, :].astype(F32)
            if source is not None:
                value += source[rows, :].astype(F32)
            put(rows, value)
            return carry

        lax.fori_loop(0, each // 128, body, 0)
        square = own_sq[d % vh] + untail(pair_in[d, each:, :])
        if source is not None:
            square += untail(source[each:, :])
        put_square(square)

    def chain(step):
        for direction in range(2):
            rank = chip if direction == 0 else chips - 1 - chip
            ahead = chips - step
            d = chip + ahead if direction == 0 else chip - ahead
            last = step == chips - 1

            def block():
                return chain_last.at[direction] if last else chain_out.at[direction, d]

            def put(rows, value):
                block()[rows, :] = value.astype(BF16)

            def put_square(square):
                block()[each:, :] = tail(square)

            @pl.when(rank < step)
            def _():
                @pl.when(rank == 0)
                def _():
                    sum_up(d, None, put, put_square)

                if step > 1:
                    @pl.when(rank > 0)
                    def _():
                        link(direction, d).wait_recv()
                        sum_up(d, chain_in.at[direction, d], put, put_square)

                if not last:
                    link(direction, d).start()

    relay(1)
    swap.wait_recv()
    if chips > 2:
        chain(1)
    mine.wait()
    project_hop(0)
    for hop in range(2, chips):
        relay(hop)
        if hop < chips - 1:
            chain(hop)
        project_hop(hop - 1)

    def put_mine(rows, value):
        mine_ref[rows, :] = value

    def put_mine_square(square):
        mine_sq[...] = square

    sum_up(chip, None, put_mine, put_mine_square)
    chain(chips - 1)
    project_hop(chips - 1)

    def drain():
        swap.wait_send()
        for piece in range(PIECES):
            give(chip, piece, 0).wait_send()
            for direction in range(2):
                for hop in range(chips):
                    if hop < chips - 1:
                        @pl.when(jnp.logical_and(exists(direction, hop), has(direction)))
                        def _():
                            pass_on(direction, hop, piece).wait_send()
                    if hop > 0:
                        @pl.when(exists(direction, hop))
                        def _():
                            give(origin_of(direction, hop), piece, hop).wait_send()
        for direction in range(2):
            for d in range(chips):
                @pl.when(chip < d - 1 if direction == 0 else chip > d + 1)
                def _():
                    link(direction, d).wait_send()

    return drain


def spread_of(rows, width, places):
    best = (1, 1)
    for down in range(1, rows // 16 + 1):
        for across in range(1, width // 128 + 1):
            if rows % (16 * down) or width % (128 * across) or down * across > places:
                continue
            if down * across > best[0] * best[1]:
                best = (down, across)
    return best


def middle_kernel(sizes, ctxs, *refs):
    (
        qkv_ref, wout_ref, gain_ref, chain_ref, mine_ref, sq_ref, patches, wmerge_hbm,
        visual_ref, share_ref,
        held, wall, wmerge, mixed, merged, token_sum, values, staged, chain_in,
        load_sem, send_sem, recv_sem, near_send, near_recv, merge_send, merge_recv,
        chain_send, chain_recv,
        line_send, line_recv, plane_send, plane_recv, pair_send, pair_recv,
    ) = refs
    chips, vh = sizes[0] * sizes[1], sizes[1]
    core, ctx = lax.axis_index("core"), lax.axis_index("ctx")
    vk_index, vh_index = lax.axis_index("vk"), lax.axis_index("vh")
    chip = vk_index * vh + vh_index
    me = chip * 2 + core
    each = mine_ref.shape[0]
    subs = each // SUBROWS
    deep, width = wout_ref.shape
    total = qkv_ref.shape[0]
    half = total // 2
    blocks = half // LANES
    heads = deep // VHD
    planes = ctxs * vh
    plane = ctx * vh + vh_index

    def at(where, which):
        return {"vk": where // vh, "vh": where % vh, "core": which}

    def beside(where):
        return {"ctx": where // vh, "vh": where % vh}

    def neighbour(direction):
        return chip + 1 if direction == 0 else chip - 1

    def has(direction):
        return chip < chips - 1 if direction == 0 else chip > 0

    def remote(src, dst, send, recv, device):
        return pltpu.make_async_remote_copy(
            src_ref=src, dst_ref=dst, send_sem=send, recv_sem=recv,
            device_id=device, device_id_type=MESH,
        )

    twin = at(chip, 1 - core)
    load = pltpu.make_async_copy(wmerge_hbm, wmerge, load_sem.at[0])
    load.start()
    my_rows = pl.ds(pl.multiple_of(me * deep, 16), deep)
    keep = pltpu.make_async_copy(wout_ref, wall.at[my_rows], load_sem.at[1])
    keep.start()

    def last_link(direction):
        return remote(
            chain_ref.at[direction], chain_in.at[direction],
            chain_send.at[direction], chain_recv.at[direction], at(neighbour(direction), core),
        )

    down, across = spread_of(deep, width, ctxs)
    used, high, wide = down * across, deep // down, width // across

    def part(origin, which, index):
        first = pl.multiple_of((origin * 2 + which) * deep + (index // across) * high, 16)
        lane = pl.multiple_of((index % across) * wide, 128)
        return wall.at[pl.ds(first, high), pl.ds(lane, wide)]

    def line_part(k):
        first = pl.multiple_of((ctx // across) * high, 16)
        lane = pl.multiple_of((ctx % across) * wide, 128)
        return remote(
            wout_ref.at[pl.ds(first, high), pl.ds(lane, wide)], part(chip, core, ctx),
            line_send.at[k], line_recv.at[k], at((chip + k) % chips, core),
        )

    def from_line(k, j):
        block = part((chip - k) % chips, core, ctx)
        return remote(
            block, block, plane_send.at[k, j], plane_recv.at[k, j], {"ctx": (ctx + j) % ctxs}
        )

    def to_twin(k, j, which):
        block = part((chip - k) % chips, which, (ctx - j) % ctxs)
        return remote(block, block, pair_send.at[k, j], pair_recv.at[k, j], twin)

    def own_to_twin():
        return remote(wout_ref, wall.at[my_rows], pair_send.at[0, 0], pair_recv.at[0, 0], twin)

    for k in range(1, chips):
        @pl.when(ctx < used)
        def _():
            line_part(k).start()
    own_to_twin().start()

    def lanes_of(piece):
        return pl.ds(pl.multiple_of(piece * LANES, LANES), LANES)

    def slot(origin, piece):
        first = pl.multiple_of(origin * 2 * deep, 16)
        return held.at[pl.ds(first, 2 * deep), lanes_of(piece)]

    def origin_of(direction, hop):
        return chip - hop if direction == 0 else chip + hop

    def exists(direction, hop):
        return chip >= hop if direction == 0 else chip + hop < chips

    def pass_on(direction, hop, piece):
        block = slot(origin_of(direction, hop), piece)
        return remote(
            block, block, send_sem.at[direction, hop, piece], recv_sem.at[direction, hop, piece],
            at(neighbour(direction), core),
        )

    def arrival(direction, hop, piece):
        block = slot(origin_of(direction, hop), piece)
        return remote(
            block, block, send_sem.at[direction, hop - 1, piece],
            recv_sem.at[direction, hop - 1, piece], twin,
        )

    def give(piece):
        return remote(
            staged.at[:, lanes_of(piece)], held.at[my_rows, lanes_of(piece)],
            near_send.at[piece], near_recv.at[piece], twin,
        )

    def taken(piece):
        first = pl.multiple_of((chip * 2 + 1 - core) * deep, 16)
        block = held.at[pl.ds(first, deep), lanes_of(piece)]
        return remote(block, block, near_send.at[piece], near_recv.at[piece], twin)

    scale = 1.0 / math.sqrt(VHD)
    for h in range(heads):
        first = (h * 3 + 2) * 128
        values[h] = jnp.transpose(qkv_ref[:, first : first + 128].astype(F32)).astype(BF16)

    def attend(piece, side, put):
        places = pl.ds(pl.multiple_of(side * half + piece * LANES, LANES), LANES)
        for h in range(heads):
            first = h * 3 * 128
            query = qkv_ref[places, first : first + 128]
            keys = qkv_ref[:, first + 128 : first + 256]
            scores = lax.dot_general(
                keys, query, (((1,), (1,)), ((), ())), preferred_element_type=F32
            ) * scale
            expo = jnp.exp(scores - jnp.max(scores, axis=0, keepdims=True))
            summed = jnp.sum(expo, axis=0, keepdims=True)
            mix = jnp.dot(values[h], expo.astype(BF16), preferred_element_type=F32)
            put(h, (mix[:VHD] / summed).astype(BF16))

    def attend_far(piece, carry):
        def put(h, value):
            staged[h * VHD : (h + 1) * VHD, lanes_of(piece)] = value

        attend(piece, 1 - core, put)
        give(piece).start()
        return carry

    def attend_near(piece, carry):
        def put(h, value):
            rows = pl.ds(pl.multiple_of(me * deep + h * VHD, 16), VHD)
            held[rows, lanes_of(piece)] = value

        attend(piece, core, put)
        taken(piece).wait_recv()
        for direction in range(2):
            @pl.when(has(direction))
            def _():
                pass_on(direction, 0, piece).start()
        return carry

    lax.fori_loop(0, blocks, attend_far, 0)
    lax.fori_loop(0, blocks, attend_near, 0)

    def relay(hop):
        def body(piece, carry):
            for direction in range(2):
                @pl.when(exists(direction, hop))
                def _():
                    arrival(direction, hop, piece).wait_recv()
                    if hop < chips - 1:
                        @pl.when(has(direction))
                        def _():
                            pass_on(direction, hop, piece).start()
            return carry

        lax.fori_loop(0, blocks, body, 0)

    def untail(block):
        block = block.astype(F32)
        return block[:8] + block[8:]

    def gain_from(direction):
        last_link(direction).wait_recv()

        def body(i, carry):
            rows = pl.ds(pl.multiple_of(i * 128, 128), 128)
            mine_ref[rows, :] += chain_in[direction, rows, :].astype(F32)
            return carry

        lax.fori_loop(0, each // 128, body, 0)
        sq_ref[...] += untail(chain_in[direction, each:, :])

    def finish_text():
        for direction in range(2):
            @pl.when(has(1 - direction))
            def _():
                gain_from(direction)
        inverse = lax.rsqrt(sq_ref[...] / D + EPS)
        for s in range(subs):
            factor = jnp.transpose(jnp.broadcast_to(inverse[s : s + 1], (128, SUBROWS)))
            for side in range(2):
                lanes = slice(side * HD, (side + 1) * HD)
                rows = slice(s * SUBROWS, (s + 1) * SUBROWS)
                share_ref[rows, lanes] = (mine_ref[rows, lanes] * factor).astype(BF16)

    for k in range(1, chips):
        @pl.when(ctx < used)
        def _():
            line_part(k).wait_recv()
            for j in range(1, ctxs):
                from_line(k, j).start()
            to_twin(k, 0, core).start()
    relay(1)
    def add_chip(origin, fresh):
        rows = pl.ds(pl.multiple_of(origin * 2 * deep, 16), 2 * deep)

        def body(i, carry):
            places = pl.ds(pl.multiple_of(i * LANES, LANES), LANES)
            product = lax.dot_general(
                held[rows, places], wall[rows, :], (((0,), (0,)), ((), ())),
                preferred_element_type=F32,
            )
            if fresh:
                mine_in = pl.ds(pl.multiple_of(core * half + i * LANES, LANES), LANES)
                product += patches[mine_in, :].astype(F32)
            for c in range(width // 128):
                lanes = product[:, c * 128 : (c + 1) * 128]
                mixed[c, places, :] = lanes if fresh else mixed[c, places, :] + lanes
            return carry

        lax.fori_loop(0, blocks, body, 0)

    def add_hop(hop):
        for direction in range(2 if hop else 1):
            @pl.when(exists(direction, hop))
            def _():
                add_chip(origin_of(direction, hop), hop == 0)

    keep.wait()
    own_to_twin().wait_recv()
    add_hop(0)
    def last_sends():
        for direction in range(2):
            @pl.when(has(direction))
            def _():
                last_link(direction).start()

    if chips > 2:
        relay(2)
    if chips < 5:
        last_sends()
    for k in range(1, chips):
        for j in range(1, ctxs):
            @pl.when((ctx - j) % ctxs < used)
            def _():
                block = part((chip - k) % chips, core, (ctx - j) % ctxs)
                remote(
                    block, block, plane_send.at[k, j], plane_recv.at[k, j], twin
                ).wait_recv()
                to_twin(k, j, core).start()
    for k in range(1, chips):
        for j in range(ctxs):
            @pl.when((ctx - j) % ctxs < used)
            def _():
                to_twin(k, j, 1 - core).wait_recv()
    add_hop(1)
    for hop in range(3, chips):
        add_hop(hop - 1)
        relay(hop)
        if hop == chips - 2:
            last_sends()
    if chips > 2:
        add_hop(chips - 1)

    tokens = half // 4
    my_tokens = pl.ds(pl.multiple_of(core * tokens, LNROWS), tokens)

    def merge_link(r, which):
        block = merged.at[r, pl.ds(pl.multiple_of(which * tokens, LNROWS), tokens)]
        return remote(block, block, merge_send.at[r], merge_recv.at[r], twin)

    for r in range(4):
        def norm_rows(i, carry):
            every = pl.ds(i * 4 * LNROWS + r, LNROWS, stride=4)
            rows = jnp.concatenate([mixed[c, every, :] for c in range(width // 128)], axis=1)
            place = pl.ds(pl.multiple_of(core * tokens + i * LNROWS, LNROWS), LNROWS)
            merged[r, place, :] = layer_norm(rows, gain_ref[...]).astype(BF16)
            return carry

        lax.fori_loop(0, tokens // LNROWS, norm_rows, 0)
        merge_link(r, core).start()
    load.wait()
    for r in range(4):
        merge_link(r, 1 - core).wait_recv()

        def column(c, carry):
            lanes = pl.ds(pl.multiple_of(c * LANES, LANES), LANES)
            value = jnp.dot(
                merged[r], wmerge[r * width : (r + 1) * width, lanes], preferred_element_type=F32
            )
            if r:
                value += token_sum[:, lanes]
            if r < 3:
                token_sum[:, lanes] = value
            else:
                visual_ref[:, lanes] = value.astype(BF16)
            return carry

        lax.fori_loop(0, visual_ref.shape[1] // LANES, column, 0)

    finish_text()
    def drain():
        own_to_twin().wait_send()
        for k in range(1, chips):
            @pl.when(ctx < used)
            def _():
                line_part(k).wait_send()
                for j in range(1, ctxs):
                    from_line(k, j).wait_send()
            for j in range(ctxs):
                @pl.when((ctx - j) % ctxs < used)
                def _():
                    to_twin(k, j, core).wait_send()
        for direction in range(2):
            @pl.when(has(direction))
            def _():
                last_link(direction).wait_send()

        for r in range(4):
            merge_link(r, core).wait_send()

        def drain_line(piece, carry):
            give(piece).wait_send()
            for direction in range(2):
                for hop in range(chips - 1):
                    @pl.when(jnp.logical_and(exists(direction, hop), has(direction)))
                    def _():
                        pass_on(direction, hop, piece).wait_send()
            return carry

        lax.fori_loop(0, blocks, drain_line, 0)

    return drain


def tail_kernel(sizes, ctxs, mine, shard_rows, *refs):
    (
        visual_ref, tgain_ref, dest_ref, row_ref, len_ref, share_ref, wkv, query_hbm, own_hbm,
        out_ref,
        query_in, query, own_kv, bias, text, image, own, own_sq, pair_out, pair_in, line_out, line_in,
        high, summed, mix,
        load_sem, swap_sem, line_send, line_recv, plane_send, plane_recv, twin_send, twin_recv,
        text_send, text_recv, pass_send, pass_recv, send_sem, recv_sem, near_send, near_recv,
    ) = refs
    chips, vh = sizes[0] * sizes[1], sizes[1]
    core, ctx = lax.axis_index("core"), lax.axis_index("ctx")
    vh_index = lax.axis_index("vh")
    chip = lax.axis_index("vk") * vh + vh_index
    me = chip * 2 + core
    parts = 2 * vh
    each = visual_ref.shape[0] // parts
    planes = ctxs * vh
    plane = ctx * vh + vh_index
    resp = query_in.shape[0]
    group = QH // KVH

    def at(where, which):
        return {"vk": where // vh, "vh": where % vh, "core": which}

    def beside(where):
        return {"ctx": where // vh, "vh": where % vh}

    def neighbour(direction):
        return chip + 1 if direction == 0 else chip - 1

    def has(direction):
        return chip < chips - 1 if direction == 0 else chip > 0

    def remote(src, dst, send, recv, device):
        return pltpu.make_async_remote_copy(
            src_ref=src, dst_ref=dst, send_sem=send, recv_sem=recv,
            device_id=device, device_id_type=MESH,
        )

    twin = at(chip, 1 - core)
    lane = pl.multiple_of(me * mine * HD, HD)
    head = pl.multiple_of(((me * mine) // group) * HD, HD)
    loads = [
        pltpu.make_async_copy(query_hbm.at[:, pl.ds(lane, mine * HD)], query_in, load_sem.at[1]),
        pltpu.make_async_copy(own_hbm.at[:, pl.ds(head, HD)], own_kv.at[0], load_sem.at[2]),
        pltpu.make_async_copy(
            own_hbm.at[:, pl.ds(pl.multiple_of(KVH * HD + head, HD), HD)], own_kv.at[1], load_sem.at[3]
        ),
    ]
    for load in loads:
        load.start()

    rows_text = share_ref.shape[0]

    def text_slot(place, which):
        return text.at[pl.ds(pl.multiple_of((place * 2 + which) * rows_text, 16), rows_text)]

    def text_link(j):
        return remote(
            share_ref, text_slot(plane, core), text_send.at[j], text_recv.at[j],
            beside((plane + j) % planes),
        )

    def text_from(j):
        block = text_slot((plane - j) % planes, core)
        return remote(block, block, text_send.at[j], text_recv.at[j], twin)

    def text_twin(j, which):
        block = text_slot((plane - j) % planes, which)
        return remote(block, block, pass_send.at[j], pass_recv.at[j], twin)

    def text_own():
        return remote(share_ref, text_slot(plane, core), pass_send.at[0], pass_recv.at[0], twin)

    for j in range(1, planes):
        text_link(j).start()
    text_own().start()

    def token_rows(v, which, write):
        first = pl.multiple_of((v * 2 + which) * each, each)
        rows = visual_ref[pl.ds(first, each), :].astype(F32)
        total = jnp.sum(rows * rows, axis=1, keepdims=True)
        own_sq[v, 0:1, :each] = jnp.transpose(jnp.broadcast_to(total, (each, 128)))[0:1]
        scaled = (rows * tgain_ref[...]).astype(BF16)
        for side in range(2):
            for pair in range(KVH // 2):
                begin = (side * KVH + pair * 2) * HD
                raw = jnp.dot(scaled, wkv[:, begin : begin + 2 * HD], preferred_element_type=F32)
                for i in range(2):
                    write((pair * 2 + i) * vh + v, side, raw[:, i * HD : (i + 1) * HD])

    def split(total):
        coarse = total.astype(BF16).astype(F32)
        return jnp.concatenate([coarse, total - coarse], axis=0).astype(BF16)

    def joined(block):
        block = block.astype(F32)
        return block[:8] + block[8:]

    def write_pair(d, side, value):
        pair_out[d, :each, side * HD : (side + 1) * HD] = value.astype(BF16)

    def write_own(d, side, value):
        own[d, :, side * HD : (side + 1) * HD] = value

    own_sq[...] = jnp.zeros_like(own_sq)
    for v in range(vh):
        token_rows(v, 1 - core, write_pair)
        for h in range(KVH):
            pair_out[h * vh + v, each:, :] = split(own_sq[v])
    swap = remote(pair_out, pair_in, swap_sem.at[0], swap_sem.at[1], twin)
    swap.start()
    for v in range(vh):
        token_rows(v, core, write_own)
    for load in loads:
        load.wait()
    for j in range(mine):
        query[j * resp : (j + 1) * resp, :] = query_in[:, j * HD : (j + 1) * HD]

    def line_link(k):
        d = (chip + k) % chips
        return remote(
            line_out.at[d], line_in.at[k], line_send.at[k], line_recv.at[k], at(d, core)
        )

    swap.wait_recv()
    for k in range(1, chips):
        d = (chip + k) % chips
        line_out[d, :each, :] = (own[d] + pair_in[d, :each, :].astype(F32)).astype(BF16)
        line_out[d, each:, :] = split(own_sq[d % vh] + joined(pair_in[d, each:, :]))
        line_link(k).start()

    padded = bias.shape[1]
    count = jnp.zeros((128, padded), F32)
    for i in range(dest_ref.shape[0]):
        flat = dest_ref[i : i + 1, :] * shard_rows + row_ref[i : i + 1, :]
        low = lax.broadcasted_iota(jnp.int32, (128, flat.shape[1]), 0) == flat % 128
        upper = lax.broadcasted_iota(jnp.int32, (padded, flat.shape[1]), 0) == flat // 128
        count += lax.dot_general(
            jnp.where(low, 1.0, 0.0).astype(BF16), jnp.where(upper, 1.0, 0.0).astype(BF16),
            (((1,), (1,)), ((), ())), preferred_element_type=F32,
        )
    bias[...] = count.astype(BF16)

    high[...] = jnp.full_like(high, -1e30)
    summed[...] = jnp.zeros_like(summed)
    mix[...] = jnp.zeros_like(mix)
    scale = 1.0 / math.sqrt(HD)

    def attend(keys, values, mask, lanes=slice(None)):
        scores = lax.dot_general(
            keys, query[lanes, :], (((1,), (1,)), ((), ())), preferred_element_type=F32
        ) * scale
        scores = mask(scores)
        top = jnp.maximum(high[:, lanes], jnp.max(scores, axis=0, keepdims=True))
        fade = jnp.exp(high[:, lanes] - top)
        expo = jnp.exp(scores - top)
        high[:, lanes] = top
        summed[:, lanes] = summed[:, lanes] * fade + jnp.sum(expo, axis=0, keepdims=True)
        mix[:, lanes] = mix[:, lanes] * fade + jnp.dot(
            jnp.transpose(values.astype(F32)).astype(BF16), expo.astype(BF16),
            preferred_element_type=F32,
        )

    def causal(scores):
        key = lax.broadcasted_iota(jnp.int32, scores.shape, 0)
        place = lax.broadcasted_iota(jnp.int32, scores.shape, 1) % resp
        return jnp.where(key <= place, scores, -1e30)

    def text_rows(place, which):
        first = (place * 2 + which) * rows_text
        rows = pl.ds(pl.multiple_of(first, 128), rows_text)

        def mask(scores):
            upper = lax.broadcasted_iota(jnp.int32, (padded, scores.shape[1]), 0)
            taken = [
                jnp.dot(
                    bias[...], jnp.where(upper == first // 128 + i, 1.0, 0.0).astype(BF16),
                    preferred_element_type=F32,
                )
                for i in range(rows_text // 128)
            ]
            return jnp.where(jnp.concatenate(taken, axis=0) > 0.5, -1e30, scores)

        attend(text[rows, :HD], text[rows, HD:], mask)

    attend(own_kv[0], own_kv[1], causal)
    first_row = pl.multiple_of((plane * 2 + core) * rows_text, 128)
    text[pl.ds(first_row, rows_text), :] = share_ref[...]
    text_rows(plane, core)
    text_twin(0, 1 - core).wait_recv()
    text_rows(plane, 1 - core)

    def slot(place, which):
        return image.at[pl.ds(pl.multiple_of((place * 2 + which) * each, 16), each)]

    def plane_link(j):
        block = slot(plane, core)
        return remote(
            block, block, plane_send.at[j], plane_recv.at[j], beside((plane + j) % planes)
        )

    def plane_from(j):
        block = slot((plane - j) % planes, core)
        return remote(block, block, plane_send.at[j], plane_recv.at[j], twin)

    def twin_link(j, which):
        block = slot((plane - j) % planes, which)
        return remote(block, block, twin_send.at[j], twin_recv.at[j], twin)

    for k in range(1, chips):
        line_link(k).wait_recv()
    total = own[chip] + pair_in[chip, :each, :].astype(F32)
    square = own_sq[chip % vh] + joined(pair_in[chip, each:, :])
    for k in range(1, chips):
        total += line_in[k, :each, :].astype(F32)
        square += joined(line_in[k, each:, :])
    inverse = lax.rsqrt(square / D + EPS)
    factor = jnp.transpose(jnp.broadcast_to(inverse[0:1, :each], (128, each)))
    place = pl.multiple_of((plane * 2 + core) * each, 16)
    for side in range(2):
        lanes = slice(side * HD, (side + 1) * HD)
        image[pl.ds(place, each), lanes] = (total[:, lanes] * factor).astype(BF16)
    for j in range(1, planes):
        plane_link(j).start()
    twin_link(0, core).start()
    for j in range(1, planes):
        text_from(j).wait_recv()
        text_twin(j, core).start()

    def text_near(j, carry):
        text_rows((plane - j) % planes, core)
        return carry

    def text_far(j, carry):
        text_twin(j, 1 - core).wait_recv()
        text_rows((plane - j) % planes, 1 - core)
        return carry

    lax.fori_loop(1, planes, text_near, 0)
    for j in range(1, planes):
        plane_from(j).wait_recv()
        twin_link(j, core).start()
    lax.fori_loop(1, planes, text_far, 0)
    for j in range(planes):
        twin_link(j, 1 - core).wait_recv()

    def result_slot(origin, which, piece):
        first = ((origin * 2 + which) * mine + piece) * HD
        return out_ref.at[:, pl.ds(pl.multiple_of(first, HD), HD)]

    def origin_of(direction, hop):
        return chip - hop if direction == 0 else chip + hop

    def exists(direction, hop):
        return chip >= hop if direction == 0 else chip + hop < chips

    def pass_on(direction, hop, piece):
        block = result_slot(origin_of(direction, hop), core, piece)
        return remote(
            block, block, send_sem.at[direction, hop, piece], recv_sem.at[direction, hop, piece],
            at(neighbour(direction), core),
        )

    def arrival(direction, hop, piece):
        block = result_slot(origin_of(direction, hop), core, piece)
        return remote(
            block, block, send_sem.at[direction, hop - 1, piece],
            recv_sem.at[direction, hop - 1, piece], twin,
        )

    def give(origin, piece, which):
        block = result_slot(origin, which, piece)
        return remote(
            block, block, near_send.at[origin, piece], near_recv.at[origin, piece], twin
        )

    live = lax.broadcasted_iota(jnp.int32, (resp, HD), 0) < len_ref[0]
    for piece in range(mine):
        lanes = slice(piece * resp, (piece + 1) * resp)

        def image_chunk(i, carry):
            rows = pl.ds(pl.multiple_of(i * KEYS, KEYS), KEYS)
            attend(image[rows, :HD], image[rows, HD:], lambda scores: scores, lanes)
            return carry

        lax.fori_loop(0, image.shape[0] // KEYS, image_chunk, 0)
        value = jnp.transpose(mix[:, lanes] / summed[:, lanes])
        out_ref[:, pl.ds(pl.multiple_of(lane + piece * HD, HD), HD)] = jnp.where(
            live, value, 0.0
        ).astype(BF16)
        for direction in range(2):
            @pl.when(has(direction))
            def _():
                pass_on(direction, 0, piece).start()
        give(chip, piece, core).start()
    for hop in range(1, chips):
        for piece in range(mine):
            for direction in range(2):
                @pl.when(exists(direction, hop))
                def _():
                    arrival(direction, hop, piece).wait_recv()
                    if hop < chips - 1:
                        @pl.when(has(direction))
                        def _():
                            pass_on(direction, hop, piece).start()
                    give(origin_of(direction, hop), piece, core).start()

    swap.wait_send()
    for k in range(1, chips):
        line_link(k).wait_send()
    text_own().wait_send()
    for j in range(planes):
        twin_link(j, core).wait_send()
        if j:
            plane_link(j).wait_send()
            text_link(j).wait_send()
            text_twin(j, core).wait_send()
    for piece in range(mine):
        for origin in range(chips):
            give(origin, piece, 1 - core).wait_recv()
        give(chip, piece, core).wait_send()
        for direction in range(2):
            for hop in range(chips):
                if hop < chips - 1:
                    @pl.when(jnp.logical_and(exists(direction, hop), has(direction)))
                    def _():
                        pass_on(direction, hop, piece).wait_send()
                if hop > 0:
                    @pl.when(exists(direction, hop))
                    def _():
                        give(origin_of(direction, hop), piece, core).wait_send()


def in_hbm(array):
    return pltpu.with_memory_space_constraint(array, pltpu.MemorySpace.HBM)


def whole_kernel(sizes, ctxs, mine, shard_rows, groups, *refs):
    (
        vis_gain, tgain, merge_gain, dest, row, length,
        patches, w_out, w_qkv, text, w_kv, w_merge, queries, resp_kv, out,
    ) = refs[:15]
    scratch = refs[15:]
    first, second = groups
    front_refs, middle_refs = scratch[:first], scratch[first : first + second]
    tail_refs = scratch[first + second :]
    chips, vh = sizes[0] * sizes[1], sizes[1]
    core, ctx = lax.axis_index("core"), lax.axis_index("ctx")
    chip = lax.axis_index("vk") * vh + lax.axis_index("vh")
    planes = ctxs * vh
    plane = ctx * vh + lax.axis_index("vh")

    def greet():
        barrier = pltpu.get_barrier_semaphore()
        pl.semaphore_signal(barrier, inc=1, device_id={"core": 1 - core}, device_id_type=MESH)
        for k in range(1, chips):
            other = (chip + k) % chips
            pl.semaphore_signal(
                barrier, inc=1, device_id={"vk": other // vh, "vh": other % vh}, device_id_type=MESH
            )
        for j in range(1, planes):
            other = (plane + j) % planes
            pl.semaphore_signal(
                barrier, inc=1, device_id={"ctx": other // vh, "vh": other % vh}, device_id_type=MESH
            )
        pl.semaphore_wait(barrier, chips + planes - 1)

    qkv, held, chain_last, sums, squares = front_refs[:5]
    wkv = front_refs[7]
    visual, share = middle_refs[:2]
    drains = [
        front_kernel(sizes, patches, vis_gain, tgain, w_qkv, text, w_kv, greet, *front_refs),
        middle_kernel(
            sizes, ctxs, qkv, w_out, merge_gain, chain_last, sums, squares, held, w_merge,
            *middle_refs
        ),
    ]
    tail_kernel(
        sizes, ctxs, mine, shard_rows, visual, tgain, dest, row, length, share, wkv, queries,
        resp_kv, out, *tail_refs
    )
    for drain in drains:
        drain()


def per_device(
    patches,
    vis_gain,
    w_qkv,
    w_out,
    merge_gain,
    w_merge,
    token_dest,
    token_row,
    prompt_text,
    kv_gain,
    w_kv,
    queries,
    resp_kv,
    resp_len,
):
    sizes = tuple(lax.axis_size(name) for name in VIS)
    ctxs = lax.axis_size("ctx")
    chips, planes, parts = sizes[0] * sizes[1], ctxs * sizes[1], sizes[1] * 2
    count, width = patches.shape
    shard_rows = prompt_text.shape[0]
    each = shard_rows // parts
    heads3 = w_qkv.shape[1] // VHD
    total = 2 * chips * count
    half = total // 2
    blocks = half // LANES
    tokens = total // 4
    token_part = tokens // parts
    mine = QH // (2 * chips)
    resp = queries.shape[0]
    DMA, V = pltpu.SemaphoreType.DMA, pltpu.VMEM
    text_block = (each + 16, 2 * HD)
    image_block = (chips, token_part + 16, 2 * HD)
    front_scratch = [
        V((total, heads3 * 128), BF16),
        V((total, width), BF16),
        V((2,) + text_block, BF16),
        V((each, 2 * HD), F32),
        V((8, SUBROWS), F32),
        V((heads3 * 128, width), BF16),
        V(prompt_text.shape, BF16),
        V(w_kv.shape, BF16),
        V((2 * count, width), BF16),
        V((chips, each, 2 * HD), F32),
        V((sizes[1], 8, SUBROWS), F32),
        V((chips,) + text_block, BF16),
        V((chips,) + text_block, BF16),
        V((2, chips) + text_block, BF16),
        V((2, chips) + text_block, BF16),
        DMA((3 + heads3,)),
        DMA((2, chips, PIECES)),
        DMA((2, chips, PIECES)),
        DMA((chips, PIECES)),
        DMA((chips, PIECES)),
        DMA((2,)),
        DMA((2, chips)),
        DMA((2, chips)),
    ]
    middle_scratch = [
        V((tokens, w_merge.shape[1]), BF16),
        V((each, 2 * HD), BF16),
        V((VD, half), BF16),
        V((VD, width), BF16),
        V(w_merge.shape, BF16),
        V((width // 128, half, 128), F32),
        V((4, tokens, width), BF16),
        V((tokens, w_merge.shape[1]), F32),
        V((w_out.shape[0] // VHD, 128, total), BF16),
        V((w_out.shape[0], half), BF16),
        V((2,) + text_block, BF16),
        DMA((2,)),
        DMA((2, chips, blocks)),
        DMA((2, chips, blocks)),
        DMA((blocks,)),
        DMA((blocks,)),
        DMA((4,)),
        DMA((4,)),
        DMA((2,)),
        DMA((2,)),
        DMA((chips,)),
        DMA((chips,)),
        DMA((chips, ctxs)),
        DMA((chips, ctxs)),
        DMA((chips, ctxs)),
        DMA((chips, ctxs)),
    ]
    tail_scratch = [
        V((resp, mine * HD), BF16),
        V((mine * resp, HD), BF16),
        V((2, resp, HD), BF16),
        V((128, -(-ctxs * shard_rows // 16384) * 128), BF16),
        V((planes * 2 * each, 2 * HD), BF16),
        V((planes * 2 * token_part, 2 * HD), BF16),
        V((chips, token_part, 2 * HD), F32),
        V((sizes[1], 8, 2 * HD), F32),
        V(image_block, BF16),
        V(image_block, BF16),
        V(image_block, BF16),
        V(image_block, BF16),
        V((1, mine * resp), F32),
        V((1, mine * resp), F32),
        V((HD, mine * resp), F32),
        DMA((4,)),
        DMA((2,)),
        DMA((chips,)),
        DMA((chips,)),
        DMA((planes,)),
        DMA((planes,)),
        DMA((planes,)),
        DMA((planes,)),
        DMA((planes,)),
        DMA((planes,)),
        DMA((planes,)),
        DMA((planes,)),
        DMA((2, chips, mine)),
        DMA((2, chips, mine)),
        DMA((chips, mine)),
        DMA((chips, mine)),
    ]
    room = sum(
        math.prod(item.shape) * item.dtype.itemsize
        for item in front_scratch + middle_scratch + tail_scratch
        if item.memory_space == pltpu.MemorySpace.VMEM
    )
    groups = (len(front_scratch), len(middle_scratch))
    return pl.pallas_call(
        functools.partial(whole_kernel, sizes, ctxs, mine, shard_rows, groups),
        out_shape=jax.ShapeDtypeStruct((resp, QH * HD), BF16),
        in_specs=[VMEM] * 5 + [pl.BlockSpec(memory_space=pltpu.SMEM)] + [ANY] * 8,
        out_specs=VMEM,
        scratch_shapes=front_scratch + middle_scratch + tail_scratch,
        compiler_params=pltpu.CompilerParams(
            collective_id=0, has_side_effects=True, vmem_limit_bytes=min(67_000_000, room + 6 * 2**20)
        ),
    )(
        vis_gain, kv_gain.reshape(1, -1), merge_gain, token_dest, token_row, resp_len,
        *map(in_hbm, (patches, w_out, w_qkv.T, prompt_text, w_kv, w_merge, queries, resp_kv)),
    )


def solution(mesh):
    ctx_count, vis_count = mesh.shape["ctx"], mesh.shape["vis"]
    parts = vis_count // KVH
    shape = (ctx_count, vis_count // parts, parts // 2, 2)
    fine = Mesh(mesh.devices.reshape(shape), ("ctx",) + VIS)
    return jax.shard_map(
        per_device,
        mesh=fine,
        in_specs=(
            P(("ctx",) + VIS, None),
            P(),
            P(None, VIS),
            P(VIS, None),
            P(),
            P(None, VIS),
            P(),
            P(),
            P("ctx", VIS),
            P(VIS),
            P(VIS, None),
            P("ctx", None),
            P("ctx", None),
            P("ctx"),
        ),
        out_specs=P("ctx", None),
        check_vma=False,
    )
```

```python
import functools
import math

import jax
import jax.numpy as jnp
from jax import lax
from jax.experimental import pallas as pl
from jax.experimental.pallas import tpu as pltpu
from jax.sharding import Mesh, PartitionSpec as P

VD = 1280
D = 8192
HD = 128
QH = 32
KVH = 4
VHD = 80
MD = 5120


EPS = 1e-06
VIS = ("vk", "vh", "core")
MESH = pl.DeviceIdType.MESH
VMEM = pl.BlockSpec(memory_space=pltpu.VMEM)
ANY = pl.BlockSpec(memory_space=pl.ANY)
F32 = jnp.float32
BF16 = jnp.bfloat16
PIECES = 2
SUBROWS = 256
LNROWS = 64
LANES = 256
KEYS = 1024


def layer_norm(values, gain):
    center = values - jnp.mean(values, axis=-1, keepdims=True)
    spread = jnp.mean(center * center, axis=-1, keepdims=True)
    return center * lax.rsqrt(spread + EPS) * gain


def front_kernel(sizes, *refs):
    (
        patches_ref, gain_ref, tgain_ref, wqkv_hbm, text_hbm, wkv_hbm, greet, settle,
        qkv_ref, held, chain_last, mine_ref, mine_sq,
        wpad, text, wkv, normed, own, own_sq, pair_out, pair_in, chain_out, chain_in,
        load_sem, send_sem, recv_sem, near_send, near_recv, pair_sem, chain_send, chain_recv,
    ) = refs
    chips, vh = sizes[0] * sizes[1], sizes[1]
    core = lax.axis_index("core")
    chip = lax.axis_index("vk") * vh + lax.axis_index("vh")
    count = patches_ref.shape[0]
    half = count // PIECES
    each = mine_ref.shape[0]
    subs = each // SUBROWS

    def at(where, which):
        return {"vk": where // vh, "vh": where % vh, "core": which}

    def neighbour(direction):
        return chip + 1 if direction == 0 else chip - 1

    def has(direction):
        return chip < chips - 1 if direction == 0 else chip > 0

    def remote(src, dst, send, recv, where, which):
        return pltpu.make_async_remote_copy(
            src_ref=src, dst_ref=dst, send_sem=send, recv_sem=recv,
            device_id=at(where, which), device_id_type=MESH,
        )

    loads = [
        pltpu.make_async_copy(text_hbm, text, load_sem.at[0]),
        pltpu.make_async_copy(wkv_hbm, wkv, load_sem.at[1]),
    ] + [
        pltpu.make_async_copy(
            wqkv_hbm.at[pl.ds(part * VHD, VHD)], wpad.at[pl.ds(part * 128, VHD)],
            load_sem.at[2 + part],
        )
        for part in range(wqkv_hbm.shape[0] // VHD)
    ]
    for load in loads:
        load.start()

    greet()

    def slot(origin, which, piece):
        first = pl.multiple_of((origin * 2 + which) * count + piece * half, 16)
        return held.at[pl.ds(first, half)]

    def source(origin, piece, hop):
        return patches_ref.at[pl.ds(piece * half, half)] if hop == 0 else slot(origin, core, piece)

    def origin_of(direction, hop):
        return chip - hop if direction == 0 else chip + hop

    def exists(direction, hop):
        return chip >= hop if direction == 0 else chip + hop < chips

    def pass_on(direction, hop, piece):
        origin = origin_of(direction, hop)
        return remote(
            source(origin, piece, hop), slot(origin, core, piece),
            send_sem.at[direction, hop, piece], recv_sem.at[direction, hop, piece],
            neighbour(direction), core,
        )

    def arrival(direction, hop, piece):
        origin = origin_of(direction, hop)
        return remote(
            slot(origin, core, piece), slot(origin, core, piece),
            send_sem.at[direction, hop - 1, piece], recv_sem.at[direction, hop - 1, piece],
            chip, 1 - core,
        )

    def give(origin, piece, hop):
        return remote(
            source(origin, piece, hop), slot(origin, core, piece),
            near_send.at[origin, piece], near_recv.at[origin, piece], chip, 1 - core,
        )

    def taken(origin, piece):
        return remote(
            slot(origin, 1 - core, piece), slot(origin, 1 - core, piece),
            near_send.at[origin, piece], near_recv.at[origin, piece], chip, 1 - core,
        )

    for piece in range(PIECES):
        for direction in range(2):
            @pl.when(has(direction))
            def _():
                pass_on(direction, 0, piece).start()
    my_rows = pl.ds(pl.multiple_of((chip * 2 + core) * count, 16), count)
    mine = pltpu.make_async_copy(patches_ref, held.at[my_rows], load_sem.at[len(loads)])
    mine.start()
    for piece in range(PIECES):
        give(chip, piece, 0).start()

    def relay(hop):
        for piece in range(PIECES):
            for direction in range(2):
                @pl.when(exists(direction, hop))
                def _():
                    arrival(direction, hop, piece).wait_recv()
                    if hop < chips - 1:
                        @pl.when(has(direction))
                        def _():
                            pass_on(direction, hop, piece).start()
                    give(origin_of(direction, hop), piece, hop).start()

    def text_rows(v, which, write):
        for s in range(subs):
            first = pl.multiple_of((v * 2 + which) * each + s * SUBROWS, SUBROWS)
            rows = text[pl.ds(first, SUBROWS), :].astype(F32)
            total = jnp.sum(rows * rows, axis=1, keepdims=True)
            line = jnp.transpose(jnp.broadcast_to(total, (SUBROWS, 128)))
            own_sq[v, s : s + 1, :] = line[0:1]
            scaled = (rows * tgain_ref[...]).astype(BF16)
            for side in range(2):
                for pair in range(KVH // 2):
                    begin = (side * KVH + pair * 2) * HD
                    raw = jnp.dot(scaled, wkv[:, begin : begin + 2 * HD], preferred_element_type=F32)
                    for i in range(2):
                        write((pair * 2 + i) * vh + v, s, side, raw[:, i * HD : (i + 1) * HD])

    def tail(total):
        coarse = total.astype(BF16).astype(F32)
        return jnp.concatenate([coarse, total - coarse], axis=0).astype(BF16)

    def untail(block):
        block = block.astype(F32)
        return block[:8] + block[8:]

    def write_pair(d, s, side, value):
        pair_out[d, s * SUBROWS : (s + 1) * SUBROWS, side * HD : (side + 1) * HD] = value.astype(BF16)

    def write_own(d, s, side, value):
        own[d, s * SUBROWS : (s + 1) * SUBROWS, side * HD : (side + 1) * HD] = value

    own_sq[...] = jnp.zeros_like(own_sq)
    settle()
    loads[0].wait()
    loads[1].wait()
    for v in range(vh):
        text_rows(v, 1 - core, write_pair)
        for h in range(KVH):
            pair_out[h * vh + v, each:, :] = tail(own_sq[v])
    swap = remote(pair_out, pair_in, pair_sem.at[0], pair_sem.at[1], chip, 1 - core)
    swap.start()
    for v in range(vh):
        text_rows(v, core, write_own)

    for part, load in enumerate(loads[2:]):
        wpad[part * 128 + VHD : (part + 1) * 128, :] = jnp.zeros((128 - VHD, wpad.shape[1]), BF16)
        load.wait()

    def project(origin):
        def norm_rows(i, carry):
            begin = pl.multiple_of(origin * 2 * count + i * LNROWS, LNROWS)
            floats = held[pl.ds(begin, LNROWS), :].astype(F32)
            place = pl.multiple_of(i * LNROWS, LNROWS)
            normed[pl.ds(place, LNROWS), :] = layer_norm(floats, gain_ref[...]).astype(BF16)
            return carry

        lax.fori_loop(0, 2 * count // LNROWS, norm_rows, 0)
        first = pl.multiple_of(origin * 2 * count, 2 * count)
        qkv_ref[pl.ds(first, 2 * count), :] = lax.dot_general(
            normed[...], wpad[...], (((1,), (1,)), ((), ())), preferred_element_type=F32
        ).astype(BF16)

    def project_hop(hop):
        for direction in range(2 if hop else 1):
            @pl.when(exists(direction, hop))
            def _():
                origin = origin_of(direction, hop)
                for piece in range(PIECES):
                    taken(origin, piece).wait_recv()
                project(origin)

    def link(direction, d):
        return remote(
            chain_out.at[direction, d], chain_in.at[direction, d],
            chain_send.at[direction, d], chain_recv.at[direction, d], neighbour(direction), core,
        )

    def sum_up(d, source, put, put_square):
        def body(i, carry):
            rows = pl.ds(pl.multiple_of(i * 128, 128), 128)
            value = own[d, rows, :] + pair_in[d, rows, :].astype(F32)
            if source is not None:
                value += source[rows, :].astype(F32)
            put(rows, value)
            return carry

        lax.fori_loop(0, each // 128, body, 0)
        square = own_sq[d % vh] + untail(pair_in[d, each:, :])
        if source is not None:
            square += untail(source[each:, :])
        put_square(square)

    def chain(step):
        for direction in range(2):
            rank = chip if direction == 0 else chips - 1 - chip
            ahead = chips - step
            d = chip + ahead if direction == 0 else chip - ahead
            last = step == chips - 1

            def block():
                return chain_last.at[direction] if last else chain_out.at[direction, d]

            def put(rows, value):
                block()[rows, :] = value.astype(BF16)

            def put_square(square):
                block()[each:, :] = tail(square)

            @pl.when(rank < step)
            def _():
                @pl.when(rank == 0)
                def _():
                    sum_up(d, None, put, put_square)

                if step > 1:
                    @pl.when(rank > 0)
                    def _():
                        link(direction, d).wait_recv()
                        sum_up(d, chain_in.at[direction, d], put, put_square)

                if not last:
                    link(direction, d).start()

    relay(1)
    swap.wait_recv()
    if chips > 2:
        chain(1)
    mine.wait()
    project_hop(0)
    for hop in range(2, chips):
        relay(hop)
        if hop < chips - 1:
            chain(hop)
        project_hop(hop - 1)

    def put_mine(rows, value):
        mine_ref[rows, :] = value

    def put_mine_square(square):
        mine_sq[...] = square

    sum_up(chip, None, put_mine, put_mine_square)
    chain(chips - 1)
    project_hop(chips - 1)

    def drain():
        swap.wait_send()
        for piece in range(PIECES):
            give(chip, piece, 0).wait_send()
            for direction in range(2):
                for hop in range(chips):
                    if hop < chips - 1:
                        @pl.when(jnp.logical_and(exists(direction, hop), has(direction)))
                        def _():
                            pass_on(direction, hop, piece).wait_send()
                    if hop > 0:
                        @pl.when(exists(direction, hop))
                        def _():
                            give(origin_of(direction, hop), piece, hop).wait_send()
        for direction in range(2):
            for d in range(chips):
                @pl.when(chip < d - 1 if direction == 0 else chip > d + 1)
                def _():
                    link(direction, d).wait_send()

    return drain


def spread_of(rows, width, places):
    best = (1, 1)
    for down in range(1, rows // 16 + 1):
        for across in range(1, width // 128 + 1):
            if rows % (16 * down) or width % (128 * across) or down * across > places:
                continue
            if down * across > best[0] * best[1]:
                best = (down, across)
    return best


def middle_kernel(sizes, ctxs, *refs):
    (
        qkv_ref, wout_ref, gain_ref, chain_ref, mine_ref, sq_ref, patches, wmerge_hbm,
        visual_ref, share_ref,
        held, wall, wmerge, mixed, merged, token_sum, values, staged, chain_in,
        load_sem, send_sem, recv_sem, near_send, near_recv, merge_send, merge_recv,
        chain_send, chain_recv,
        line_send, line_recv, plane_send, plane_recv, pair_send, pair_recv,
    ) = refs
    chips, vh = sizes[0] * sizes[1], sizes[1]
    core, ctx = lax.axis_index("core"), lax.axis_index("ctx")
    vk_index, vh_index = lax.axis_index("vk"), lax.axis_index("vh")
    chip = vk_index * vh + vh_index
    me = chip * 2 + core
    each = mine_ref.shape[0]
    subs = each // SUBROWS
    deep, width = wout_ref.shape
    total = qkv_ref.shape[0]
    half = total // 2
    blocks = half // LANES
    heads = deep // VHD
    planes = ctxs * vh
    plane = ctx * vh + vh_index

    def at(where, which):
        return {"vk": where // vh, "vh": where % vh, "core": which}

    def beside(where):
        return {"ctx": where // vh, "vh": where % vh}

    def neighbour(direction):
        return chip + 1 if direction == 0 else chip - 1

    def has(direction):
        return chip < chips - 1 if direction == 0 else chip > 0

    def remote(src, dst, send, recv, device):
        return pltpu.make_async_remote_copy(
            src_ref=src, dst_ref=dst, send_sem=send, recv_sem=recv,
            device_id=device, device_id_type=MESH,
        )

    twin = at(chip, 1 - core)
    load = pltpu.make_async_copy(wmerge_hbm, wmerge, load_sem.at[0])
    load.start()
    my_rows = pl.ds(pl.multiple_of(me * deep, 16), deep)
    keep = pltpu.make_async_copy(wout_ref, wall.at[my_rows], load_sem.at[1])
    keep.start()

    def last_link(direction):
        return remote(
            chain_ref.at[direction], chain_in.at[direction],
            chain_send.at[direction], chain_recv.at[direction], at(neighbour(direction), core),
        )

    down, across = spread_of(deep, width, ctxs)
    used, high, wide = down * across, deep // down, width // across

    def part(origin, which, index):
        first = pl.multiple_of((origin * 2 + which) * deep + (index // across) * high, 16)
        lane = pl.multiple_of((index % across) * wide, 128)
        return wall.at[pl.ds(first, high), pl.ds(lane, wide)]

    def line_part(k):
        first = pl.multiple_of((ctx // across) * high, 16)
        lane = pl.multiple_of((ctx % across) * wide, 128)
        return remote(
            wout_ref.at[pl.ds(first, high), pl.ds(lane, wide)], part(chip, core, ctx),
            line_send.at[k], line_recv.at[k], at((chip + k) % chips, core),
        )

    def from_line(k, j):
        block = part((chip - k) % chips, core, ctx)
        return remote(
            block, block, plane_send.at[k, j], plane_recv.at[k, j], {"ctx": (ctx + j) % ctxs}
        )

    def to_twin(k, j, which):
        block = part((chip - k) % chips, which, (ctx - j) % ctxs)
        return remote(block, block, pair_send.at[k, j], pair_recv.at[k, j], twin)

    def own_to_twin():
        return remote(wout_ref, wall.at[my_rows], pair_send.at[0, 0], pair_recv.at[0, 0], twin)

    for k in range(1, chips):
        @pl.when(ctx < used)
        def _():
            line_part(k).start()
    own_to_twin().start()

    def lanes_of(piece):
        return pl.ds(pl.multiple_of(piece * LANES, LANES), LANES)

    def slot(origin, piece):
        first = pl.multiple_of(origin * 2 * deep, 16)
        return held.at[pl.ds(first, 2 * deep), lanes_of(piece)]

    def origin_of(direction, hop):
        return chip - hop if direction == 0 else chip + hop

    def exists(direction, hop):
        return chip >= hop if direction == 0 else chip + hop < chips

    def pass_on(direction, hop, piece):
        block = slot(origin_of(direction, hop), piece)
        return remote(
            block, block, send_sem.at[direction, hop, piece], recv_sem.at[direction, hop, piece],
            at(neighbour(direction), core),
        )

    def arrival(direction, hop, piece):
        block = slot(origin_of(direction, hop), piece)
        return remote(
            block, block, send_sem.at[direction, hop - 1, piece],
            recv_sem.at[direction, hop - 1, piece], twin,
        )

    def give(piece):
        return remote(
            staged.at[:, lanes_of(piece)], held.at[my_rows, lanes_of(piece)],
            near_send.at[piece], near_recv.at[piece], twin,
        )

    def taken(piece):
        first = pl.multiple_of((chip * 2 + 1 - core) * deep, 16)
        block = held.at[pl.ds(first, deep), lanes_of(piece)]
        return remote(block, block, near_send.at[piece], near_recv.at[piece], twin)

    scale = 1.0 / math.sqrt(VHD)
    for h in range(heads):
        first = (h * 3 + 2) * 128
        values[h] = jnp.transpose(qkv_ref[:, first : first + 128].astype(F32)).astype(BF16)

    def attend(piece, side, put):
        places = pl.ds(pl.multiple_of(side * half + piece * LANES, LANES), LANES)
        for h in range(heads):
            first = h * 3 * 128
            query = qkv_ref[places, first : first + 128]
            keys = qkv_ref[:, first + 128 : first + 256]
            scores = lax.dot_general(
                keys, query, (((1,), (1,)), ((), ())), preferred_element_type=F32
            ) * scale
            expo = jnp.exp(scores - jnp.max(scores, axis=0, keepdims=True))
            summed = jnp.sum(expo, axis=0, keepdims=True)
            mix = jnp.dot(values[h], expo.astype(BF16), preferred_element_type=F32)
            put(h, (mix[:VHD] / summed).astype(BF16))

    def attend_far(piece, carry):
        def put(h, value):
            staged[h * VHD : (h + 1) * VHD, lanes_of(piece)] = value

        attend(piece, 1 - core, put)
        give(piece).start()
        return carry

    def attend_near(piece, carry):
        def put(h, value):
            rows = pl.ds(pl.multiple_of(me * deep + h * VHD, 16), VHD)
            held[rows, lanes_of(piece)] = value

        attend(piece, core, put)
        taken(piece).wait_recv()
        for direction in range(2):
            @pl.when(has(direction))
            def _():
                pass_on(direction, 0, piece).start()
        return carry

    lax.fori_loop(0, blocks, attend_far, 0)
    lax.fori_loop(0, blocks, attend_near, 0)

    def relay(hop):
        def body(piece, carry):
            for direction in range(2):
                @pl.when(exists(direction, hop))
                def _():
                    arrival(direction, hop, piece).wait_recv()
                    if hop < chips - 1:
                        @pl.when(has(direction))
                        def _():
                            pass_on(direction, hop, piece).start()
            return carry

        lax.fori_loop(0, blocks, body, 0)

    def untail(block):
        block = block.astype(F32)
        return block[:8] + block[8:]

    def gain_from(direction):
        last_link(direction).wait_recv()

        def body(i, carry):
            rows = pl.ds(pl.multiple_of(i * 128, 128), 128)
            mine_ref[rows, :] += chain_in[direction, rows, :].astype(F32)
            return carry

        lax.fori_loop(0, each // 128, body, 0)
        sq_ref[...] += untail(chain_in[direction, each:, :])

    def finish_text():
        for direction in range(2):
            @pl.when(has(1 - direction))
            def _():
                gain_from(direction)
        inverse = lax.rsqrt(sq_ref[...] / D + EPS)
        for s in range(subs):
            factor = jnp.transpose(jnp.broadcast_to(inverse[s : s + 1], (128, SUBROWS)))
            for side in range(2):
                lanes = slice(side * HD, (side + 1) * HD)
                rows = slice(s * SUBROWS, (s + 1) * SUBROWS)
                share_ref[rows, lanes] = (mine_ref[rows, lanes] * factor).astype(BF16)

    for k in range(1, chips):
        @pl.when(ctx < used)
        def _():
            line_part(k).wait_recv()
            for j in range(1, ctxs):
                from_line(k, j).start()
            to_twin(k, 0, core).start()
    relay(1)
    def add_chip(origin, fresh):
        rows = pl.ds(pl.multiple_of(origin * 2 * deep, 16), 2 * deep)

        def body(i, carry):
            places = pl.ds(pl.multiple_of(i * LANES, LANES), LANES)
            product = lax.dot_general(
                held[rows, places], wall[rows, :], (((0,), (0,)), ((), ())),
                preferred_element_type=F32,
            )
            if fresh:
                mine_in = pl.ds(pl.multiple_of(core * half + i * LANES, LANES), LANES)
                product += patches[mine_in, :].astype(F32)
            for c in range(width // 128):
                lanes = product[:, c * 128 : (c + 1) * 128]
                mixed[c, places, :] = lanes if fresh else mixed[c, places, :] + lanes
            return carry

        lax.fori_loop(0, blocks, body, 0)

    def add_hop(hop):
        for direction in range(2 if hop else 1):
            @pl.when(exists(direction, hop))
            def _():
                add_chip(origin_of(direction, hop), hop == 0)

    keep.wait()
    own_to_twin().wait_recv()
    add_hop(0)
    def last_sends():
        for direction in range(2):
            @pl.when(has(direction))
            def _():
                last_link(direction).start()

    if chips > 2:
        relay(2)
    if chips < 5:
        last_sends()
    for k in range(1, chips):
        for j in range(1, ctxs):
            @pl.when((ctx - j) % ctxs < used)
            def _():
                block = part((chip - k) % chips, core, (ctx - j) % ctxs)
                remote(
                    block, block, plane_send.at[k, j], plane_recv.at[k, j], twin
                ).wait_recv()
                to_twin(k, j, core).start()
    for k in range(1, chips):
        for j in range(ctxs):
            @pl.when((ctx - j) % ctxs < used)
            def _():
                to_twin(k, j, 1 - core).wait_recv()
    add_hop(1)
    for hop in range(3, chips):
        add_hop(hop - 1)
        relay(hop)
        if hop == chips - 2:
            last_sends()
    if chips > 2:
        add_hop(chips - 1)

    tokens = half // 4
    my_tokens = pl.ds(pl.multiple_of(core * tokens, LNROWS), tokens)

    def merge_link(r, which):
        block = merged.at[r, pl.ds(pl.multiple_of(which * tokens, LNROWS), tokens)]
        return remote(block, block, merge_send.at[r], merge_recv.at[r], twin)

    for r in range(4):
        def norm_rows(i, carry):
            every = pl.ds(i * 4 * LNROWS + r, LNROWS, stride=4)
            rows = jnp.concatenate([mixed[c, every, :] for c in range(width // 128)], axis=1)
            place = pl.ds(pl.multiple_of(core * tokens + i * LNROWS, LNROWS), LNROWS)
            merged[r, place, :] = layer_norm(rows, gain_ref[...]).astype(BF16)
            return carry

        lax.fori_loop(0, tokens // LNROWS, norm_rows, 0)
        merge_link(r, core).start()
    load.wait()
    for r in range(4):
        merge_link(r, 1 - core).wait_recv()

        def column(c, carry):
            lanes = pl.ds(pl.multiple_of(c * LANES, LANES), LANES)
            value = jnp.dot(
                merged[r], wmerge[r * width : (r + 1) * width, lanes], preferred_element_type=F32
            )
            if r:
                value += token_sum[:, lanes]
            if r < 3:
                token_sum[:, lanes] = value
            else:
                visual_ref[:, lanes] = value.astype(BF16)
            return carry

        lax.fori_loop(0, visual_ref.shape[1] // LANES, column, 0)

    finish_text()
    def drain():
        own_to_twin().wait_send()
        for k in range(1, chips):
            @pl.when(ctx < used)
            def _():
                line_part(k).wait_send()
                for j in range(1, ctxs):
                    from_line(k, j).wait_send()
            for j in range(ctxs):
                @pl.when((ctx - j) % ctxs < used)
                def _():
                    to_twin(k, j, core).wait_send()
        for direction in range(2):
            @pl.when(has(direction))
            def _():
                last_link(direction).wait_send()

        for r in range(4):
            merge_link(r, core).wait_send()

        def drain_line(piece, carry):
            give(piece).wait_send()
            for direction in range(2):
                for hop in range(chips - 1):
                    @pl.when(jnp.logical_and(exists(direction, hop), has(direction)))
                    def _():
                        pass_on(direction, hop, piece).wait_send()
            return carry

        lax.fori_loop(0, blocks, drain_line, 0)

    return drain


def tail_kernel(sizes, ctxs, mine, shard_rows, *refs):
    (
        visual_ref, tgain_ref, dest_ref, row_ref, len_ref, share_ref, wkv, query_hbm, own_hbm,
        out_ref,
        query_in, query, own_kv, bias, text, image, own, own_sq, pair_out, pair_in, line_out, line_in,
        high, summed, mix,
        load_sem, swap_sem, line_send, line_recv, plane_send, plane_recv, twin_send, twin_recv,
        text_send, text_recv, pass_send, pass_recv, send_sem, recv_sem, near_send, near_recv,
    ) = refs
    chips, vh = sizes[0] * sizes[1], sizes[1]
    core, ctx = lax.axis_index("core"), lax.axis_index("ctx")
    vh_index = lax.axis_index("vh")
    chip = lax.axis_index("vk") * vh + vh_index
    me = chip * 2 + core
    parts = 2 * vh
    each = visual_ref.shape[0] // parts
    planes = ctxs * vh
    plane = ctx * vh + vh_index
    resp = query_in.shape[0]
    group = QH // KVH

    def at(where, which):
        return {"vk": where // vh, "vh": where % vh, "core": which}

    def beside(where):
        return {"ctx": where // vh, "vh": where % vh}

    def neighbour(direction):
        return chip + 1 if direction == 0 else chip - 1

    def has(direction):
        return chip < chips - 1 if direction == 0 else chip > 0

    def remote(src, dst, send, recv, device):
        return pltpu.make_async_remote_copy(
            src_ref=src, dst_ref=dst, send_sem=send, recv_sem=recv,
            device_id=device, device_id_type=MESH,
        )

    twin = at(chip, 1 - core)
    lane = pl.multiple_of(me * mine * HD, HD)
    head = pl.multiple_of(((me * mine) // group) * HD, HD)
    loads = [
        pltpu.make_async_copy(query_hbm.at[:, pl.ds(lane, mine * HD)], query_in, load_sem.at[1]),
        pltpu.make_async_copy(own_hbm.at[:, pl.ds(head, HD)], own_kv.at[0], load_sem.at[2]),
        pltpu.make_async_copy(
            own_hbm.at[:, pl.ds(pl.multiple_of(KVH * HD + head, HD), HD)], own_kv.at[1], load_sem.at[3]
        ),
    ]
    for load in loads:
        load.start()

    rows_text = share_ref.shape[0]

    def text_slot(place, which):
        return text.at[pl.ds(pl.multiple_of((place * 2 + which) * rows_text, 16), rows_text)]

    def text_link(j):
        return remote(
            share_ref, text_slot(plane, core), text_send.at[j], text_recv.at[j],
            beside((plane + j) % planes),
        )

    def text_from(j):
        block = text_slot((plane - j) % planes, core)
        return remote(block, block, text_send.at[j], text_recv.at[j], twin)

    def text_twin(j, which):
        block = text_slot((plane - j) % planes, which)
        return remote(block, block, pass_send.at[j], pass_recv.at[j], twin)

    def text_own():
        return remote(share_ref, text_slot(plane, core), pass_send.at[0], pass_recv.at[0], twin)

    for j in range(1, planes):
        text_link(j).start()
    text_own().start()

    def token_rows(v, which, write):
        first = pl.multiple_of((v * 2 + which) * each, each)
        rows = visual_ref[pl.ds(first, each), :].astype(F32)
        total = jnp.sum(rows * rows, axis=1, keepdims=True)
        own_sq[v, 0:1, :each] = jnp.transpose(jnp.broadcast_to(total, (each, 128)))[0:1]
        scaled = (rows * tgain_ref[...]).astype(BF16)
        for side in range(2):
            for pair in range(KVH // 2):
                begin = (side * KVH + pair * 2) * HD
                raw = jnp.dot(scaled, wkv[:, begin : begin + 2 * HD], preferred_element_type=F32)
                for i in range(2):
                    write((pair * 2 + i) * vh + v, side, raw[:, i * HD : (i + 1) * HD])

    def split(total):
        coarse = total.astype(BF16).astype(F32)
        return jnp.concatenate([coarse, total - coarse], axis=0).astype(BF16)

    def joined(block):
        block = block.astype(F32)
        return block[:8] + block[8:]

    def write_pair(d, side, value):
        pair_out[d, :each, side * HD : (side + 1) * HD] = value.astype(BF16)

    def write_own(d, side, value):
        own[d, :, side * HD : (side + 1) * HD] = value

    own_sq[...] = jnp.zeros_like(own_sq)
    for v in range(vh):
        token_rows(v, 1 - core, write_pair)
        for h in range(KVH):
            pair_out[h * vh + v, each:, :] = split(own_sq[v])
    swap = remote(pair_out, pair_in, swap_sem.at[0], swap_sem.at[1], twin)
    swap.start()
    for v in range(vh):
        token_rows(v, core, write_own)
    for load in loads:
        load.wait()
    for j in range(mine):
        query[j * resp : (j + 1) * resp, :] = query_in[:, j * HD : (j + 1) * HD]

    def line_link(k):
        d = (chip + k) % chips
        return remote(
            line_out.at[d], line_in.at[k], line_send.at[k], line_recv.at[k], at(d, core)
        )

    swap.wait_recv()
    for k in range(1, chips):
        d = (chip + k) % chips
        line_out[d, :each, :] = (own[d] + pair_in[d, :each, :].astype(F32)).astype(BF16)
        line_out[d, each:, :] = split(own_sq[d % vh] + joined(pair_in[d, each:, :]))
        line_link(k).start()

    padded = bias.shape[1]
    count = jnp.zeros((128, padded), F32)
    for i in range(dest_ref.shape[0]):
        flat = dest_ref[i : i + 1, :] * shard_rows + row_ref[i : i + 1, :]
        low = lax.broadcasted_iota(jnp.int32, (128, flat.shape[1]), 0) == flat % 128
        upper = lax.broadcasted_iota(jnp.int32, (padded, flat.shape[1]), 0) == flat // 128
        count += lax.dot_general(
            jnp.where(low, 1.0, 0.0).astype(BF16), jnp.where(upper, 1.0, 0.0).astype(BF16),
            (((1,), (1,)), ((), ())), preferred_element_type=F32,
        )
    bias[...] = count.astype(BF16)

    high[...] = jnp.full_like(high, -1e30)
    summed[...] = jnp.zeros_like(summed)
    mix[...] = jnp.zeros_like(mix)
    scale = 1.0 / math.sqrt(HD)

    def attend(keys, values, mask, lanes=slice(None)):
        scores = lax.dot_general(
            keys, query[lanes, :], (((1,), (1,)), ((), ())), preferred_element_type=F32
        ) * scale
        scores = mask(scores)
        top = jnp.maximum(high[:, lanes], jnp.max(scores, axis=0, keepdims=True))
        fade = jnp.exp(high[:, lanes] - top)
        expo = jnp.exp(scores - top)
        high[:, lanes] = top
        summed[:, lanes] = summed[:, lanes] * fade + jnp.sum(expo, axis=0, keepdims=True)
        mix[:, lanes] = mix[:, lanes] * fade + jnp.dot(
            jnp.transpose(values.astype(F32)).astype(BF16), expo.astype(BF16),
            preferred_element_type=F32,
        )

    def causal(scores):
        key = lax.broadcasted_iota(jnp.int32, scores.shape, 0)
        place = lax.broadcasted_iota(jnp.int32, scores.shape, 1) % resp
        return jnp.where(key <= place, scores, -1e30)

    def text_rows(place, which):
        first = (place * 2 + which) * rows_text
        rows = pl.ds(pl.multiple_of(first, 128), rows_text)

        def mask(scores):
            upper = lax.broadcasted_iota(jnp.int32, (padded, scores.shape[1]), 0)
            taken = [
                jnp.dot(
                    bias[...], jnp.where(upper == first // 128 + i, 1.0, 0.0).astype(BF16),
                    preferred_element_type=F32,
                )
                for i in range(rows_text // 128)
            ]
            return jnp.where(jnp.concatenate(taken, axis=0) > 0.5, -1e30, scores)

        attend(text[rows, :HD], text[rows, HD:], mask)

    attend(own_kv[0], own_kv[1], causal)
    first_row = pl.multiple_of((plane * 2 + core) * rows_text, 128)
    text[pl.ds(first_row, rows_text), :] = share_ref[...]
    text_rows(plane, core)
    text_twin(0, 1 - core).wait_recv()
    text_rows(plane, 1 - core)

    def slot(place, which):
        return image.at[pl.ds(pl.multiple_of((place * 2 + which) * each, 16), each)]

    def plane_link(j):
        block = slot(plane, core)
        return remote(
            block, block, plane_send.at[j], plane_recv.at[j], beside((plane + j) % planes)
        )

    def plane_from(j):
        block = slot((plane - j) % planes, core)
        return remote(block, block, plane_send.at[j], plane_recv.at[j], twin)

    def twin_link(j, which):
        block = slot((plane - j) % planes, which)
        return remote(block, block, twin_send.at[j], twin_recv.at[j], twin)

    for k in range(1, chips):
        line_link(k).wait_recv()
    total = own[chip] + pair_in[chip, :each, :].astype(F32)
    square = own_sq[chip % vh] + joined(pair_in[chip, each:, :])
    for k in range(1, chips):
        total += line_in[k, :each, :].astype(F32)
        square += joined(line_in[k, each:, :])
    inverse = lax.rsqrt(square / D + EPS)
    factor = jnp.transpose(jnp.broadcast_to(inverse[0:1, :each], (128, each)))
    place = pl.multiple_of((plane * 2 + core) * each, 16)
    for side in range(2):
        lanes = slice(side * HD, (side + 1) * HD)
        image[pl.ds(place, each), lanes] = (total[:, lanes] * factor).astype(BF16)
    for j in range(1, planes):
        plane_link(j).start()
    twin_link(0, core).start()
    for j in range(1, planes):
        text_from(j).wait_recv()
        text_twin(j, core).start()

    def text_near(j, carry):
        text_rows((plane - j) % planes, core)
        return carry

    def text_far(j, carry):
        text_twin(j, 1 - core).wait_recv()
        text_rows((plane - j) % planes, 1 - core)
        return carry

    lax.fori_loop(1, planes, text_near, 0)
    for j in range(1, planes):
        plane_from(j).wait_recv()
        twin_link(j, core).start()
    lax.fori_loop(1, planes, text_far, 0)
    for j in range(planes):
        twin_link(j, 1 - core).wait_recv()

    def result_slot(origin, which, piece):
        first = ((origin * 2 + which) * mine + piece) * HD
        return out_ref.at[:, pl.ds(pl.multiple_of(first, HD), HD)]

    def origin_of(direction, hop):
        return chip - hop if direction == 0 else chip + hop

    def exists(direction, hop):
        return chip >= hop if direction == 0 else chip + hop < chips

    def pass_on(direction, hop, piece):
        block = result_slot(origin_of(direction, hop), core, piece)
        return remote(
            block, block, send_sem.at[direction, hop, piece], recv_sem.at[direction, hop, piece],
            at(neighbour(direction), core),
        )

    def arrival(direction, hop, piece):
        block = result_slot(origin_of(direction, hop), core, piece)
        return remote(
            block, block, send_sem.at[direction, hop - 1, piece],
            recv_sem.at[direction, hop - 1, piece], twin,
        )

    def give(origin, piece, which):
        block = result_slot(origin, which, piece)
        return remote(
            block, block, near_send.at[origin, piece], near_recv.at[origin, piece], twin
        )

    live = lax.broadcasted_iota(jnp.int32, (resp, HD), 0) < len_ref[0]
    for piece in range(mine):
        lanes = slice(piece * resp, (piece + 1) * resp)

        def image_chunk(i, carry):
            rows = pl.ds(pl.multiple_of(i * KEYS, KEYS), KEYS)
            attend(image[rows, :HD], image[rows, HD:], lambda scores: scores, lanes)
            return carry

        lax.fori_loop(0, image.shape[0] // KEYS, image_chunk, 0)
        value = jnp.transpose(mix[:, lanes] / summed[:, lanes])
        out_ref[:, pl.ds(pl.multiple_of(lane + piece * HD, HD), HD)] = jnp.where(
            live, value, 0.0
        ).astype(BF16)
        for direction in range(2):
            @pl.when(has(direction))
            def _():
                pass_on(direction, 0, piece).start()
        give(chip, piece, core).start()
    for hop in range(1, chips):
        for piece in range(mine):
            for direction in range(2):
                @pl.when(exists(direction, hop))
                def _():
                    arrival(direction, hop, piece).wait_recv()
                    if hop < chips - 1:
                        @pl.when(has(direction))
                        def _():
                            pass_on(direction, hop, piece).start()
                    give(origin_of(direction, hop), piece, core).start()

    swap.wait_send()
    for k in range(1, chips):
        line_link(k).wait_send()
    text_own().wait_send()
    for j in range(planes):
        twin_link(j, core).wait_send()
        if j:
            plane_link(j).wait_send()
            text_link(j).wait_send()
            text_twin(j, core).wait_send()
    for piece in range(mine):
        for origin in range(chips):
            give(origin, piece, 1 - core).wait_recv()
        give(chip, piece, core).wait_send()
        for direction in range(2):
            for hop in range(chips):
                if hop < chips - 1:
                    @pl.when(jnp.logical_and(exists(direction, hop), has(direction)))
                    def _():
                        pass_on(direction, hop, piece).wait_send()
                if hop > 0:
                    @pl.when(exists(direction, hop))
                    def _():
                        give(origin_of(direction, hop), piece, core).wait_send()


def in_hbm(array):
    return pltpu.with_memory_space_constraint(array, pltpu.MemorySpace.HBM)


def whole_kernel(sizes, ctxs, mine, shard_rows, groups, *refs):
    (
        length, vis_gain_hbm, tgain_hbm, merge_gain_hbm, dest_hbm, row_hbm,
        patches, w_out, w_qkv, text, w_kv, w_merge, queries, resp_kv, out,
    ) = refs[:15]
    vis_gain, tgain, merge_gain, dest, row, small_sem = refs[15:21]
    scratch = refs[21:]
    first, second = groups
    smalls = [
        pltpu.make_async_copy(source, target, small_sem.at[i])
        for i, (source, target) in enumerate(
            [
                (tgain_hbm, tgain), (vis_gain_hbm, vis_gain), (merge_gain_hbm, merge_gain),
                (dest_hbm, dest), (row_hbm, row),
            ]
        )
    ]
    front_refs, middle_refs = scratch[:first], scratch[first : first + second]
    tail_refs = scratch[first + second :]
    chips, vh = sizes[0] * sizes[1], sizes[1]
    core, ctx = lax.axis_index("core"), lax.axis_index("ctx")
    chip = lax.axis_index("vk") * vh + lax.axis_index("vh")
    planes = ctxs * vh
    plane = ctx * vh + lax.axis_index("vh")

    def greet():
        barrier = pltpu.get_barrier_semaphore()
        pl.semaphore_signal(barrier, inc=1, device_id={"core": 1 - core}, device_id_type=MESH)
        for k in range(1, chips):
            other = (chip + k) % chips
            pl.semaphore_signal(
                barrier, inc=1, device_id={"vk": other // vh, "vh": other % vh}, device_id_type=MESH
            )
        for j in range(1, planes):
            other = (plane + j) % planes
            pl.semaphore_signal(
                barrier, inc=1, device_id={"ctx": other // vh, "vh": other % vh}, device_id_type=MESH
            )
        for small in smalls:
            small.start()
        pl.semaphore_wait(barrier, chips + planes - 1)

    def settle():
        for small in smalls:
            small.wait()

    qkv, held, chain_last, sums, squares = front_refs[:5]
    wkv = front_refs[7]
    visual, share = middle_refs[:2]
    drains = [
        front_kernel(sizes, patches, vis_gain, tgain, w_qkv, text, w_kv, greet, settle, *front_refs),
        middle_kernel(
            sizes, ctxs, qkv, w_out, merge_gain, chain_last, sums, squares, held, w_merge,
            *middle_refs
        ),
    ]
    tail_kernel(
        sizes, ctxs, mine, shard_rows, visual, tgain, dest, row, length, share, wkv, queries,
        resp_kv, out, *tail_refs
    )
    for drain in drains:
        drain()


def per_device(
    patches,
    vis_gain,
    w_qkv,
    w_out,
    merge_gain,
    w_merge,
    token_dest,
    token_row,
    prompt_text,
    kv_gain,
    w_kv,
    queries,
    resp_kv,
    resp_len,
):
    sizes = tuple(lax.axis_size(name) for name in VIS)
    ctxs = lax.axis_size("ctx")
    chips, planes, parts = sizes[0] * sizes[1], ctxs * sizes[1], sizes[1] * 2
    count, width = patches.shape
    shard_rows = prompt_text.shape[0]
    each = shard_rows // parts
    heads3 = w_qkv.shape[1] // VHD
    total = 2 * chips * count
    half = total // 2
    blocks = half // LANES
    tokens = total // 4
    token_part = tokens // parts
    mine = QH // (2 * chips)
    resp = queries.shape[0]
    DMA, V = pltpu.SemaphoreType.DMA, pltpu.VMEM
    text_block = (each + 16, 2 * HD)
    image_block = (chips, token_part + 16, 2 * HD)
    front_scratch = [
        V((total, heads3 * 128), BF16),
        V((total, width), BF16),
        V((2,) + text_block, BF16),
        V((each, 2 * HD), F32),
        V((8, SUBROWS), F32),
        V((heads3 * 128, width), BF16),
        V(prompt_text.shape, BF16),
        V(w_kv.shape, BF16),
        V((2 * count, width), BF16),
        V((chips, each, 2 * HD), F32),
        V((sizes[1], 8, SUBROWS), F32),
        V((chips,) + text_block, BF16),
        V((chips,) + text_block, BF16),
        V((2, chips) + text_block, BF16),
        V((2, chips) + text_block, BF16),
        DMA((3 + heads3,)),
        DMA((2, chips, PIECES)),
        DMA((2, chips, PIECES)),
        DMA((chips, PIECES)),
        DMA((chips, PIECES)),
        DMA((2,)),
        DMA((2, chips)),
        DMA((2, chips)),
    ]
    middle_scratch = [
        V((tokens, w_merge.shape[1]), BF16),
        V((each, 2 * HD), BF16),
        V((VD, half), BF16),
        V((VD, width), BF16),
        V(w_merge.shape, BF16),
        V((width // 128, half, 128), F32),
        V((4, tokens, width), BF16),
        V((tokens, w_merge.shape[1]), F32),
        V((w_out.shape[0] // VHD, 128, total), BF16),
        V((w_out.shape[0], half), BF16),
        V((2,) + text_block, BF16),
        DMA((2,)),
        DMA((2, chips, blocks)),
        DMA((2, chips, blocks)),
        DMA((blocks,)),
        DMA((blocks,)),
        DMA((4,)),
        DMA((4,)),
        DMA((2,)),
        DMA((2,)),
        DMA((chips,)),
        DMA((chips,)),
        DMA((chips, ctxs)),
        DMA((chips, ctxs)),
        DMA((chips, ctxs)),
        DMA((chips, ctxs)),
    ]
    tail_scratch = [
        V((resp, mine * HD), BF16),
        V((mine * resp, HD), BF16),
        V((2, resp, HD), BF16),
        V((128, -(-ctxs * shard_rows // 16384) * 128), BF16),
        V((planes * 2 * each, 2 * HD), BF16),
        V((planes * 2 * token_part, 2 * HD), BF16),
        V((chips, token_part, 2 * HD), F32),
        V((sizes[1], 8, 2 * HD), F32),
        V(image_block, BF16),
        V(image_block, BF16),
        V(image_block, BF16),
        V(image_block, BF16),
        V((1, mine * resp), F32),
        V((1, mine * resp), F32),
        V((HD, mine * resp), F32),
        DMA((4,)),
        DMA((2,)),
        DMA((chips,)),
        DMA((chips,)),
        DMA((planes,)),
        DMA((planes,)),
        DMA((planes,)),
        DMA((planes,)),
        DMA((planes,)),
        DMA((planes,)),
        DMA((planes,)),
        DMA((planes,)),
        DMA((2, chips, mine)),
        DMA((2, chips, mine)),
        DMA((chips, mine)),
        DMA((chips, mine)),
    ]
    smalls = (vis_gain, kv_gain.reshape(1, -1), merge_gain, token_dest, token_row)
    small_scratch = [V(item.shape, item.dtype) for item in smalls] + [DMA((len(smalls),))]
    room = sum(
        math.prod(item.shape) * item.dtype.itemsize
        for item in front_scratch + middle_scratch + tail_scratch
        if item.memory_space == pltpu.MemorySpace.VMEM
    )
    groups = (len(front_scratch), len(middle_scratch))
    return pl.pallas_call(
        functools.partial(whole_kernel, sizes, ctxs, mine, shard_rows, groups),
        out_shape=jax.ShapeDtypeStruct((resp, QH * HD), BF16),
        in_specs=[pl.BlockSpec(memory_space=pltpu.SMEM)] + [ANY] * 13,
        out_specs=VMEM,
        scratch_shapes=small_scratch + front_scratch + middle_scratch + tail_scratch,
        compiler_params=pltpu.CompilerParams(
            collective_id=0, has_side_effects=True, vmem_limit_bytes=min(67_000_000, room + 6 * 2**20)
        ),
    )(
        resp_len,
        *map(in_hbm, smalls),
        *map(in_hbm, (patches, w_out, w_qkv.T, prompt_text, w_kv, w_merge, queries, resp_kv)),
    )


def solution(mesh):
    ctx_count, vis_count = mesh.shape["ctx"], mesh.shape["vis"]
    parts = vis_count // KVH
    shape = (ctx_count, vis_count // parts, parts // 2, 2)
    fine = Mesh(mesh.devices.reshape(shape), ("ctx",) + VIS)
    return jax.shard_map(
        per_device,
        mesh=fine,
        in_specs=(
            P(("ctx",) + VIS, None),
            P(),
            P(None, VIS),
            P(VIS, None),
            P(),
            P(None, VIS),
            P(),
            P(),
            P("ctx", VIS),
            P(VIS),
            P(VIS, None),
            P("ctx", None),
            P("ctx", None),
            P("ctx"),
        ),
        out_specs=P("ctx", None),
        check_vma=False,
    )
```
